32 devices in a mesh: rows: 8 (over z, y), cam: 4 (over x, core).
Axes of the slice: x: 2, y: 2, z: 4, core: 2. Of those that a mesh axis runs over, the one named last changes fastest.
Arguments:
- prefix_tokens: bfloat16 [4096, 2048], P(('rows', 'cam')), may hold values from -6 to 6
- action_tokens: bfloat16 [512, 1024], P(('rows', 'cam')), may hold values from -6 to 6
- prefix_cotangent: bfloat16 [4096, 2048], P(('rows', 'cam')), may hold values from -6 to 6
- action_cotangent: bfloat16 [512, 1024], P(('rows', 'cam')), may hold values from -6 to 6
- prefix_segments: int32 [8, 512], P('rows'), may hold values from 0 to 1, as said below
- action_codes: int32 [8, 64], P('rows'), may hold values from 1 to 2, as said below
- prefix_query: bfloat16 [2048, 2048], P(('rows', 'cam')), may hold values from -0.125 to 0.125
- prefix_key: bfloat16 [2048, 256], P(('rows', 'cam')), may hold values from -0.125 to 0.125
- prefix_value: bfloat16 [2048, 256], P(('rows', 'cam')), may hold values from -0.125 to 0.125
- prefix_mixer: bfloat16 [2048, 2048], P(('rows', 'cam')), may hold values from -2.5 to 2.5
- action_query: bfloat16 [1024, 2048], P(('rows', 'cam')), may hold values from -0.1875 to 0.1875
- action_key: bfloat16 [1024, 256], P(('rows', 'cam')), may hold values from -0.1875 to 0.1875
- action_value: bfloat16 [1024, 256], P(('rows', 'cam')), may hold values from -0.1875 to 0.1875
- action_mixer: bfloat16 [1024, 2048], P(('rows', 'cam')), may hold values from -2.5 to 2.5
- prefix_prenorm: float32 [2048], replicated, may hold values from 0.5 to 1.5
- prefix_midnorm: float32 [2048], replicated, may hold values from 0.5 to 1.5
- action_prenorm: float32 [1024], replicated, may hold values from 0.5 to 1.5
- action_midnorm: float32 [1024], replicated, may hold values from 0.5 to 1.5
- prefix_gate: bfloat16 [2048, 16384], P('rows', 'cam'), may hold values from -0.125 to 0.125
- prefix_expand: bfloat16 [2048, 16384], P('rows', 'cam'), may hold values from -0.125 to 0.125
- prefix_down: bfloat16 [2048, 16384], P('rows', 'cam'), may hold values from -0.046875 to 0.046875
- action_gate: bfloat16 [1024, 4096], P('rows', 'cam'), may hold values from -0.1875 to 0.1875
- action_expand: bfloat16 [1024, 4096], P('rows', 'cam'), may hold values from -0.1875 to 0.1875
- action_down: bfloat16 [1024, 4096], P('rows', 'cam'), may hold values from -0.09375 to 0.09375
Outputs:
- prefix_result: bfloat16 [4096, 2048], P(('rows', 'cam'))
- action_result: bfloat16 [512, 1024], P(('rows', 'cam'))
- prefix_backward: bfloat16 [4096, 2048], P(('rows', 'cam'))
- action_backward: bfloat16 [512, 1024], P(('rows', 'cam'))
- prefix_query_grad: float32 [2048, 2048], P(('rows', 'cam'))
- prefix_key_grad: float32 [2048, 256], P(('rows', 'cam'))
- prefix_value_grad: float32 [2048, 256], P(('rows', 'cam'))
- prefix_mixer_grad: float32 [2048, 2048], P(('rows', 'cam'))
- action_query_grad: float32 [1024, 2048], P(('rows', 'cam'))
- action_key_grad: float32 [1024, 256], P(('rows', 'cam'))
- action_value_grad: float32 [1024, 256], P(('rows', 'cam'))
- action_mixer_grad: float32 [1024, 2048], P(('rows', 'cam'))
- prefix_prenorm_grad: float32 [2048], P(('rows', 'cam'))
- prefix_midnorm_grad: float32 [2048], P(('rows', 'cam'))
- action_prenorm_grad: float32 [1024], P(('rows', 'cam'))
- action_midnorm_grad: float32 [1024], P(('rows', 'cam'))
- prefix_gate_grad: float32 [2048, 16384], P('rows', 'cam')
- prefix_expand_grad: float32 [2048, 16384], P('rows', 'cam')
- prefix_down_grad: float32 [2048, 16384], P('rows', 'cam')
- action_gate_grad: float32 [1024, 4096], P('rows', 'cam')
- action_expand_grad: float32 [1024, 4096], P('rows', 'cam')
- action_down_grad: float32 [1024, 4096], P('rows', 'cam')
The draws below stay inside these ranges and needn't reach their ends.
Inputs may be any that keep to these rules, and one draw needn't show every extreme that they name: `prefix_segments`: in each row, position t below 384 belongs to episode (t mod 128) // 64; the last 128 positions hold the texts of the 2 episodes in order, each one token or more. `action_codes`: each episode's 32 tokens lie in a row at positions e * 32 to (e + 1) * 32 - 1; the first 1 to 4 of them have code 1, the others code 2.
All inputs are finite; a program needn't handle non-finite values.
Results may differ from the reference program's by a relative error of at most 0.03.
Values may be sent and summed in bfloat16 or wider, within the bound.
A program may use at most 320 MiB of HBM per device.

```python
import jax
import jax.numpy as jnp
from jax import lax

DP = 2048
FFP = 16384
DA = 1024
FFA = 4096
HEADS = 8
HD = 256
ITEMS = 2
IMG = 64
ACTT = 32
PTOK = 128
ATD = 16
PACKS = 8
N_CAM = 4


def draw_prefix_segments(key, part):
    mixed_key = jax.random.fold_in(key, 11)
    shares = jax.random.randint(mixed_key, (PACKS, ITEMS), 1, 5)
    bounds = jnp.cumsum(shares, axis=1) * PTOK // jnp.sum(shares, axis=1, keepdims=True)
    places = jnp.arange(PTOK, dtype=jnp.int32)
    text_ids = jnp.sum((places[None, :, None] >= bounds[:, None, :]).astype(jnp.int32), axis=2)
    camera_ids = jnp.arange(3 * PTOK, dtype=jnp.int32) % PTOK // IMG
    camera_ids = jnp.broadcast_to(camera_ids[None, :], (PACKS, 3 * PTOK))
    return jnp.concatenate([camera_ids, text_ids], axis=1).astype(jnp.int32)


def draw_action_codes(key, part):
    mixed_key = jax.random.fold_in(key, 23)
    states = jax.random.randint(mixed_key, (PACKS, ITEMS, 1), 1, 5)
    places = jnp.arange(ACTT, dtype=jnp.int32)[None, None, :]
    codes = jnp.where(places < states, 1, 2)
    return codes.reshape(PACKS, ITEMS * ACTT).astype(jnp.int32)


def block_scale(stream_key, dims, split, smallest, largest):
    gain, own = 1.0, jax.random.fold_in(stream_key, 6)
    for dim, shards_of in split:
        draws = jnp.exp(jax.random.uniform(jax.random.fold_in(own, dim), (shards_of,), jnp.float32, smallest / len(split), largest / len(split)))
        gain = gain * jnp.repeat(draws, dims[dim] // shards_of).reshape([-1 if axis == dim else 1 for axis in range(len(dims))])
    return gain


def normal_values(rng, extent, spread, reach, shards=(), kind=jnp.bfloat16):
    array = jax.random.normal(rng, extent, jnp.float32) * spread
    if len(shards) > 0:
        array = block_scale(rng, extent, shards, -0.22, 0.18) * array
    return jnp.clip(array, min=-reach, max=reach).astype(kind)


def setup_inputs(seed: int = 0) -> dict:
    key_of = jax.random.split(jax.random.key(seed), 25)
    return {
        "prefix_tokens": normal_values(key_of[0], (PACKS * N_CAM * PTOK, DP), 1.0, 6.0, ((0, 32),)),
        "action_tokens": normal_values(key_of[1], (PACKS * N_CAM * ATD, DA), 1.0, 6.0, ((0, 32),)),
        "prefix_cotangent": normal_values(key_of[2], (PACKS * N_CAM * PTOK, DP), 1.0, 6.0, ((0, 32),)),
        "action_cotangent": normal_values(key_of[3], (PACKS * N_CAM * ATD, DA), 1.0, 6.0, ((0, 32),)),
        "prefix_segments": draw_prefix_segments(jax.random.fold_in(key_of[24], 71), 0),
        "action_codes": draw_action_codes(jax.random.fold_in(key_of[24], 71), 0),
        "prefix_query": normal_values(key_of[6], (DP, HEADS * HD), DP ** -0.5, 0.125, ((0, 32),)),
        "prefix_key": normal_values(key_of[7], (DP, HD), DP ** -0.5, 0.125, ((0, 32),)),
        "prefix_value": normal_values(key_of[8], (DP, HD), DP ** -0.5, 0.125, ((0, 32),)),
        "prefix_mixer": normal_values(key_of[9], (DP, HEADS * HD), (max(HEADS * HD // (3 * IMG + PTOK), 1)) ** -0.5, 2.5, ((0, 32),)),
        "action_query": normal_values(key_of[10], (DA, HEADS * HD), DA ** -0.5, 0.1875, ((0, 32),)),
        "action_key": normal_values(key_of[11], (DA, HD), DA ** -0.5, 0.1875, ((0, 32),)),
        "action_value": normal_values(key_of[12], (DA, HD), DA ** -0.5, 0.1875, ((0, 32),)),
        "action_mixer": normal_values(key_of[13], (DA, HEADS * HD), (max(HEADS * HD // (3 * IMG + PTOK), 1)) ** -0.5, 2.5, ((0, 32),)),
        "prefix_prenorm": jnp.clip(1.0 + 0.1 * jax.random.normal(key_of[14], (DP,), jnp.float32), 0.5, 1.5),
        "prefix_midnorm": jnp.clip(1.0 + 0.1 * jax.random.normal(key_of[15], (DP,), jnp.float32), 0.5, 1.5),
        "action_prenorm": jnp.clip(1.0 + 0.1 * jax.random.normal(key_of[16], (DA,), jnp.float32), 0.5, 1.5),
        "action_midnorm": jnp.clip(1.0 + 0.1 * jax.random.normal(key_of[17], (DA,), jnp.float32), 0.5, 1.5),
        "prefix_gate": normal_values(key_of[18], (DP, FFP), DP ** -0.5, 0.125, ((0, 8), (1, 4))),
        "prefix_expand": normal_values(key_of[19], (DP, FFP), DP ** -0.5, 0.125, ((0, 8), (1, 4))),
        "prefix_down": normal_values(key_of[20], (DP, FFP), FFP ** -0.5, 0.046875, ((0, 8), (1, 4))),
        "action_gate": normal_values(key_of[21], (DA, FFA), DA ** -0.5, 0.1875, ((0, 8), (1, 4))),
        "action_expand": normal_values(key_of[22], (DA, FFA), DA ** -0.5, 0.1875, ((0, 8), (1, 4))),
        "action_down": normal_values(key_of[23], (DA, FFA), FFA ** -0.5, 0.09375, ((0, 8), (1, 4))),
    }


@jax.custom_vjp
def low(v):
    return lax.optimization_barrier(v.astype(jnp.bfloat16)).astype(jnp.float32)

@jax.custom_vjp
def low_back(v):
    return v

def low_keep(v):
    return (low(v), None)

def low_pass(kept, grad):
    return (grad,)

def back_keep(v):
    return (v, None)

def back_low(kept, grad):
    return (low(grad),)
low.defvjp(low_keep, low_pass)
low_back.defvjp(back_keep, back_low)
epsilon = 1e-06
highest = lax.Precision.HIGHEST
masked_score = -1e+30

def root_norm(values, gain_vector):
    return values * lax.rsqrt(lax.optimization_barrier(jnp.mean(values * values, axis=-1, keepdims=True)) + epsilon) * gain_vector

def project(operand, matrix):
    return jnp.dot(operand, matrix, precision=highest)

def feed_forward(hidden, gain_vector, gate_weight, expand_weight, down_weight):
    normed_rows = low(root_norm(hidden, gain_vector))
    gate_value = low_back(project(normed_rows, gate_weight))
    expand_value = low_back(project(normed_rows, expand_weight))
    inside = low(jax.nn.gelu(gate_value, approximate=True) * expand_value)
    return project(inside, down_weight.T)

def single_row(weight_set, row_data):
    prefix_query, prefix_key, prefix_value, prefix_mixer, action_query, action_key, action_value, action_mixer, prefix_prenorm, prefix_midnorm, action_prenorm, action_midnorm, prefix_gate, prefix_expand, prefix_down, action_gate, action_expand, action_down = weight_set
    lead_rows, tail_rows, segment_row, code_row = row_data
    lead_count = lead_rows.shape[0]
    lead_normed = low(root_norm(lead_rows, prefix_prenorm))
    tail_normed = low(root_norm(tail_rows, action_prenorm))
    queries = low(low_back(jnp.concatenate([project(lead_normed, prefix_query), project(tail_normed, action_query)], 0)))
    local_keys = low(low_back(jnp.concatenate([project(lead_normed, prefix_key), project(tail_normed, action_key)], 0)))
    local_values = low(low_back(jnp.concatenate([project(lead_normed, prefix_value), project(tail_normed, action_value)], 0)))
    action_ids = (jnp.arange(tail_rows.shape[0]) // ACTT).astype(jnp.int32)
    token_ids = jnp.concatenate([segment_row.astype(jnp.int32), action_ids])
    token_codes = jnp.concatenate([jnp.zeros(segment_row.shape, jnp.int32), code_row.astype(jnp.int32)])
    allowed = jnp.logical_and(token_ids[:, None] == token_ids[None, :], token_codes[None, :] <= token_codes[:, None])
    head_rows = queries.reshape(queries.shape[0], HEADS, HD)
    logits = jnp.einsum('qhd,kd->hqk', head_rows, local_keys, precision=highest)
    scores = jnp.where(allowed[None], low_back(logits * HD ** (-0.5)), masked_score)
    maximum = lax.optimization_barrier(jnp.max(scores, axis=2, keepdims=True))
    exponent = jnp.exp(scores - maximum)
    totals = lax.optimization_barrier(jnp.sum(exponent, axis=2))
    unscaled = low_back(jnp.einsum('hqk,kd->qhd', low(exponent), local_values, precision=highest))
    attention = unscaled / jnp.transpose(totals)[:, :, None]
    mixed_rows = low(attention.reshape(attention.shape[0], HEADS * HD))
    lead_hidden = lead_rows + low_back(project(mixed_rows[:lead_count], prefix_mixer.T))
    tail_hidden = tail_rows + low_back(project(mixed_rows[lead_count:], action_mixer.T))
    lead_final = lead_hidden + feed_forward(lead_hidden, prefix_midnorm, prefix_gate, prefix_expand, prefix_down)
    tail_final = tail_hidden + feed_forward(tail_hidden, action_midnorm, action_gate, action_expand, action_down)
    return (lead_final, tail_final)

def reference(prefix_tokens, action_tokens, prefix_cotangent, action_cotangent, prefix_segments, action_codes, prefix_query, prefix_key, prefix_value, prefix_mixer, action_query, action_key, action_value, action_mixer, prefix_prenorm, prefix_midnorm, action_prenorm, action_midnorm, prefix_gate, prefix_expand, prefix_down, action_gate, action_expand, action_down):
    row_count = prefix_segments.shape[0]
    weight_set = tuple((matrix.astype(jnp.float32) for matrix in (prefix_query, prefix_key, prefix_value, prefix_mixer, action_query, action_key, action_value, action_mixer, prefix_prenorm, prefix_midnorm, action_prenorm, action_midnorm, prefix_gate, prefix_expand, prefix_down, action_gate, action_expand, action_down)))
    lead_all = prefix_tokens.astype(jnp.float32).reshape(row_count, -1, prefix_tokens.shape[1])
    tail_all = action_tokens.astype(jnp.float32).reshape(row_count, -1, action_tokens.shape[1])
    lead_cot = prefix_cotangent.astype(jnp.float32).reshape(row_count, -1, prefix_tokens.shape[1])
    tail_cot = action_cotangent.astype(jnp.float32).reshape(row_count, -1, action_tokens.shape[1])

    def forward(lead_input, tail_input, weights_now):

        def row_step(row_data):
            return single_row(weights_now, row_data)
        return lax.map(jax.checkpoint(row_step), (lead_input, tail_input, prefix_segments, action_codes))
    outputs, pullback = jax.vjp(forward, lead_all, tail_all, weight_set)
    lead_grad, tail_grad, weight_grads = pullback((lead_cot, tail_cot))
    return (outputs[0].reshape(prefix_tokens.shape).astype(jnp.bfloat16), outputs[1].reshape(action_tokens.shape).astype(jnp.bfloat16), lead_grad.reshape(prefix_tokens.shape).astype(jnp.bfloat16), tail_grad.reshape(action_tokens.shape).astype(jnp.bfloat16), weight_grads[0], weight_grads[1], weight_grads[2], weight_grads[3], weight_grads[4], weight_grads[5], weight_grads[6], weight_grads[7], weight_grads[8], weight_grads[9], weight_grads[10], weight_grads[11], weight_grads[12], weight_grads[13], weight_grads[14], weight_grads[15], weight_grads[16], weight_grads[17])
```

```python
import functools

import jax
import jax.numpy as jnp
from jax import lax
from jax.experimental import pallas as pl
from jax.experimental.pallas import tpu as pltpu
from jax.sharding import PartitionSpec as P

ACTT = 32


epsilon = 1e-06
masked_score = -1e30


class Place:
    def __init__(self, depth, breadth):
        self.depth, self.breadth = depth, breadth
        row, member = lax.axis_index("rows"), lax.axis_index("cam")
        self.z, self.y = row // 2, row % 2
        self.x, self.k = member // 2, member % 2

    def device(self, z=None, y=None, x=None, k=None):
        z = self.z if z is None else z
        y = self.y if y is None else y
        x = self.x if x is None else x
        k = self.k if k is None else k
        return (z * 2 + y, x * 2 + k)

    def later_x(self, step):
        return lax.rem(self.x + step, self.breadth)

    def later_z(self, step):
        return lax.rem(self.z + step, self.depth)


def guarded(condition, action):
    if condition is None:
        action()
    else:
        pl.when(condition)(action)


class Transfer:
    def __init__(self, net, source, target, device, sends=None, gets=None):
        self.net, self.number = net, net.remote
        net.remote += 1
        self.source, self.target, self.device = source, target, device
        self.sends, self.gets = sends, gets
        net.pending.append(self)

    def describe(self):
        return pltpu.make_async_remote_copy(
            src_ref=self.source(),
            dst_ref=self.target(),
            send_sem=self.net.sent.at[self.number],
            recv_sem=self.net.received.at[self.number],
            device_id=self.device,
            device_id_type=pl.DeviceIdType.MESH,
        )

    def start(self):
        guarded(self.sends, lambda: self.describe().start())

    def got(self):
        guarded(self.gets, lambda: self.describe().wait_recv())

    def finish(self):
        guarded(self.sends, lambda: self.describe().wait_send())


class Local:
    def __init__(self, net, source, target):
        self.net, self.number = net, net.local
        net.local += 1
        self.source, self.target = source, target

    def describe(self):
        return pltpu.make_async_copy(
            self.source(), self.target(), self.net.moved.at[self.number]
        )

    def start(self):
        self.describe().start()
        return self

    def wait(self):
        self.describe().wait()


class Net:
    def __init__(self, sent, received, moved):
        self.sent, self.received, self.moved = sent, received, moved
        self.remote, self.local = 0, 0
        self.pending = []

    def settle(self):
        for transfer in self.pending:
            transfer.finish()


def greet(at, kinds):
    peers = []
    count = 0
    if "z" in kinds and "deal" not in kinds:
        count = count + (at.z > 0).astype(jnp.int32) + (at.z < at.depth - 1).astype(jnp.int32)
        peers.append((at.z > 0, at.device(z=at.z - 1)))
        peers.append((at.z < at.depth - 1, at.device(z=at.z + 1)))
    if "deal" in kinds:
        peers += [(None, at.device(z=at.later_z(step))) for step in range(1, at.depth)]
    if "y" in kinds:
        peers.append((None, at.device(y=1 - at.y)))
    if "cam" in kinds:
        for step in range(at.breadth):
            for core in (at.k, 1 - at.k):
                if step > 0 or core is not at.k:
                    peers.append((None, at.device(x=at.later_x(step), k=core)))
    barrier = pltpu.get_barrier_semaphore()
    for condition, device in peers:
        guarded(
            condition,
            lambda device=device: pl.semaphore_signal(
                barrier, inc=1, device_id=device, device_id_type=pl.DeviceIdType.MESH
            ),
        )
    count = count + sum(1 for condition, _ in peers if condition is None)
    pl.semaphore_wait(barrier, count)


def run_all(routines):
    routines = list(routines)
    while routines:
        alive = []
        for routine in routines:
            try:
                next(routine)
                alive.append(routine)
            except StopIteration:
                pass
        routines = alive


def add_rows(target, first, second):
    count = target.shape[0]
    step = 16 if count % 16 == 0 else 8

    def one(index, carry):
        rows = pl.ds(pl.multiple_of(index * step, step), step)
        total = first[rows, :].astype(jnp.float32) + second[rows, :].astype(jnp.float32)
        target[rows, :] = total.astype(target.dtype)
        return carry

    lax.fori_loop(0, count // step, one, 0)


def widen_rows(target, source):
    count = target.shape[0]
    step = 16 if count % 16 == 0 else 8

    def one(index, carry):
        rows = pl.ds(pl.multiple_of(index * step, step), step)
        target[rows, :] = source[rows, :].astype(target.dtype)
        return carry

    lax.fori_loop(0, count // step, one, 0)


class Chain:
    def __init__(self, net, at, own, place):
        depth = at.depth
        self.up, self.down = {}, {}
        for step in range(1, depth):
            low, high = at.z - step + 1, at.z + step - 1
            self.up[step] = Transfer(
                net,
                own if step == 1 else (lambda low=low: place(low)),
                lambda low=low: place(low),
                at.device(z=at.z + 1),
                sends=(at.z + 1 < depth) & (low >= 0),
                gets=at.z - step >= 0,
            )
            self.down[step] = Transfer(
                net,
                own if step == 1 else (lambda high=high: place(high)),
                lambda high=high: place(high),
                at.device(z=at.z - 1),
                sends=(at.z > 0) & (high < depth),
                gets=at.z + step < depth,
            )


def tags_of(at, chained):
    tags = [("own", at.z, None)]
    if chained:
        for step in range(1, at.depth):
            tags.append((("up", step), at.z - step, at.z - step >= 0))
            tags.append((("down", step), at.z + step, at.z + step < at.depth))
    return tags


def spread(net, at, shards, outs, chained):
    if chained:
        place = lambda out, z, x, k: out.at[z, x, k]
    else:
        place = lambda out, z, x, k: out.at[x, k]
    tags = tags_of(at, chained)
    chains, across, partner, locals_ = [], {}, {}, []
    for i, (shard, out) in enumerate(zip(shards, outs)):
        own = lambda shard=shard: shard
        if chained:
            chains.append(
                Chain(net, at, own, lambda z, out=out: place(out, z, at.x, at.k))
            )
        locals_.append(Local(net, own, lambda out=out: place(out, at.z, at.x, at.k)))
        for name, z, condition in tags:
            held = own if name == "own" else (lambda out=out, z=z: place(out, z, at.x, at.k))
            target = lambda out=out, z=z: place(out, z, at.x, at.k)
            partner[i, name, 0] = Transfer(
                net, held, target, at.device(k=1 - at.k), condition, condition
            )
            for step in range(1, at.breadth):
                across[i, name, step] = Transfer(
                    net, held, target, at.device(x=at.later_x(step)), condition, condition
                )
                other = at.later_x(at.breadth - step)
                arrived = lambda out=out, z=z, other=other: place(out, z, other, at.k)
                partner[i, name, step] = Transfer(
                    net, arrived, arrived, at.device(k=1 - at.k), condition, condition
                )
    count = len(shards)

    def launch(name):
        for i in range(count):
            for step in range(1, at.breadth):
                across[i, name, step].start()
        for i in range(count):
            partner[i, name, 0].start()

    def forward(name):
        for i in range(count):
            for step in range(1, at.breadth):
                across[i, name, step].got()
                partner[i, name, step].start()

    for chain in chains:
        chain.up[1].start()
        chain.down[1].start()
    launch("own")
    for move in locals_:
        move.start()
    yield
    previous = ["own"]
    if chained:
        for step in range(1, at.depth):
            for chain in chains:
                chain.up[step].got()
                if step + 1 < at.depth:
                    chain.up[step + 1].start()
            launch(("up", step))
            yield
            for chain in chains:
                chain.down[step].got()
                if step + 1 < at.depth:
                    chain.down[step + 1].start()
            launch(("down", step))
            yield
            for name in previous:
                forward(name)
            previous = [("up", step), ("down", step)]
    for name in previous:
        yield
        forward(name)
    yield
    for transfer in partner.values():
        transfer.got()
    for move in locals_:
        move.wait()


def fan(net, at, packs, outs):
    members = 2 * at.breadth
    swap, chains, across, locals_ = {}, [], {}, []
    mine = at.x * 2 + at.k
    for i, (pack, out) in enumerate(zip(packs, outs)):
        slot = lambda out=out: out.at[at.z, at.y, mine]
        locals_.append(Local(net, lambda pack=pack: pack.at[mine], slot))
        for step in range(at.breadth):
            for flip in (0, 1):
                if step == 0 and flip == 0:
                    continue
                x = at.later_x(step)
                k = 1 - at.k if flip else at.k
                swap[i, step, flip] = Transfer(
                    net,
                    lambda pack=pack, x=x, k=k: pack.at[x * 2 + k],
                    slot,
                    at.device(x=x, k=k),
                )
        block = lambda z, out=out: out.at[z, at.y]
        chains.append(Chain(net, at, lambda block=block: block(at.z), block))
        for name, z, condition in tags_of(at, True):
            held = lambda block=block, z=z: block(z)
            across[i, name] = Transfer(
                net, held, held, at.device(y=1 - at.y), condition, condition
            )
    for transfer in swap.values():
        transfer.start()
    for move in locals_:
        move.start()
    yield
    for transfer in swap.values():
        transfer.got()
    for move in locals_:
        move.wait()
    count = len(packs)
    for chain in chains:
        chain.up[1].start()
        chain.down[1].start()
    for i in range(count):
        across[i, "own"].start()
    for step in range(1, at.depth):
        yield
        for chain in chains:
            chain.up[step].got()
            if step + 1 < at.depth:
                chain.up[step + 1].start()
        for i in range(count):
            across[i, ("up", step)].start()
        yield
        for chain in chains:
            chain.down[step].got()
            if step + 1 < at.depth:
                chain.down[step + 1].start()
        for i in range(count):
            across[i, ("down", step)].start()
    yield
    for transfer in across.values():
        transfer.got()


def deal(net, at, sources, outs, stages):
    moves, across, loads, stores = {}, {}, [], []
    for i, (source, out, stage) in enumerate(zip(sources, outs, stages)):
        slot = lambda out=out: out.at[at.z, at.y]
        held = lambda stage=stage: stage
        loads.append(Local(net, lambda source=source: source(at.z), held))
        stores.append(Local(net, held, slot))
        across[i, 0] = Transfer(net, held, slot, at.device(y=1 - at.y))
        for step in range(1, at.depth):
            z = at.later_z(step)
            moves[i, step] = Transfer(
                net, lambda source=source, z=z: source(z), slot, at.device(z=z)
            )
            origin = at.later_z(at.depth - step)
            arrived = lambda out=out, origin=origin: out.at[origin, at.y]
            across[i, step] = Transfer(net, arrived, arrived, at.device(y=1 - at.y))
    for load in loads:
        load.start()
    count = len(loads)
    for i in range(count):
        for step in range(1, at.depth):
            moves[i, step].start()
    yield
    for i in range(count):
        loads[i].wait()
        stores[i].start()
        across[i, 0].start()
    for i in range(count):
        for step in range(1, at.depth):
            yield
            moves[i, step].got()
            across[i, step].start()
    yield
    for transfer in across.values():
        transfer.got()
    for store in stores:
        store.wait()


def chain_sum(net, at, own, up, down):
    rise, fall = {}, {}
    for t in range(at.depth):
        rise[t] = Transfer(
            net,
            lambda t=t: own(t),
            lambda t=t: up(t),
            at.device(z=at.z + 1),
            sends=at.z < t,
            gets=(at.z > 0) & (at.z <= t),
        )
        fall[t] = Transfer(
            net,
            lambda t=t: own(t),
            lambda t=t: down(t),
            at.device(z=at.z - 1),
            sends=at.z > t,
            gets=(at.z < at.depth - 1) & (at.z >= t),
        )
    return rise, fall


def edges_first(depth):
    order = []
    for i in range((depth + 1) // 2):
        order.append(depth - 1 - i)
        if i != depth - 1 - i:
            order.append(i)
    return order


def collect(net, at, parts, outs, buffers, chained):
    depth = at.depth if chained else 1
    order = edges_first(depth)
    part_of = (
        (lambda part, t, x, k: part.at[t, x, k]) if chained else (lambda part, t, x, k: part.at[x, k])
    )
    loads, partner, across, chains = {}, {}, {}, []
    for i, (part, buffer) in enumerate(zip(parts, buffers)):
        own, core, wide = buffer["own"], buffer["core"], buffer["wide"]
        for t in order:
            for step in range(at.breadth):
                x = at.later_x(step)
                loads[i, t, step] = Local(
                    net,
                    lambda part=part, t=t, x=x: part_of(part, t, x, at.k),
                    lambda own=own, t=t, x=x: own.at[t, x],
                )
                partner[i, t, step] = Transfer(
                    net,
                    lambda part=part, t=t, x=x: part_of(part, t, x, 1 - at.k),
                    lambda core=core, t=t, x=x: core.at[t, x],
                    at.device(k=1 - at.k),
                )
                if step > 0:
                    across[i, t, step] = Transfer(
                        net,
                        lambda own=own, t=t, x=x: own.at[t, x],
                        lambda wide=wide, t=t, step=step: wide.at[step - 1, t],
                        at.device(x=x),
                    )
        if chained:
            chains.append(
                chain_sum(
                    net,
                    at,
                    lambda t, own=own: own.at[t, at.x],
                    lambda t, buffer=buffer: buffer["up"].at[t],
                    lambda t, buffer=buffer: buffer["down"].at[t],
                )
            )
    steps = list(range(1, at.breadth)) + [0]
    count = len(parts)
    for i in range(count):
        for t in order:
            for step in steps:
                partner[i, t, step].start()
                loads[i, t, step].start()
    for i in range(count):
        own, core = buffers[i]["own"], buffers[i]["core"]
        for t in order:
            yield
            for step in steps:
                x = at.later_x(step)
                loads[i, t, step].wait()
                partner[i, t, step].got()
                add_rows(own.at[t, x], own.at[t, x], core.at[t, x])
            for step in steps[:-1]:
                across[i, t, step].start()
    for i in range(count):
        buffer = buffers[i]
        own, wide = buffer["own"], buffer["wide"]
        for t in order:
            yield
            for step in steps[:-1]:
                across[i, t, step].got()
                last = not chained and step == steps[-2]
                target = outs[i] if last else own.at[t, at.x]
                add_rows(target, own.at[t, at.x], wide.at[step - 1, t])
            if chained:
                rise, fall = chains[i]
                yield

                def finish(i=i, t=t, buffer=buffer, rise=rise, fall=fall):
                    widen_rows(outs[i], buffer["own"].at[t, at.x])
                    for moves, name in ((rise, "up"), (fall, "down")):

                        def more(moves=moves, name=name):
                            moves[t].describe().wait_recv()
                            add_rows(outs[i], outs[i], buffer[name].at[t])

                        pl.when(moves[t].gets)(more)

                def passing(t=t, buffer=buffer, rise=rise, fall=fall):
                    for moves, name in ((rise, "up"), (fall, "down")):

                        def more(moves=moves, name=name):
                            moves[t].describe().wait_recv()
                            held = buffer["own"].at[t, at.x]
                            add_rows(held, held, buffer[name].at[t])

                        pl.when(moves[t].gets)(more)

                pl.when(at.z == t)(finish)
                pl.when(at.z != t)(passing)
                rise[t].start()
                fall[t].start()


def give_back(net, at, parts, slots, buffers):
    loads, across, moves, stores = {}, {}, {}, []
    for i, (part, buffer) in enumerate(zip(parts, buffers)):
        own, core = buffer["own"], buffer["core"]
        for step in range(at.depth):
            z = at.later_z(step)
            loads[i, step] = Local(
                net,
                lambda part=part, z=z: part.at[z, at.y],
                lambda own=own, z=z: own.at[z],
            )
            across[i, step] = Transfer(
                net,
                lambda part=part, z=z: part.at[z, 1 - at.y],
                lambda core=core, z=z: core.at[z],
                at.device(y=1 - at.y),
            )
            if step > 0:
                moves[i, step] = Transfer(
                    net,
                    lambda own=own, z=z: own.at[z],
                    lambda i=i: slots[i](at.z),
                    at.device(z=z),
                )
            else:
                stores.append(
                    Local(net, lambda own=own: own.at[at.z], lambda i=i: slots[i](at.z))
                )
    count = len(parts)
    steps = list(range(1, at.depth)) + [0]
    for i in range(count):
        for step in steps:
            loads[i, step].start()
            across[i, step].start()
    for i in range(count):
        own, core = buffers[i]["own"], buffers[i]["core"]
        for step in steps:
            yield
            z = at.later_z(step)
            loads[i, step].wait()
            across[i, step].got()
            add_rows(own.at[z], own.at[z], core.at[z])
            if step > 0:
                moves[i, step].start()
            else:
                stores[i].start()
    for transfer in moves.values():
        yield
        transfer.got()
    for store in stores:
        store.wait()


def fold(net, at, parts, outs, buffers):
    mine = at.x * 2 + at.k
    members = 2 * at.breadth
    order = edges_first(at.depth)
    loads, across, chains, swap, stores = {}, {}, [], {}, []
    for i, (part, buffer) in enumerate(zip(parts, buffers)):
        own, core = buffer["own"], buffer["core"]
        for t in order:
            loads[i, t] = Local(
                net, lambda part=part, t=t: part.at[t, at.y], lambda own=own, t=t: own.at[t]
            )
            across[i, t] = Transfer(
                net,
                lambda part=part, t=t: part.at[t, 1 - at.y],
                lambda core=core, t=t: core.at[t],
                at.device(y=1 - at.y),
            )
        chains.append(
            chain_sum(
                net,
                at,
                lambda t, own=own: own.at[t],
                lambda t, buffer=buffer: buffer["up"].at[t],
                lambda t, buffer=buffer: buffer["down"].at[t],
            )
        )
        slot = lambda i=i: outs[i].at[mine]
        stores.append(Local(net, lambda own=own: own.at[at.z, mine], slot))
        for step in range(at.breadth):
            for flip in (0, 1):
                if step == 0 and flip == 0:
                    continue
                x = at.later_x(step)
                k = 1 - at.k if flip else at.k
                swap[i, step, flip] = Transfer(
                    net,
                    lambda own=own, x=x, k=k: own.at[at.z, x * 2 + k],
                    slot,
                    at.device(x=x, k=k),
                )
    count = len(parts)
    for i in range(count):
        for t in order:
            across[i, t].start()
            loads[i, t].start()
    for i in range(count):
        buffer = buffers[i]
        own, core = buffer["own"], buffer["core"]
        rise, fall = chains[i]
        for t in order:
            yield
            loads[i, t].wait()
            across[i, t].got()
            for member in range(members):
                add_rows(own.at[t, member], own.at[t, member], core.at[t, member])
            yield
            for moves, name in ((rise, "up"), (fall, "down")):

                def more(moves=moves, name=name, t=t, own=own, buffer=buffer):
                    moves[t].describe().wait_recv()
                    for member in range(members):
                        held = own.at[t, member]
                        add_rows(held, held, buffer[name].at[t, member])

                pl.when(moves[t].gets)(more)
            rise[t].start()
            fall[t].start()
        stores[i].start()
        for (j, step, flip), transfer in swap.items():
            if j == i:
                transfer.start()
    yield
    for transfer in swap.values():
        transfer.got()
    for store in stores:
        store.wait()


def exchange(label, ident, sizes, kinds, inputs, outputs, scratch, routines):
    space = lambda inside: pltpu.VMEM if inside else pl.ANY

    def kernel(*refs):
        sources = refs[: len(inputs)]
        targets = refs[len(inputs) : len(inputs) + len(outputs)]
        held = refs[len(inputs) + len(outputs) : -3]
        at, net = Place(*sizes), Net(*refs[-3:])
        greet(at, kinds)
        run_all(routines(net, at, sources, targets, held))
        net.settle()

    slots = 48 * sizes[0]
    return pl.pallas_call(
        kernel,
        name=label,
        out_shape=[shape for shape, _ in outputs],
        in_specs=[pl.BlockSpec(memory_space=space(inside)) for _, inside in inputs],
        out_specs=[pl.BlockSpec(memory_space=space(inside)) for _, inside in outputs],
        scratch_shapes=list(scratch)
        + [pltpu.SemaphoreType.DMA((slots,))] * 2
        + [pltpu.SemaphoreType.DMA((slots,))],
        compiler_params=pltpu.CompilerParams(
            collective_id=ident, has_side_effects=True, vmem_limit_bytes=60 << 20
        ),
    )(*[array for array, _ in inputs])


def shape_of(dims, kind=jnp.bfloat16):
    return jax.ShapeDtypeStruct(tuple(dims), kind)


def multiply(operand, matrix):
    return jnp.dot(operand, matrix, preferred_element_type=jnp.float32)


def against(operand, matrix):
    return lax.dot_general(
        operand, matrix, (((1,), (1,)), ((), ())), preferred_element_type=jnp.float32
    )


def outer_sum(operand, matrix):
    return lax.dot_general(
        operand, matrix, (((0,), (0,)), ((), ())), preferred_element_type=jnp.float32
    )


def norm_forward(values):
    scaling = lax.rsqrt(jnp.mean(values * values, axis=-1, keepdims=True) + epsilon)
    return (values * scaling, scaling)


def norm_backward(upstream, normed_unit, scaling, gain_vector):
    weighted = upstream * gain_vector
    average = jnp.mean(weighted * normed_unit, axis=-1, keepdims=True)
    return (scaling * (weighted - normed_unit * average), jnp.sum(upstream * normed_unit, axis=0))


def visible(query_ids, query_codes, key_ids, key_codes):
    matches = query_ids[:, None] == key_ids[None, :]
    return jnp.logical_and(matches, key_codes[None, :] <= query_codes[:, None])


def gated(gate_value, expand_value):
    return jax.nn.gelu(gate_value, approximate=True) * expand_value


def low(values):
    return values.astype(jnp.bfloat16)


def feed_forward(normed_rows, cotangent, gate_weight, expand_weight, down_weight):
    gate_value = multiply(normed_rows, gate_weight)
    expand_value = multiply(normed_rows, expand_weight)
    inside, pullback = jax.vjp(gated, gate_value, expand_value)
    inside_low = low(inside)
    part = low(against(inside_low, down_weight))
    inside_grad = multiply(cotangent, down_weight)
    gate_grad, expand_grad = pullback(inside_grad)
    gate_low, expand_low = low(gate_grad), low(expand_grad)
    normed_grad = low(against(gate_low, gate_weight) + against(expand_low, expand_weight))
    weight_grads = (
        outer_sum(normed_rows, gate_low),
        outer_sum(normed_rows, expand_low),
        outer_sum(cotangent, inside_low),
    )
    return (part, normed_grad, weight_grads)


def by_member(parts, members):
    rows = parts[0].shape[0]
    columns = jnp.concatenate([part.reshape(rows, members, -1) for part in parts], 2)
    return jnp.swapaxes(columns, 0, 1)


def body(
    prefix_tokens,
    action_tokens,
    prefix_cotangent,
    action_cotangent,
    prefix_segments,
    action_codes,
    prefix_query,
    prefix_key,
    prefix_value,
    prefix_mixer,
    action_query,
    action_key,
    action_value,
    action_mixer,
    prefix_prenorm,
    prefix_midnorm,
    action_prenorm,
    action_midnorm,
    prefix_gate,
    prefix_expand,
    prefix_down,
    action_gate,
    action_expand,
    action_down,
):
    members = lax.axis_size("cam")
    row_count = lax.axis_size("rows")
    depth, breadth = row_count // 2, members // 2
    sizes = (depth, breadth)
    head_size = prefix_key.shape[1]
    width = prefix_query.shape[1] // members
    heads = width // head_size
    pair = 2 * head_size // members
    inverse = float(head_size) ** (-0.5)
    lead_count, lead_width = prefix_tokens.shape
    tail_count, tail_width = action_tokens.shape
    idents = iter(range(100))

    def cam_spread(label, shards):
        return exchange(
            label,
            next(idents),
            sizes,
            ("cam",),
            [(shard, True) for shard in shards],
            [(shape_of((breadth, 2) + shard.shape), False) for shard in shards],
            [],
            lambda net, at, ins, outs, held: [spread(net, at, ins, outs, False)],
        )

    def cam_collect(label, parts):
        blocks = [part.shape[-2:] for part in parts]
        scratch = []
        for block in blocks:
            scratch += [
                pltpu.VMEM((1, breadth) + block, jnp.bfloat16),
                pltpu.VMEM((1, breadth) + block, jnp.bfloat16),
                pltpu.VMEM((breadth - 1, 1) + block, jnp.bfloat16),
            ]

        def routines(net, at, ins, outs, held):
            buffers = [
                dict(own=held[3 * i], core=held[3 * i + 1], wide=held[3 * i + 2])
                for i in range(len(parts))
            ]
            return [collect(net, at, ins, outs, buffers, False)]

        return exchange(
            label,
            next(idents),
            sizes,
            ("cam",),
            [(part, False) for part in parts],
            [(shape_of(block, jnp.float32), True) for block in blocks],
            scratch,
            routines,
        )

    lead_float = prefix_tokens.astype(jnp.float32)
    tail_float = action_tokens.astype(jnp.float32)
    lead_unit, lead_scale = norm_forward(lead_float)
    tail_unit, tail_scale = norm_forward(tail_float)
    lead_low = low(lead_unit * prefix_prenorm)
    tail_low = low(tail_unit * action_prenorm)
    lead_pack = by_member([prefix_query, jnp.concatenate([prefix_key, prefix_value], 1)], members)
    tail_pack = by_member([action_query, jnp.concatenate([action_key, action_value], 1)], members)
    first = [lead_low, tail_low, lead_pack, tail_pack]
    fanned = lambda pack: (shape_of((depth, 2) + pack.shape), False)
    lead_normed, tail_normed, lead_in, tail_in = exchange(
        "first",
        next(idents),
        sizes,
        ("z", "y", "cam"),
        [(array, True) for array in first],
        [(shape_of((breadth, 2) + array.shape), False) for array in first[:2]]
        + [fanned(lead_pack), fanned(tail_pack)],
        [],
        lambda net, at, ins, outs, held: [
            fan(net, at, ins[2:], outs[2:]),
            spread(net, at, ins[:2], outs[:2], False),
        ],
    )
    lead_normed = lead_normed.reshape(-1, lead_width)
    tail_normed = tail_normed.reshape(-1, tail_width)
    member_place = lax.axis_index("cam")
    lead_in = lead_in.reshape(lead_width, -1)
    tail_in = tail_in.reshape(tail_width, -1)
    lead_total, tail_total = lead_normed.shape[0], tail_normed.shape[0]

    projected = low(
        jnp.concatenate([multiply(lead_normed, lead_in), multiply(tail_normed, tail_in)], 0)
    )
    (pairs,) = cam_spread("pairs", [projected[:, width:]])
    pairs = jnp.swapaxes(pairs.reshape(members, -1, pair), 0, 1).reshape(-1, 2 * head_size)

    lead_mixers = by_member([prefix_mixer], members)
    tail_mixers = by_member([action_mixer], members)
    lead_slice = prefix_gate.shape[1] // depth
    tail_slice = action_gate.shape[1] // depth
    lead_block, tail_block = prefix_gate.shape[0], action_gate.shape[0]
    tail_weights = [
        jnp.swapaxes(weight.reshape(tail_block, depth, tail_slice), 0, 1)
        for weight in (action_gate, action_expand, action_down)
    ]
    second = (
        [(prefix_gate, False), (prefix_expand, False), (prefix_down, False)]
        + [(weight, False) for weight in tail_weights]
        + [(lead_mixers, True), (tail_mixers, True)]
    )

    def second_routines(net, at, ins, outs, held):
        def columns(ref):
            return lambda z: ref.at[
                :, pl.ds(pl.multiple_of(z * lead_slice, lead_slice), lead_slice)
            ]

        def planes(ref):
            return lambda z: ref.at[z]

        sources = [columns(ref) for ref in ins[:3]] + [planes(ref) for ref in ins[3:6]]
        return [
            fan(net, at, ins[6:8], outs[6:8]),
            deal(net, at, sources, outs[:6], held),
        ]

    dealt = exchange(
        "second",
        next(idents),
        sizes,
        ("z", "deal", "y", "cam"),
        second,
        [(shape_of((depth, 2, lead_block, lead_slice)), False)] * 3
        + [(shape_of((depth, 2, tail_block, tail_slice)), False)] * 3
        + [fanned(lead_mixers), fanned(tail_mixers)],
        [pltpu.VMEM((lead_block, lead_slice), jnp.bfloat16)] * 3
        + [pltpu.VMEM((tail_block, tail_slice), jnp.bfloat16)] * 3,
        second_routines,
    )
    lead_gate, lead_expand, lead_down = [w.reshape(lead_width, lead_slice) for w in dealt[:3]]
    tail_gate, tail_expand, tail_down = [w.reshape(tail_width, tail_slice) for w in dealt[3:6]]
    mine = lambda fans, total: fans.reshape(total, width)
    lead_mix, tail_mix = mine(dealt[6], lead_width), mine(dealt[7], tail_width)

    segment_row = prefix_segments[0]
    code_row = action_codes[0]
    token_ids = jnp.concatenate(
        [segment_row, jnp.arange(code_row.shape[0], dtype=jnp.int32) // ACTT]
    )
    token_codes = jnp.concatenate([jnp.zeros(segment_row.shape, jnp.int32), code_row])
    queries = projected[:, :width].reshape(-1, heads, head_size)
    keys, values = pairs[:, :head_size], pairs[:, head_size:]
    allowed = visible(token_ids, token_codes, token_ids, token_codes)
    logits = jnp.einsum("qhd,kd->hqk", queries, keys, preferred_element_type=jnp.float32) * inverse
    scores = jnp.where(allowed[None], logits, masked_score)
    exponent = jnp.exp(scores - jnp.max(scores, axis=2, keepdims=True))
    totals = jnp.transpose(jnp.sum(exponent, axis=2))[:, :, None]
    probs = low(exponent)
    attention = (
        jnp.einsum("hqk,kd->qhd", probs, values, preferred_element_type=jnp.float32) / totals
    )
    mixed = low(attention.reshape(-1, width))
    cam_blocks = lambda rows: low(rows).reshape(breadth, 2, -1, rows.shape[1])
    lead_sum, tail_sum = cam_collect(
        "mixing",
        [
            cam_blocks(against(mixed[:lead_total], lead_mix)),
            cam_blocks(against(mixed[lead_total:], tail_mix)),
        ],
    )
    lead_hidden = lead_float + lead_sum
    tail_hidden = tail_float + tail_sum
    lead_center, lead_factor = norm_forward(lead_hidden)
    tail_center, tail_factor = norm_forward(tail_hidden)
    lead_second = low(lead_center * prefix_midnorm)
    tail_second = low(tail_center * action_midnorm)

    chunks = max(1, depth // 4)
    lead_rows, tail_rows = lead_count // chunks, tail_count // chunks
    sums, grads = [], None
    for chunk in range(chunks):
        cut = lambda array: array.reshape(chunks, -1, array.shape[1])[chunk]
        shards = [cut(prefix_cotangent), cut(action_cotangent), cut(lead_second), cut(tail_second)]
        if chunk > 0:
            shards, sums = lax.optimization_barrier((shards, sums))
        gathered = exchange(
            "gather" + str(chunk),
            next(idents),
            sizes,
            ("z", "cam"),
            [(shard, True) for shard in shards],
            [(shape_of((depth, breadth, 2) + shard.shape), False) for shard in shards],
            [],
            lambda net, at, ins, outs, held: [
                spread(net, at, ins[2:], outs[2:], True),
                spread(net, at, ins[:2], outs[:2], True),
            ],
        )
        lead_upper, tail_upper, lead_all, tail_all = [
            array.reshape(-1, array.shape[-1]) for array in gathered
        ]
        lead_out, lead_back, lead_ffgrads = feed_forward(
            lead_all, lead_upper, lead_gate, lead_expand, lead_down
        )
        tail_out, tail_back, tail_ffgrads = feed_forward(
            tail_all, tail_upper, tail_gate, tail_expand, tail_down
        )
        fresh = list(lead_ffgrads) + list(tail_ffgrads)
        grads = fresh if grads is None else [one + other for one, other in zip(grads, fresh)]
        last = chunk + 1 == chunks
        parts = [
            rows.reshape(depth, breadth, 2, -1, rows.shape[1])
            for rows in (lead_back, tail_back, lead_out, tail_out)
        ]
        blocks = [part.shape[3:] for part in parts]
        scratch = []
        for block in blocks:
            scratch += [
                pltpu.VMEM((depth, breadth) + block, jnp.bfloat16),
                pltpu.VMEM((depth, breadth) + block, jnp.bfloat16),
                pltpu.VMEM((breadth - 1, depth) + block, jnp.bfloat16),
                pltpu.VMEM((depth,) + block, jnp.bfloat16),
                pltpu.VMEM((depth,) + block, jnp.bfloat16),
            ]

        def routines(net, at, ins, outs, held):
            names = ("own", "core", "wide", "up", "down")
            buffers = [dict(zip(names, held[5 * i : 5 * i + 5])) for i in range(len(parts))]
            return [collect(net, at, ins, outs, buffers, True)]

        sums.append(
            exchange(
                "collect" + str(chunk),
                next(idents),
                sizes,
                ("z", "cam"),
                [(part, False) for part in parts],
                [(shape_of(block, jnp.float32), True) for block in blocks],
                scratch,
                routines,
            )
        )
    lead_summed, tail_summed, lead_branch, tail_branch = [
        parts[0] if chunks == 1 else jnp.concatenate(parts, 0) for parts in zip(*sums)
    ]
    lead_result = low(lead_hidden + lead_branch)
    tail_result = low(tail_hidden + tail_branch)

    grads = [low(grad) for grad in grads]
    lead_returns = [grad.reshape(depth, 2, lead_block, lead_slice) for grad in grads[:3]]
    tail_returns = [grad.reshape(depth, 2, tail_block, tail_slice) for grad in grads[3:]]

    def return_routines(net, at, ins, outs, held):
        def columns(ref):
            return lambda z: ref.at[
                :, pl.ds(pl.multiple_of(z * lead_slice, lead_slice), lead_slice)
            ]

        def planes(ref):
            return lambda z: ref.at[z]

        slots = [columns(ref) for ref in outs[:3]] + [planes(ref) for ref in outs[3:]]
        buffers = [dict(own=held[2 * i], core=held[2 * i + 1]) for i in range(6)]
        return [give_back(net, at, ins, slots, buffers)]

    returned = exchange(
        "returns",
        next(idents),
        sizes,
        ("deal", "y"),
        [(part, False) for part in lead_returns + tail_returns],
        [(shape_of(prefix_gate.shape), False)] * 3
        + [(shape_of((depth, tail_block, tail_slice)), False)] * 3,
        [pltpu.VMEM((depth, lead_block, lead_slice), jnp.bfloat16)] * 6
        + [pltpu.VMEM((depth, tail_block, tail_slice), jnp.bfloat16)] * 6,
        return_routines,
    )
    ff_grads = [part.astype(jnp.float32) for part in returned[:3]] + [
        jnp.swapaxes(part, 0, 1).reshape(tail_block, -1).astype(jnp.float32)
        for part in returned[3:]
    ]

    lead_residual, lead_middle = norm_backward(
        lead_summed, lead_center, lead_factor, prefix_midnorm
    )
    tail_residual, tail_middle = norm_backward(
        tail_summed, tail_center, tail_factor, action_midnorm
    )
    lead_upstream = prefix_cotangent.astype(jnp.float32) + lead_residual
    tail_upstream = action_cotangent.astype(jnp.float32) + tail_residual
    lead_sent, tail_sent = cam_spread("sent", [low(lead_upstream), low(tail_upstream)])
    lead_sent = lead_sent.reshape(-1, lead_width)
    tail_sent = tail_sent.reshape(-1, tail_width)
    lead_mixing = outer_sum(lead_sent, mixed[:lead_total])
    tail_mixing = outer_sum(tail_sent, mixed[lead_total:])
    attention_grad = jnp.concatenate(
        [multiply(lead_sent, lead_mix), multiply(tail_sent, tail_mix)], 0
    ).reshape(-1, heads, head_size)
    scaled_grad = low(attention_grad / totals)
    deltas = jnp.sum(attention_grad * attention, axis=2, keepdims=True) / totals
    value_grad = jnp.einsum("hqk,qhd->kd", probs, scaled_grad, preferred_element_type=jnp.float32)
    prob_grad = jnp.einsum("qhd,kd->hqk", scaled_grad, values, preferred_element_type=jnp.float32)
    score_grad = low(exponent * (prob_grad - jnp.transpose(deltas, (1, 0, 2))))
    key_grad = (
        jnp.einsum("hqk,qhd->kd", score_grad, queries, preferred_element_type=jnp.float32) * inverse
    )
    query_grad = (
        jnp.einsum("hqk,kd->qhd", score_grad, keys, preferred_element_type=jnp.float32) * inverse
    )
    pair_parts = low(jnp.concatenate([key_grad, value_grad], 1)).reshape(-1, members, pair)
    (pair_grad,) = cam_collect(
        "pair_grads", [jnp.swapaxes(pair_parts, 0, 1).reshape(breadth, 2, -1, pair)]
    )
    low_grad = jnp.concatenate([low(query_grad.reshape(-1, width)), low(pair_grad)], 1)
    lead_part, tail_part = low_grad[:lead_total], low_grad[lead_total:]
    lead_back, tail_back = cam_collect(
        "backs",
        [cam_blocks(against(lead_part, lead_in)), cam_blocks(against(tail_part, tail_in))],
    )
    lead_back, lead_first = norm_backward(lead_back, lead_unit, lead_scale, prefix_prenorm)
    tail_back, tail_first = norm_backward(tail_back, tail_unit, tail_scale, action_prenorm)
    lead_input = low(lead_upstream + lead_back)
    tail_input = low(tail_upstream + tail_back)

    owned_lead, owned_tail = prefix_query.shape[0], action_query.shape[0]
    split_rows = lambda grad, rows: low(grad).reshape(depth, 2, members, rows, grad.shape[1])
    attention_parts = [
        split_rows(outer_sum(lead_normed, lead_part), owned_lead),
        split_rows(outer_sum(tail_normed, tail_part), owned_tail),
        split_rows(lead_mixing, owned_lead),
        split_rows(tail_mixing, owned_tail),
    ]
    scratch = []
    for part in attention_parts:
        block = part.shape[2:]
        scratch += [pltpu.VMEM((depth,) + block, jnp.bfloat16)] * 4

    def fold_routines(net, at, ins, outs, held):
        names = ("own", "core", "up", "down")
        buffers = [dict(zip(names, held[4 * i : 4 * i + 4])) for i in range(4)]
        return [fold(net, at, ins, outs, buffers)]

    folded = exchange(
        "fold",
        next(idents),
        sizes,
        ("z", "y", "cam"),
        [(part, False) for part in attention_parts],
        [(shape_of(part.shape[2:]), False) for part in attention_parts],
        scratch,
        fold_routines,
    )

    def split(projection, mixer):
        projection = jnp.swapaxes(projection, 0, 1).astype(jnp.float32)
        rows = projection.shape[0]
        query = projection[:, :, :width].reshape(rows, -1)
        pairs = projection[:, :, width:].reshape(rows, -1)
        mixer = jnp.swapaxes(mixer, 0, 1).reshape(rows, -1).astype(jnp.float32)
        return (query, pairs[:, :head_size], pairs[:, head_size:], mixer)

    lead_grads = split(folded[0], folded[2])
    tail_grads = split(folded[1], folded[3])

    gains = [lead_first, lead_middle, tail_first, tail_middle]
    total = lax.psum(jnp.concatenate(gains), ("rows", "cam"))
    place = lax.axis_index("rows") * members + member_place
    gain_grads = []
    offset = 0
    for gain in gains:
        share = gain.shape[0] // (row_count * members)
        gain_grads.append(lax.dynamic_slice_in_dim(total, offset + place * share, share))
        offset += gain.shape[0]

    return (
        (lead_result, tail_result, lead_input, tail_input)
        + lead_grads
        + tail_grads
        + tuple(gain_grads)
        + tuple(ff_grads)
    )


def solution(mesh):
    in_specs = (
        P(("rows", "cam"), None),
        P(("rows", "cam"), None),
        P(("rows", "cam"), None),
        P(("rows", "cam"), None),
        P("rows", None),
        P("rows", None),
        P(("rows", "cam"), None),
        P(("rows", "cam"), None),
        P(("rows", "cam"), None),
        P(("rows", "cam"), None),
        P(("rows", "cam"), None),
        P(("rows", "cam"), None),
        P(("rows", "cam"), None),
        P(("rows", "cam"), None),
        P(),
        P(),
        P(),
        P(),
        P("rows", "cam"),
        P("rows", "cam"),
        P("rows", "cam"),
        P("rows", "cam"),
        P("rows", "cam"),
        P("rows", "cam"),
    )
    out_specs = (
        P(("rows", "cam"), None),
        P(("rows", "cam"), None),
        P(("rows", "cam"), None),
        P(("rows", "cam"), None),
        P(("rows", "cam"), None),
        P(("rows", "cam"), None),
        P(("rows", "cam"), None),
        P(("rows", "cam"), None),
        P(("rows", "cam"), None),
        P(("rows", "cam"), None),
        P(("rows", "cam"), None),
        P(("rows", "cam"), None),
        P(("rows", "cam")),
        P(("rows", "cam")),
        P(("rows", "cam")),
        P(("rows", "cam")),
        P("rows", "cam"),
        P("rows", "cam"),
        P("rows", "cam"),
        P("rows", "cam"),
        P("rows", "cam"),
        P("rows", "cam"),
    )
    return jax.shard_map(body, mesh=mesh, in_specs=in_specs, out_specs=out_specs, check_vma=False)
```

```python
import functools

import jax
import jax.numpy as jnp
from jax import lax
from jax.experimental import pallas as pl
from jax.experimental.pallas import tpu as pltpu
from jax.sharding import PartitionSpec as P

ACTT = 32


epsilon = 1e-06
masked_score = -1e30


class Place:
    def __init__(self, depth, breadth):
        self.depth, self.breadth = depth, breadth
        row, member = lax.axis_index("rows"), lax.axis_index("cam")
        self.z, self.y = row // 2, row % 2
        self.x, self.k = member // 2, member % 2

    def device(self, z=None, y=None, x=None, k=None):
        z = self.z if z is None else z
        y = self.y if y is None else y
        x = self.x if x is None else x
        k = self.k if k is None else k
        return (z * 2 + y, x * 2 + k)

    def later_x(self, step):
        return lax.rem(self.x + step, self.breadth)

    def later_z(self, step):
        return lax.rem(self.z + step, self.depth)


def guarded(condition, action):
    if condition is None:
        action()
    else:
        pl.when(condition)(action)


class Transfer:
    def __init__(self, net, source, target, device, sends=None, gets=None):
        self.net, self.number = net, net.remote
        net.remote += 1
        self.source, self.target, self.device = source, target, device
        self.sends, self.gets = sends, gets
        net.pending.append(self)

    def describe(self):
        return pltpu.make_async_remote_copy(
            src_ref=self.source(),
            dst_ref=self.target(),
            send_sem=self.net.sent.at[self.number],
            recv_sem=self.net.received.at[self.number],
            device_id=self.device,
            device_id_type=pl.DeviceIdType.MESH,
        )

    def start(self):
        guarded(self.sends, lambda: self.describe().start())

    def got(self):
        guarded(self.gets, lambda: self.describe().wait_recv())

    def finish(self):
        guarded(self.sends, lambda: self.describe().wait_send())


class Local:
    def __init__(self, net, source, target):
        self.net, self.number = net, net.local
        net.local += 1
        self.source, self.target = source, target

    def describe(self):
        return pltpu.make_async_copy(
            self.source(), self.target(), self.net.moved.at[self.number]
        )

    def start(self):
        self.describe().start()
        return self

    def wait(self):
        self.describe().wait()


class Net:
    def __init__(self, sent, received, moved):
        self.sent, self.received, self.moved = sent, received, moved
        self.remote, self.local = 0, 0
        self.pending = []

    def settle(self):
        for transfer in self.pending:
            transfer.finish()


def greet(at, kinds):
    peers = []
    count = 0
    if "all" in kinds:
        for s, flip, step, turn in everyone(at):
            peers.append(
                (
                    None,
                    at.device(
                        at.later_z(s),
                        1 - at.y if flip else at.y,
                        at.later_x(step),
                        1 - at.k if turn else at.k,
                    ),
                )
            )
    if "z" in kinds and "deal" not in kinds:
        count = count + (at.z > 0).astype(jnp.int32) + (at.z < at.depth - 1).astype(jnp.int32)
        peers.append((at.z > 0, at.device(z=at.z - 1)))
        peers.append((at.z < at.depth - 1, at.device(z=at.z + 1)))
    if "deal" in kinds:
        peers += [(None, at.device(z=at.later_z(step))) for step in range(1, at.depth)]
    if "y" in kinds:
        peers.append((None, at.device(y=1 - at.y)))
    if "cam" in kinds:
        for step in range(at.breadth):
            for core in (at.k, 1 - at.k):
                if step > 0 or core is not at.k:
                    peers.append((None, at.device(x=at.later_x(step), k=core)))
    barrier = pltpu.get_barrier_semaphore()
    for condition, device in peers:
        guarded(
            condition,
            lambda device=device: pl.semaphore_signal(
                barrier, inc=1, device_id=device, device_id_type=pl.DeviceIdType.MESH
            ),
        )
    count = count + sum(1 for condition, _ in peers if condition is None)
    pl.semaphore_wait(barrier, count)


def run_all(routines):
    routines = list(routines)
    while routines:
        alive = []
        for routine in routines:
            try:
                next(routine)
                alive.append(routine)
            except StopIteration:
                pass
        routines = alive


def add_rows(target, first, second):
    count = target.shape[0]
    step = 16 if count % 16 == 0 else 8

    def one(index, carry):
        rows = pl.ds(pl.multiple_of(index * step, step), step)
        total = first[rows, :].astype(jnp.float32) + second[rows, :].astype(jnp.float32)
        target[rows, :] = total.astype(target.dtype)
        return carry

    lax.fori_loop(0, count // step, one, 0)


def widen_rows(target, source):
    count = target.shape[0]
    step = 16 if count % 16 == 0 else 8

    def one(index, carry):
        rows = pl.ds(pl.multiple_of(index * step, step), step)
        target[rows, :] = source[rows, :].astype(target.dtype)
        return carry

    lax.fori_loop(0, count // step, one, 0)


class Chain:
    def __init__(self, net, at, own, place):
        depth = at.depth
        self.up, self.down = {}, {}
        for step in range(1, depth):
            low, high = at.z - step + 1, at.z + step - 1
            self.up[step] = Transfer(
                net,
                own if step == 1 else (lambda low=low: place(low)),
                lambda low=low: place(low),
                at.device(z=at.z + 1),
                sends=(at.z + 1 < depth) & (low >= 0),
                gets=at.z - step >= 0,
            )
            self.down[step] = Transfer(
                net,
                own if step == 1 else (lambda high=high: place(high)),
                lambda high=high: place(high),
                at.device(z=at.z - 1),
                sends=(at.z > 0) & (high < depth),
                gets=at.z + step < depth,
            )


def tags_of(at, chained):
    tags = [("own", at.z, None)]
    if chained:
        for step in range(1, at.depth):
            tags.append((("up", step), at.z - step, at.z - step >= 0))
            tags.append((("down", step), at.z + step, at.z + step < at.depth))
    return tags


def spread(net, at, shards, outs, chained):
    if chained:
        place = lambda out, z, x, k: out.at[z, x, k]
    else:
        place = lambda out, z, x, k: out.at[x, k]
    tags = tags_of(at, chained)
    chains, across, partner, locals_ = [], {}, {}, []
    for i, (shard, out) in enumerate(zip(shards, outs)):
        own = lambda shard=shard: shard
        if chained:
            chains.append(
                Chain(net, at, own, lambda z, out=out: place(out, z, at.x, at.k))
            )
        locals_.append(Local(net, own, lambda out=out: place(out, at.z, at.x, at.k)))
        for name, z, condition in tags:
            held = own if name == "own" else (lambda out=out, z=z: place(out, z, at.x, at.k))
            target = lambda out=out, z=z: place(out, z, at.x, at.k)
            partner[i, name, 0] = Transfer(
                net, held, target, at.device(k=1 - at.k), condition, condition
            )
            for step in range(1, at.breadth):
                across[i, name, step] = Transfer(
                    net, held, target, at.device(x=at.later_x(step)), condition, condition
                )
                other = at.later_x(at.breadth - step)
                arrived = lambda out=out, z=z, other=other: place(out, z, other, at.k)
                partner[i, name, step] = Transfer(
                    net, arrived, arrived, at.device(k=1 - at.k), condition, condition
                )
    count = len(shards)

    def launch(name):
        for i in range(count):
            for step in range(1, at.breadth):
                across[i, name, step].start()
        for i in range(count):
            partner[i, name, 0].start()

    def forward(name):
        for i in range(count):
            for step in range(1, at.breadth):
                across[i, name, step].got()
                partner[i, name, step].start()

    for chain in chains:
        chain.up[1].start()
        chain.down[1].start()
    launch("own")
    for move in locals_:
        move.start()
    yield
    previous = ["own"]
    if chained:
        for step in range(1, at.depth):
            for chain in chains:
                chain.up[step].got()
                if step + 1 < at.depth:
                    chain.up[step + 1].start()
            launch(("up", step))
            yield
            for chain in chains:
                chain.down[step].got()
                if step + 1 < at.depth:
                    chain.down[step + 1].start()
            launch(("down", step))
            yield
            for name in previous:
                forward(name)
            previous = [("up", step), ("down", step)]
    for name in previous:
        yield
        forward(name)
    yield
    for transfer in partner.values():
        transfer.got()
    for move in locals_:
        move.wait()


def fan(net, at, packs, outs):
    members = 2 * at.breadth
    swap, chains, across, locals_ = {}, [], {}, []
    mine = at.x * 2 + at.k
    for i, (pack, out) in enumerate(zip(packs, outs)):
        slot = lambda out=out: out.at[at.z, at.y, mine]
        locals_.append(Local(net, lambda pack=pack: pack.at[mine], slot))
        for step in range(at.breadth):
            for flip in (0, 1):
                if step == 0 and flip == 0:
                    continue
                x = at.later_x(step)
                k = 1 - at.k if flip else at.k
                swap[i, step, flip] = Transfer(
                    net,
                    lambda pack=pack, x=x, k=k: pack.at[x * 2 + k],
                    slot,
                    at.device(x=x, k=k),
                )
        block = lambda z, out=out: out.at[z, at.y]
        chains.append(Chain(net, at, lambda block=block: block(at.z), block))
        for name, z, condition in tags_of(at, True):
            held = lambda block=block, z=z: block(z)
            across[i, name] = Transfer(
                net, held, held, at.device(y=1 - at.y), condition, condition
            )
    for transfer in swap.values():
        transfer.start()
    for move in locals_:
        move.start()
    yield
    for transfer in swap.values():
        transfer.got()
    for move in locals_:
        move.wait()
    count = len(packs)
    for chain in chains:
        chain.up[1].start()
        chain.down[1].start()
    for i in range(count):
        across[i, "own"].start()
    for step in range(1, at.depth):
        yield
        for chain in chains:
            chain.up[step].got()
            if step + 1 < at.depth:
                chain.up[step + 1].start()
        for i in range(count):
            across[i, ("up", step)].start()
        yield
        for chain in chains:
            chain.down[step].got()
            if step + 1 < at.depth:
                chain.down[step + 1].start()
        for i in range(count):
            across[i, ("down", step)].start()
    yield
    for transfer in across.values():
        transfer.got()


def add_all(target, sources):
    count = target.shape[0]
    step = 16 if count % 16 == 0 else 8

    def one(index, carry):
        rows = pl.ds(pl.multiple_of(index * step, step), step)
        total = sources[0][rows, :].astype(jnp.float32)
        for source in sources[1:]:
            total = total + source[rows, :].astype(jnp.float32)
        target[rows, :] = total.astype(target.dtype)
        return carry

    lax.fori_loop(0, count // step, one, 0)


def collect(net, at, parts, outs, buffers, chained):
    depth = at.depth if chained else 1
    part_of = (
        (lambda part, t, x, k: part.at[t, x, k]) if chained else (lambda part, t, x, k: part.at[x, k])
    )
    loads, partner, across, beyond = {}, {}, {}, {}
    for i, (part, buffer) in enumerate(zip(parts, buffers)):
        own, core, wide = buffer["own"], buffer["core"], buffer["wide"]
        for s in range(depth):
            t = at.later_z(s) if chained else 0
            for step in range(at.breadth):
                x = at.later_x(step)
                loads[i, s, step] = Local(
                    net,
                    lambda part=part, t=t, x=x: part_of(part, t, x, at.k),
                    lambda own=own, s=s, step=step: own.at[s, step],
                )
                partner[i, s, step] = Transfer(
                    net,
                    lambda part=part, t=t, x=x: part_of(part, t, x, 1 - at.k),
                    lambda core=core, s=s, step=step: core.at[s, step],
                    at.device(k=1 - at.k),
                )
                if step > 0:
                    across[i, s, step] = Transfer(
                        net,
                        lambda own=own, s=s, step=step: own.at[s, step],
                        lambda wide=wide, s=s, step=step: wide.at[step - 1, s],
                        at.device(x=x),
                    )
            if s > 0:
                beyond[i, s] = Transfer(
                    net,
                    lambda own=own, s=s: own.at[s, 0],
                    lambda buffer=buffer, s=s: buffer["far"].at[s - 1],
                    at.device(z=t),
                )
    steps = list(range(1, at.breadth)) + [0]
    spans = list(range(1, depth)) + [0]
    count = len(parts)
    for i in range(count):
        for s in spans:
            for step in steps:
                partner[i, s, step].start()
                loads[i, s, step].start()
    for i in range(count):
        own, core = buffers[i]["own"], buffers[i]["core"]
        for s in spans:
            yield
            for step in steps:
                loads[i, s, step].wait()
                partner[i, s, step].got()
                if step > 0:
                    add_rows(own.at[s, step], own.at[s, step], core.at[s, step])
                    across[i, s, step].start()
    for i in range(count):
        own, core, wide = buffers[i]["own"], buffers[i]["core"], buffers[i]["wide"]
        for s in spans:
            yield
            for step in steps[:-1]:
                across[i, s, step].got()
            terms = [own.at[s, 0], core.at[s, 0]] + [wide.at[step - 1, s] for step in steps[:-1]]
            if s > 0:
                add_all(own.at[s, 0], terms)
                beyond[i, s].start()
            else:
                add_all(outs[i], terms)
    for i in range(count):
        if depth > 1:
            yield
            for s in spans[:-1]:
                beyond[i, s].got()
            add_all(outs[i], [outs[i]] + [buffers[i]["far"].at[s - 1] for s in spans[:-1]])


def fold(net, at, parts, outs, buffers):
    mine = at.x * 2 + at.k
    members = 2 * at.breadth
    loads, across, beyond, swap, stores = {}, {}, {}, {}, []
    for i, (part, buffer) in enumerate(zip(parts, buffers)):
        own, core, far = buffer["own"], buffer["core"], buffer["far"]
        for s in range(at.depth):
            t = at.later_z(s)
            loads[i, s] = Local(
                net,
                lambda part=part, t=t: part.at[t, at.y],
                lambda own=own, s=s: own.at[s],
            )
            across[i, s] = Transfer(
                net,
                lambda part=part, t=t: part.at[t, 1 - at.y],
                lambda core=core, s=s: core.at[s],
                at.device(y=1 - at.y),
            )
            if s > 0:
                beyond[i, s] = Transfer(
                    net,
                    lambda own=own, s=s: own.at[s],
                    lambda far=far, s=s: far.at[s - 1],
                    at.device(z=t),
                )
        slot = lambda i=i: outs[i].at[mine]
        stores.append(Local(net, lambda own=own: own.at[0, mine], slot))
        for step in range(at.breadth):
            for flip in (0, 1):
                if step == 0 and flip == 0:
                    continue
                x = at.later_x(step)
                k = 1 - at.k if flip else at.k
                swap[i, step, flip] = Transfer(
                    net,
                    lambda own=own, x=x, k=k: own.at[0, x * 2 + k],
                    slot,
                    at.device(x=x, k=k),
                )
    count = len(parts)
    spans = list(range(1, at.depth)) + [0]
    for i in range(count):
        for s in spans:
            across[i, s].start()
            loads[i, s].start()
    for i in range(count):
        own, core = buffers[i]["own"], buffers[i]["core"]
        for s in spans:
            yield
            loads[i, s].wait()
            across[i, s].got()
            if s > 0:
                for member in range(members):
                    add_rows(own.at[s, member], own.at[s, member], core.at[s, member])
                beyond[i, s].start()
    for i in range(count):
        yield
        own, core, far = buffers[i]["own"], buffers[i]["core"], buffers[i]["far"]
        for s in spans[:-1]:
            beyond[i, s].got()
        for member in range(members):
            add_all(
                own.at[0, member],
                [own.at[0, member], core.at[0, member]]
                + [far.at[s - 1, member] for s in spans[:-1]],
            )
        stores[i].start()
        for (j, step, flip), transfer in swap.items():
            if j == i:
                transfer.start()
    yield
    for transfer in swap.values():
        transfer.got()
    for store in stores:
        store.wait()


def everyone(at):
    return [
        (s, flip, step, turn)
        for s in range(at.depth)
        for flip in (0, 1)
        for step in range(at.breadth)
        for turn in (0, 1)
        if (s, flip, step, turn) != (0, 0, 0, 0)
    ]


def hand_out(net, at, table, out):
    members = 2 * at.breadth
    number = lambda z, y, x, k: (z * 2 + y) * members + x * 2 + k
    mine = number(at.z, at.y, at.x, at.k)
    transfers = []
    for s, flip, step, turn in everyone(at):
        z, x = at.later_z(s), at.later_x(step)
        y = 1 - at.y if flip else at.y
        k = 1 - at.k if turn else at.k
        transfers.append(
            Transfer(
                net,
                lambda z=z, y=y, x=x, k=k: table.at[number(z, y, x, k)],
                lambda: out.at[mine],
                at.device(z, y, x, k),
            )
        )
    kept = Local(net, lambda: table.at[mine], lambda: out.at[mine])
    for transfer in transfers:
        transfer.start()
    kept.start()
    for _ in range(64):
        yield
    kept.wait()
    for transfer in transfers:
        transfer.got()


def exchange(label, ident, sizes, kinds, inputs, outputs, scratch, routines, micros=1):
    space = lambda inside: pltpu.VMEM if inside else pl.ANY

    def kernel(*refs):
        sources = refs[: len(inputs)]
        targets = refs[len(inputs) : len(inputs) + len(outputs)]
        held = refs[len(inputs) + len(outputs) : -3]
        at, net = Place(*sizes), Net(*refs[-3:])
        greet(at, kinds)
        run_all(routines(net, at, sources, targets, held))
        net.settle()

    slots = 40 * sizes[0]
    return pl.pallas_call(
        kernel,
        name=label,
        out_shape=[shape for shape, _ in outputs],
        in_specs=[pl.BlockSpec(memory_space=space(inside)) for _, inside in inputs],
        out_specs=[pl.BlockSpec(memory_space=space(inside)) for _, inside in outputs],
        scratch_shapes=list(scratch)
        + [pltpu.SemaphoreType.DMA((slots,))] * 2
        + [pltpu.SemaphoreType.DMA((slots,))],
        cost_estimate=pl.CostEstimate(
            flops=0, bytes_accessed=micros * 3000000, transcendentals=0
        ),
        compiler_params=pltpu.CompilerParams(
            collective_id=ident,
            has_side_effects=True,
            vmem_limit_bytes=(60 if sizes[0] <= 4 else 63) << 20,
        ),
    )(*[array for array, _ in inputs])


def permute(array, depth, step, flip):
    pairs = [
        (z * 2 + y, ((z + step) % depth) * 2 + (1 - y if flip else y))
        for z in range(depth)
        for y in range(2)
    ]
    return lax.ppermute(array, "rows", pairs)


def shuffle(label, sizes, arrays, stages, outs, moves, most):
    def kernel(*refs):
        ins, targets = refs[: len(arrays)], refs[len(arrays) : len(arrays) + len(outs)]
        held = refs[len(arrays) + len(outs) : -2]
        loaded, stored = refs[-2:]
        started, copies = [], []
        plan = moves(Place(*sizes), ins, held, targets)
        for loads, _ in plan:
            for source, target in loads:
                copy = pltpu.make_async_copy(source, target, loaded.at[len(started)])
                copy.start()
                started.append(copy)
        pending = iter(started)
        for loads, stores in plan:
            for _ in loads:
                next(pending).wait()
            for source, target in stores:
                copy = pltpu.make_async_copy(source, target, stored.at[len(copies)])
                copy.start()
                copies.append(copy)
        for copy in copies:
            copy.wait()

    size = sum(stage.size * stage.dtype.itemsize for stage in stages)
    slots = most * len(stages)
    return pl.pallas_call(
        kernel,
        name=label,
        out_shape=outs,
        in_specs=[pl.BlockSpec(memory_space=pl.ANY)] * len(arrays),
        out_specs=[pl.BlockSpec(memory_space=pl.ANY)] * len(outs),
        scratch_shapes=[pltpu.VMEM(stage.shape, stage.dtype) for stage in stages]
        + [pltpu.SemaphoreType.DMA((slots,)), pltpu.SemaphoreType.DMA((slots,))],
        cost_estimate=pl.CostEstimate(flops=0, bytes_accessed=2 * size, transcendentals=0),
        compiler_params=pltpu.CompilerParams(vmem_limit_bytes=60 << 20),
    )(*arrays)


def widen(label, sizes, blocks, outs, parts):
    shares = sorted({(outs[out].shape[-2], share) for _, _, out, share, _ in parts})

    def kernel(*refs):
        ins, targets = refs[: len(blocks)], refs[len(blocks) : len(blocks) + len(outs)]
        held = refs[len(blocks) + len(outs) : -len(shares) - 2]
        wide = refs[-len(shares) - 2 : -2]
        loaded, stored = refs[-2:]
        at = Place(*sizes)
        loads = [
            pltpu.make_async_copy(source, held[i], loaded.at[i]) for i, source in enumerate(ins)
        ]
        for load in loads:
            load.start()
        waited, turns, previous = set(), {}, {}
        for block, distance, out, share, pieces in parts:
            if block not in waited:
                loads[block].wait()
                waited.add(block)
            kind = shares.index((outs[out].shape[-2], share))
            turn = turns.get(kind, 0) % 2
            turns[kind] = turns.get(kind, 0) + 1
            if (kind, turn) in previous:
                previous[kind, turn].wait()
            buffer = wide[kind].at[turn]
            for row, column, count, place in pieces:
                widen_rows(
                    buffer.at[pl.ds(place, count), :],
                    held[block].at[pl.ds(row, count), pl.ds(column, share)],
                )
            z = at.later_z((sizes[0] - distance) % sizes[0])
            if len(outs[out].shape) == 3:
                target = targets[out].at[z]
            else:
                target = targets[out].at[:, pl.ds(pl.multiple_of(z * share, share), share)]
            copy = pltpu.make_async_copy(buffer, target, stored.at[2 * kind + turn])
            copy.start()
            previous[kind, turn] = copy
        for copy in previous.values():
            copy.wait()

    size = sum(block.size for block in blocks)
    return pl.pallas_call(
        kernel,
        name=label,
        out_shape=outs,
        in_specs=[pl.BlockSpec(memory_space=pl.ANY)] * len(blocks),
        out_specs=[pl.BlockSpec(memory_space=pl.ANY)] * len(outs),
        scratch_shapes=[pltpu.VMEM(block.shape, block.dtype) for block in blocks]
        + [pltpu.VMEM((2,) + share, jnp.float32) for share in shares]
        + [pltpu.SemaphoreType.DMA((len(blocks),)), pltpu.SemaphoreType.DMA((2 * len(shares),))],
        cost_estimate=pl.CostEstimate(flops=0, bytes_accessed=6 * size, transcendentals=0),
        compiler_params=pltpu.CompilerParams(vmem_limit_bytes=60 << 20),
    )(*blocks)


def shape_of(dims, kind=jnp.bfloat16):
    return jax.ShapeDtypeStruct(tuple(dims), kind)


def multiply(operand, matrix):
    return jnp.dot(operand, matrix, preferred_element_type=jnp.float32)


def against(operand, matrix):
    return lax.dot_general(
        operand, matrix, (((1,), (1,)), ((), ())), preferred_element_type=jnp.float32
    )


def outer_sum(operand, matrix):
    return lax.dot_general(
        operand, matrix, (((0,), (0,)), ((), ())), preferred_element_type=jnp.float32
    )


def norm_forward(values):
    scaling = lax.rsqrt(jnp.mean(values * values, axis=-1, keepdims=True) + epsilon)
    return (values * scaling, scaling)


def norm_backward(upstream, normed_unit, scaling, gain_vector):
    weighted = upstream * gain_vector
    average = jnp.mean(weighted * normed_unit, axis=-1, keepdims=True)
    return (scaling * (weighted - normed_unit * average), jnp.sum(upstream * normed_unit, axis=0))


def visible(query_ids, query_codes, key_ids, key_codes):
    matches = query_ids[:, None] == key_ids[None, :]
    return jnp.logical_and(matches, key_codes[None, :] <= query_codes[:, None])


def gated(gate_value, expand_value):
    return jax.nn.gelu(gate_value, approximate=True) * expand_value


def low(values):
    return values.astype(jnp.bfloat16)


def feed_forward(normed_rows, cotangent, gate_weight, expand_weight, down_weight):
    gate_value = multiply(normed_rows, gate_weight)
    expand_value = multiply(normed_rows, expand_weight)
    inside, pullback = jax.vjp(gated, gate_value, expand_value)
    inside_low = low(inside)
    part = low(against(inside_low, down_weight))
    inside_grad = multiply(cotangent, down_weight)
    gate_grad, expand_grad = pullback(inside_grad)
    gate_low, expand_low = low(gate_grad), low(expand_grad)
    normed_grad = low(against(gate_low, gate_weight) + against(expand_low, expand_weight))
    weight_grads = (
        outer_sum(normed_rows, gate_low),
        outer_sum(normed_rows, expand_low),
        outer_sum(cotangent, inside_low),
    )
    return (part, normed_grad, weight_grads)


def by_member(parts, members):
    rows = parts[0].shape[0]
    columns = jnp.concatenate([part.reshape(rows, members, -1) for part in parts], 2)
    return jnp.swapaxes(columns, 0, 1)


def body(
    prefix_tokens,
    action_tokens,
    prefix_cotangent,
    action_cotangent,
    prefix_segments,
    action_codes,
    prefix_query,
    prefix_key,
    prefix_value,
    prefix_mixer,
    action_query,
    action_key,
    action_value,
    action_mixer,
    prefix_prenorm,
    prefix_midnorm,
    action_prenorm,
    action_midnorm,
    prefix_gate,
    prefix_expand,
    prefix_down,
    action_gate,
    action_expand,
    action_down,
):
    members = lax.axis_size("cam")
    row_count = lax.axis_size("rows")
    depth, breadth = row_count // 2, members // 2
    sizes = (depth, breadth)
    head_size = prefix_key.shape[1]
    width = prefix_query.shape[1] // members
    heads = width // head_size
    pair = 2 * head_size // members
    inverse = float(head_size) ** (-0.5)
    lead_count, lead_width = prefix_tokens.shape
    tail_count, tail_width = action_tokens.shape
    idents = iter(range(100))

    def cam_spread(label, shards):
        return exchange(
            label,
            next(idents),
            sizes,
            ("cam",),
            [(shard, True) for shard in shards],
            [(shape_of((breadth, 2) + shard.shape), False) for shard in shards],
            [],
            lambda net, at, ins, outs, held: [spread(net, at, ins, outs, False)],
        )

    def cam_collect(label, parts):
        blocks = [part.shape[-2:] for part in parts]
        scratch = []
        for block in blocks:
            scratch += [
                pltpu.VMEM((1, breadth) + block, jnp.bfloat16),
                pltpu.VMEM((1, breadth) + block, jnp.bfloat16),
                pltpu.VMEM((breadth - 1, 1) + block, jnp.bfloat16),
            ]

        def routines(net, at, ins, outs, held):
            buffers = [
                dict(own=held[3 * i], core=held[3 * i + 1], wide=held[3 * i + 2])
                for i in range(len(parts))
            ]
            return [collect(net, at, ins, outs, buffers, False)]

        return exchange(
            label,
            next(idents),
            sizes,
            ("cam",),
            [(part, False) for part in parts],
            [(shape_of(block, jnp.float32), True) for block in blocks],
            scratch,
            routines,
        )

    lead_slice = prefix_gate.shape[1] // depth
    tail_slice = action_gate.shape[1] // depth
    lead_block, tail_block = prefix_gate.shape[0], action_gate.shape[0]
    floor = lax.axis_index("rows") // 2
    side = lax.rem(lax.axis_index("rows"), 2)
    ratio = lead_slice // tail_slice
    strip = tail_block // ratio
    packed = tail_slice % 128 == 0 and strip % 16 == 0
    high = 3 * lead_block + (3 * strip if packed else 0)
    cut_shapes = [shape_of((high, lead_slice))] * depth
    if not packed:
        cut_shapes += [shape_of((3, tail_block, tail_slice))] * depth

    def strips(i, start):
        return [(start + i * strip, j * tail_slice, j * strip) for j in range(ratio)]

    def cut_moves(at, ins, held, outs):
        lists = []
        for step in range(depth):
            z = at.later_z(step)
            columns = pl.ds(pl.multiple_of(z * lead_slice, lead_slice), lead_slice)
            loads = [
                (ins[i].at[:, columns], held[step].at[pl.ds(i * lead_block, lead_block), :])
                for i in range(3)
            ]
            if packed:
                narrow = pl.ds(pl.multiple_of(z * tail_slice, tail_slice), tail_slice)
                loads += [
                    (
                        ins[3 + i].at[pl.ds(place, strip), narrow],
                        held[step].at[pl.ds(row, strip), pl.ds(column, tail_slice)],
                    )
                    for i in range(3)
                    for row, column, place in strips(i, 3 * lead_block)
                ]
            lists.append((loads, [(held[step], outs[step])]))
        return lists

    lead_weights = [prefix_gate, prefix_expand, prefix_down]
    tail_weights = [action_gate, action_expand, action_down]
    cuts = list(
        shuffle(
            "cut",
            sizes,
            lead_weights + (tail_weights if packed else []),
            cut_shapes[:depth],
            cut_shapes[:depth],
            cut_moves,
            3 + 3 * ratio if packed else 3,
        )
    )
    if not packed:
        cuts += [
            jnp.stack(
                [
                    lax.dynamic_slice_in_dim(
                        weight, lax.rem(floor + step, depth) * tail_slice, tail_slice, 1
                    )
                    for weight in tail_weights
                ]
            )
            for step in range(depth)
        ]
    groups = len(cuts) // depth
    dealt, mirrored = {}, {}

    def mirror(step):
        for group in range(groups):
            mirrored[group, step] = permute(dealt[group, step], depth, 0, True)

    def tied(arrays, steps):
        keys = [(group, step) for group in range(groups) for step in steps]
        arrays, blocks = lax.optimization_barrier((arrays, [dealt[key] for key in keys]))
        dealt.update(zip(keys, blocks))
        return arrays

    lead_float = prefix_tokens.astype(jnp.float32)
    tail_float = action_tokens.astype(jnp.float32)
    lead_unit, lead_scale = norm_forward(lead_float)
    tail_unit, tail_scale = norm_forward(tail_float)
    lead_low = low(lead_unit * prefix_prenorm)
    tail_low = low(tail_unit * action_prenorm)
    lead_pack = by_member([prefix_query, jnp.concatenate([prefix_key, prefix_value], 1)], members)
    tail_pack = by_member([action_query, jnp.concatenate([action_key, action_value], 1)], members)
    lead_mixers = by_member([prefix_mixer], members)
    tail_mixers = by_member([action_mixer], members)
    packs = [lead_pack, tail_pack, lead_mixers, tail_mixers]
    shards = [prefix_cotangent, action_cotangent]
    first = [lead_low, tail_low] + packs + shards
    fanned = lambda pack: (shape_of((depth, 2) + pack.shape), False)
    gathered = lambda shard: (shape_of((depth, breadth, 2) + shard.shape), False)
    started = exchange(
        "first",
        next(idents),
        sizes,
        ("z", "y", "cam"),
        [(array, True) for array in first],
        [(shape_of((breadth, 2) + array.shape), False) for array in first[:2]]
        + [fanned(pack) for pack in packs]
        + [gathered(shard) for shard in shards],
        [],
        lambda net, at, ins, outs, held: [
            fan(net, at, ins[2:4], outs[2:4]),
            spread(net, at, ins[:2], outs[:2], False),
            fan(net, at, ins[4:6], outs[4:6]),
            spread(net, at, ins[6:], outs[6:], True),
        ],
    )
    started, cuts = lax.optimization_barrier((started, cuts))
    for group in range(groups):
        for step in range(depth):
            cut = cuts[group * depth + step]
            dealt[group, step] = permute(cut, depth, step, False) if step > 0 else cut
    lead_normed, tail_normed, lead_in, tail_in, lead_mix, tail_mix, *uppers = started
    lead_upper, tail_upper = [array.reshape(-1, array.shape[-1]) for array in uppers]
    lead_mix, tail_mix = lead_mix.reshape(lead_width, width), tail_mix.reshape(tail_width, width)
    mirror(0)
    lead_normed = lead_normed.reshape(-1, lead_width)
    tail_normed = tail_normed.reshape(-1, tail_width)
    lead_in = lead_in.reshape(lead_width, -1)
    tail_in = tail_in.reshape(tail_width, -1)
    lead_total, tail_total = lead_normed.shape[0], tail_normed.shape[0]

    projected = low(
        jnp.concatenate([multiply(lead_normed, lead_in), multiply(tail_normed, tail_in)], 0)
    )
    (pairs,) = cam_spread("pairs", [projected[:, width:]])
    pairs = jnp.swapaxes(pairs.reshape(members, -1, pair), 0, 1).reshape(-1, 2 * head_size)

    segment_row = prefix_segments[0]
    code_row = action_codes[0]
    token_ids = jnp.concatenate(
        [segment_row, jnp.arange(code_row.shape[0], dtype=jnp.int32) // ACTT]
    )
    token_codes = jnp.concatenate([jnp.zeros(segment_row.shape, jnp.int32), code_row])
    queries = projected[:, :width].reshape(-1, heads, head_size)
    keys, values = pairs[:, :head_size], pairs[:, head_size:]
    allowed = visible(token_ids, token_codes, token_ids, token_codes)
    logits = jnp.einsum("qhd,kd->hqk", queries, keys, preferred_element_type=jnp.float32) * inverse
    scores = jnp.where(allowed[None], logits, masked_score)
    exponent = jnp.exp(scores - jnp.max(scores, axis=2, keepdims=True))
    totals = jnp.transpose(jnp.sum(exponent, axis=2))[:, :, None]
    probs = low(exponent)
    attention = (
        jnp.einsum("hqk,kd->qhd", probs, values, preferred_element_type=jnp.float32) / totals
    )
    mixed = low(attention.reshape(-1, width))
    cam_blocks = lambda rows: low(rows).reshape(breadth, 2, -1, rows.shape[1])
    lead_sum, tail_sum = cam_collect(
        "mixing",
        [
            cam_blocks(against(mixed[:lead_total], lead_mix)),
            cam_blocks(against(mixed[lead_total:], tail_mix)),
        ],
    )
    lead_sum, tail_sum = tied([lead_sum, tail_sum], [1])
    mirror(1)
    lead_hidden = lead_float + lead_sum
    tail_hidden = tail_float + tail_sum
    lead_center, lead_factor = norm_forward(lead_hidden)
    tail_center, tail_factor = norm_forward(tail_hidden)
    lead_second = low(lead_center * prefix_midnorm)
    tail_second = low(tail_center * action_midnorm)

    for step in range(2, depth):
        lead_second, tail_second = tied([lead_second, tail_second], [step])
        mirror(step)

    def place_moves(at, ins, held, outs):
        lists = []
        for number, (group, step, flip) in enumerate(marks):
            z = at.later_z((depth - step) % depth)
            y = 1 - at.y if flip else at.y
            block = held[number]
            stores = []
            if group == 0:
                stores += [
                    (block.at[pl.ds(i * lead_block, lead_block), :], outs[i].at[z, y])
                    for i in range(3)
                ]
                if packed:
                    stores += [
                        (
                            block.at[pl.ds(row, strip), pl.ds(column, tail_slice)],
                            outs[3 + i].at[z, y, pl.ds(place, strip), :],
                        )
                        for i in range(3)
                        for row, column, place in strips(i, 3 * lead_block)
                    ]
            else:
                stores += [(block.at[i], outs[3 + i].at[z, y]) for i in range(3)]
            lists.append(([(ins[number], block)], stores))
        return lists

    marks = [
        (group, step, flip) for group in range(groups) for step in range(depth) for flip in (0, 1)
    ]
    blocks = [
        (mirrored if flip else dealt)[group, step] for group, step, flip in marks
    ]
    lead_gate, lead_expand, lead_down, tail_gate, tail_expand, tail_down = [
        weight.reshape(-1, weight.shape[-1])
        for weight in shuffle(
            "place",
            sizes,
            blocks,
            blocks,
            [shape_of((depth, 2, lead_block, lead_slice))] * 3
            + [shape_of((depth, 2, tail_block, tail_slice))] * 3,
            place_moves,
            3 + 3 * ratio if packed else 3,
        )
    ]

    def send_across(packs):
        sent = []
        for pack in packs:
            pack = [low(grad).reshape(depth, 2, -1, grad.shape[1]) for grad in pack]
            if len(pack) > 1 and packed:
                pack[1:] = [
                    jnp.concatenate(jnp.split(grad, ratio, axis=2), axis=3) for grad in pack[1:]
                ]
            tables = [pack] if packed or len(pack) == 1 else [pack[:1], pack[1:]]
            for table in tables:
                take = lambda y: jnp.concatenate(
                    [lax.dynamic_index_in_dim(part, y, 1, False) for part in table], 1
                )
                own, other = take(side), permute(take(1 - side), depth, 0, True)
                sent.append((own, other))
        return sent

    def pass_on(pairs):
        summed = jnp.concatenate(
            [low(own.astype(jnp.float32) + other.astype(jnp.float32)) for own, other in pairs], 1
        )
        blocks = []
        for step in range(depth):
            block = lax.dynamic_index_in_dim(summed, lax.rem(floor + step, depth), 0, False)
            blocks.append(permute(block, depth, step, False) if step > 0 else block)
        return blocks

    shards = [lead_second, tail_second]
    lead_all, tail_all = [
        array.reshape(-1, array.shape[-1])
        for array in exchange(
            "gather",
            next(idents),
            sizes,
            ("z", "cam"),
            [(shard, True) for shard in shards],
            [gathered(shard) for shard in shards],
            [],
            lambda net, at, ins, outs, held: [spread(net, at, ins, outs, True)],
        )
    ]
    tail_out, tail_back, tail_ffgrads = feed_forward(
        tail_all, tail_upper, tail_gate, tail_expand, tail_down
    )
    gate_value = multiply(lead_all, lead_gate)
    expand_value = multiply(lead_all, lead_expand)
    inside, pullback = jax.vjp(gated, gate_value, expand_value)
    inside_low = low(inside)
    down_grad = low(outer_sum(lead_upper, inside_low))
    down_grad, lead_upper = lax.optimization_barrier((down_grad, lead_upper))
    returns = send_across([[down_grad] + list(tail_ffgrads)])
    inside_grad = multiply(lead_upper, lead_down)
    gate_grad, expand_grad = pullback(inside_grad)
    gate_low, expand_low = low(gate_grad), low(expand_grad)
    returns += send_across(
        [[outer_sum(lead_all, gate_low)], [outer_sum(lead_all, expand_low)]]
    )
    lead_out = low(against(inside_low, lead_down))
    lead_back = low(against(gate_low, lead_gate) + against(expand_low, lead_expand))
    (lead_out, lead_back), returns[:-2] = lax.optimization_barrier(
        ((lead_out, lead_back), returns[:-2])
    )
    blocks_back = [pass_on(returns[:1])]
    if not packed:
        blocks_back.append(pass_on(returns[1:2]))

    def token_blocks(rows):
        return rows.reshape(depth, breadth, 2, -1, rows.shape[1])

    def sum_scratch(parts):
        scratch = []
        for part in parts:
            block = part.shape[3:]
            scratch += [
                pltpu.VMEM((depth, breadth) + block, jnp.bfloat16),
                pltpu.VMEM((depth, breadth) + block, jnp.bfloat16),
                pltpu.VMEM((breadth - 1, depth) + block, jnp.bfloat16),
                pltpu.VMEM((depth - 1,) + block, jnp.bfloat16),
            ]
        return scratch

    def sum_routine(net, at, ins, outs, held):
        names = ("own", "core", "wide", "far")
        buffers = [dict(zip(names, held[4 * i : 4 * i + 4])) for i in range(len(ins))]
        return collect(net, at, ins, outs, buffers, True)

    backs = [token_blocks(lead_back), token_blocks(tail_back)]
    lead_summed, tail_summed = exchange(
        "collect",
        next(idents),
        sizes,
        ("deal", "cam"),
        [(part, False) for part in backs],
        [(shape_of(part.shape[3:], jnp.float32), True) for part in backs],
        sum_scratch(backs),
        lambda net, at, ins, outs, held: [sum_routine(net, at, ins, outs, held)],
    )

    (lead_summed, tail_summed), rest, blocks_back = lax.optimization_barrier(
        ((lead_summed, tail_summed), returns[-2:], blocks_back)
    )
    blocks_back.insert(1, pass_on(rest))
    lead_residual, lead_middle = norm_backward(
        lead_summed, lead_center, lead_factor, prefix_midnorm
    )
    tail_residual, tail_middle = norm_backward(
        tail_summed, tail_center, tail_factor, action_midnorm
    )
    lead_upstream = prefix_cotangent.astype(jnp.float32) + lead_residual
    tail_upstream = action_cotangent.astype(jnp.float32) + tail_residual
    lead_sent, tail_sent = cam_spread("sent", [low(lead_upstream), low(tail_upstream)])
    lead_sent = lead_sent.reshape(-1, lead_width)
    tail_sent = tail_sent.reshape(-1, tail_width)
    lead_mixing = outer_sum(lead_sent, mixed[:lead_total])
    tail_mixing = outer_sum(tail_sent, mixed[lead_total:])
    attention_grad = jnp.concatenate(
        [multiply(lead_sent, lead_mix), multiply(tail_sent, tail_mix)], 0
    ).reshape(-1, heads, head_size)
    scaled_grad = low(attention_grad / totals)
    deltas = jnp.sum(attention_grad * attention, axis=2, keepdims=True) / totals
    value_grad = jnp.einsum("hqk,qhd->kd", probs, scaled_grad, preferred_element_type=jnp.float32)
    prob_grad = jnp.einsum("qhd,kd->hqk", scaled_grad, values, preferred_element_type=jnp.float32)
    score_grad = low(exponent * (prob_grad - jnp.transpose(deltas, (1, 0, 2))))
    key_grad = (
        jnp.einsum("hqk,qhd->kd", score_grad, queries, preferred_element_type=jnp.float32) * inverse
    )
    query_grad = (
        jnp.einsum("hqk,kd->qhd", score_grad, keys, preferred_element_type=jnp.float32) * inverse
    )
    pair_parts = low(jnp.concatenate([key_grad, value_grad], 1)).reshape(-1, members, pair)
    (pair_grad,) = cam_collect(
        "pair_grads", [jnp.swapaxes(pair_parts, 0, 1).reshape(breadth, 2, -1, pair)]
    )
    low_grad = jnp.concatenate([low(query_grad.reshape(-1, width)), low(pair_grad)], 1)
    lead_part, tail_part = low_grad[:lead_total], low_grad[lead_total:]
    lead_back, tail_back = cam_collect(
        "backs",
        [cam_blocks(against(lead_part, lead_in)), cam_blocks(against(tail_part, tail_in))],
    )
    (lead_back, tail_back, low_grad, lead_mixing, tail_mixing), blocks_back = (
        lax.optimization_barrier(
            ((lead_back, tail_back, low_grad, lead_mixing, tail_mixing), blocks_back)
        )
    )
    lead_part, tail_part = low_grad[:lead_total], low_grad[lead_total:]
    lead_back, lead_first = norm_backward(lead_back, lead_unit, lead_scale, prefix_prenorm)
    tail_back, tail_first = norm_backward(tail_back, tail_unit, tail_scale, action_prenorm)
    lead_input = low(lead_upstream + lead_back)
    tail_input = low(tail_upstream + tail_back)

    owned_lead, owned_tail = prefix_query.shape[0], action_query.shape[0]
    split_rows = lambda grad, rows: low(grad).reshape(depth, 2, members, rows, grad.shape[1])
    attention_parts = [
        split_rows(outer_sum(lead_normed, lead_part), owned_lead),
        split_rows(outer_sum(tail_normed, tail_part), owned_tail),
        split_rows(lead_mixing, owned_lead),
        split_rows(tail_mixing, owned_tail),
    ]
    scratch = []
    for part in attention_parts:
        block = part.shape[2:]
        scratch += [pltpu.VMEM((depth,) + block, jnp.bfloat16)] * 2
        scratch += [pltpu.VMEM((depth - 1,) + block, jnp.bfloat16)]
    gains = [lead_first, lead_middle, tail_first, tail_middle]
    device_count = row_count * members
    table = jnp.concatenate([gain.reshape(device_count, -1) for gain in gains], 1)
    owned = table.shape[1]
    span = -(-owned // 128) * 128
    table = jnp.pad(table, ((0, 0), (0, span - owned)))[:, None, :]
    branches = [token_blocks(lead_out), token_blocks(tail_out)]

    def fold_routines(net, at, ins, outs, held):
        names = ("own", "core", "far")
        buffers = [dict(zip(names, held[3 * i : 3 * i + 3])) for i in range(4)]
        return [
            hand_out(net, at, ins[4], outs[4]),
            fold(net, at, ins[:4], outs[:4], buffers),
            sum_routine(net, at, ins[5:], outs[5:], held[12:]),
        ]

    folded = exchange(
        "fold",
        next(idents),
        sizes,
        ("all",),
        [(part, False) for part in attention_parts]
        + [(table, True)]
        + [(branch, False) for branch in branches],
        [(shape_of(part.shape[2:]), False) for part in attention_parts]
        + [(shape_of(table.shape, jnp.float32), True)]
        + [(shape_of(branch.shape[3:], jnp.float32), True) for branch in branches],
        scratch + sum_scratch(branches),
        fold_routines,
    )
    lead_result = low(lead_hidden + folded[5])
    tail_result = low(tail_hidden + folded[6])

    def split(projection, mixer):
        projection = jnp.swapaxes(projection, 0, 1).astype(jnp.float32)
        rows = projection.shape[0]
        query = projection[:, :, :width].reshape(rows, -1)
        pairs = projection[:, :, width:].reshape(rows, -1)
        mixer = jnp.swapaxes(mixer, 0, 1).reshape(rows, -1).astype(jnp.float32)
        return (query, pairs[:, :head_size], pairs[:, head_size:], mixer)

    lead_grads = split(folded[0], folded[2])
    tail_grads = split(folded[1], folded[3])

    whole_block = [(0, 0, lead_block, 0)]
    parts = []
    for step in range(depth):
        parts.append((step, step, 2, lead_slice, whole_block))
        for i in range(3):
            if packed:
                pieces = [(row, column, strip, place) for row, column, place in strips(i, lead_block)]
                parts.append((step, step, 3 + i, tail_slice, pieces))
            else:
                pieces = [(i * tail_block, 0, tail_block, 0)]
                parts.append((2 * depth + step, step, 3 + i, tail_slice, pieces))
    for step in range(depth):
        for i in range(2):
            pieces = [(i * lead_block, 0, lead_block, 0)]
            parts.append((depth + step, step, i, lead_slice, pieces))
    ff_grads = widen(
        "returns",
        sizes,
        sum(blocks_back, []),
        [shape_of(weight.shape, jnp.float32) for weight in lead_weights]
        + [
            shape_of(
                weight.shape if packed else (depth, tail_block, tail_slice), jnp.float32
            )
            for weight in tail_weights
        ],
        parts,
    )
    if not packed:
        ff_grads = list(ff_grads[:3]) + [
            jnp.swapaxes(grad, 0, 1).reshape(tail_block, -1) for grad in ff_grads[3:]
        ]

    total = jnp.sum(folded[4][:, 0], axis=0)
    gain_grads = []
    offset = 0
    for gain in gains:
        share = gain.shape[0] // device_count
        gain_grads.append(total[offset : offset + share])
        offset += share

    return (
        (lead_result, tail_result, lead_input, tail_input)
        + lead_grads
        + tail_grads
        + tuple(gain_grads)
        + tuple(ff_grads)
    )


def solution(mesh):
    in_specs = (
        P(("rows", "cam"), None),
        P(("rows", "cam"), None),
        P(("rows", "cam"), None),
        P(("rows", "cam"), None),
        P("rows", None),
        P("rows", None),
        P(("rows", "cam"), None),
        P(("rows", "cam"), None),
        P(("rows", "cam"), None),
        P(("rows", "cam"), None),
        P(("rows", "cam"), None),
        P(("rows", "cam"), None),
        P(("rows", "cam"), None),
        P(("rows", "cam"), None),
        P(),
        P(),
        P(),
        P(),
        P("rows", "cam"),
        P("rows", "cam"),
        P("rows", "cam"),
        P("rows", "cam"),
        P("rows", "cam"),
        P("rows", "cam"),
    )
    out_specs = (
        P(("rows", "cam"), None),
        P(("rows", "cam"), None),
        P(("rows", "cam"), None),
        P(("rows", "cam"), None),
        P(("rows", "cam"), None),
        P(("rows", "cam"), None),
        P(("rows", "cam"), None),
        P(("rows", "cam"), None),
        P(("rows", "cam"), None),
        P(("rows", "cam"), None),
        P(("rows", "cam"), None),
        P(("rows", "cam"), None),
        P(("rows", "cam")),
        P(("rows", "cam")),
        P(("rows", "cam")),
        P(("rows", "cam")),
        P("rows", "cam"),
        P("rows", "cam"),
        P("rows", "cam"),
        P("rows", "cam"),
        P("rows", "cam"),
        P("rows", "cam"),
    )
    return jax.shard_map(body, mesh=mesh, in_specs=in_specs, out_specs=out_specs, check_vma=False)
```

```python
import math

import jax
import jax.numpy as jnp
from jax import lax
from jax.experimental import pallas as pl
from jax.experimental.pallas import tpu as pltpu
from jax.sharding import PartitionSpec as P

ACTT = 32


epsilon = 1e-06
masked_score = -1e30


class Place:
    def __init__(self, depth, breadth):
        self.depth, self.breadth = depth, breadth
        row, member = lax.axis_index("rows"), lax.axis_index("cam")
        self.z, self.y = row // 2, row % 2
        self.x, self.k = member // 2, member % 2

    def device(self, z=None, y=None, x=None, k=None):
        z = self.z if z is None else z
        y = self.y if y is None else y
        x = self.x if x is None else x
        k = self.k if k is None else k
        return (z * 2 + y, x * 2 + k)

    def later_x(self, step):
        return lax.rem(self.x + step, self.breadth)

    def later_z(self, step):
        return lax.rem(self.z + step, self.depth)

    def flip_z(self, bits):
        z, bit = self.z, 1
        while bit < self.depth:
            if bits & bit:
                z = z + bit - 2 * bit * lax.rem(self.z // bit, 2)
            bit *= 2
        return z


def guarded(condition, action):
    if condition is None:
        action()
    else:
        pl.when(condition)(action)


class Transfer:
    def __init__(self, net, source, target, device, sends=None, gets=None):
        self.net, self.number = net, net.remote
        net.remote += 1
        self.source, self.target, self.device = source, target, device
        self.sends, self.gets = sends, gets
        net.pending.append(self)

    def describe(self):
        return pltpu.make_async_remote_copy(
            src_ref=self.source(),
            dst_ref=self.target(),
            send_sem=self.net.sent.at[self.number],
            recv_sem=self.net.received.at[self.number],
            device_id=self.device,
            device_id_type=pl.DeviceIdType.MESH,
        )

    def start(self):
        guarded(self.sends, lambda: self.describe().start())

    def got(self):
        guarded(self.gets, lambda: self.describe().wait_recv())

    def finish(self):
        guarded(self.sends, lambda: self.describe().wait_send())


class Local:
    def __init__(self, net, source, target):
        self.net, self.number = net, net.local
        net.local += 1
        self.source, self.target = source, target

    def describe(self):
        return pltpu.make_async_copy(
            self.source(), self.target(), self.net.moved.at[self.number]
        )

    def start(self):
        self.describe().start()
        return self

    def wait(self):
        self.describe().wait()


class Net:
    def __init__(self, sent, received, moved):
        self.sent, self.received, self.moved = sent, received, moved
        self.remote, self.local = 0, 0
        self.pending = []

    def settle(self):
        for transfer in self.pending:
            transfer.finish()


def greet(at, kinds):
    peers = []
    count = 0
    if "all" in kinds:
        for s, flip, step, turn in everyone(at):
            peers.append(
                (
                    None,
                    at.device(
                        at.later_z(s),
                        1 - at.y if flip else at.y,
                        at.later_x(step),
                        1 - at.k if turn else at.k,
                    ),
                )
            )
    if "z" in kinds and "deal" not in kinds:
        count = count + (at.z > 0).astype(jnp.int32) + (at.z < at.depth - 1).astype(jnp.int32)
        peers.append((at.z > 0, at.device(z=at.z - 1)))
        peers.append((at.z < at.depth - 1, at.device(z=at.z + 1)))
    if "deal" in kinds:
        peers += [(None, at.device(z=at.later_z(step))) for step in range(1, at.depth)]
    if "y" in kinds:
        peers.append((None, at.device(y=1 - at.y)))
    if "cam" in kinds:
        for step in range(at.breadth):
            for core in (at.k, 1 - at.k):
                if step > 0 or core is not at.k:
                    peers.append((None, at.device(x=at.later_x(step), k=core)))
    barrier = pltpu.get_barrier_semaphore()
    for condition, device in peers:
        guarded(
            condition,
            lambda device=device: pl.semaphore_signal(
                barrier, inc=1, device_id=device, device_id_type=pl.DeviceIdType.MESH
            ),
        )
    count = count + sum(1 for condition, _ in peers if condition is None)
    pl.semaphore_wait(barrier, count)


def run_all(routines):
    routines = list(routines)
    while routines:
        alive = []
        for routine in routines:
            try:
                next(routine)
                alive.append(routine)
            except StopIteration:
                pass
        routines = alive


def add_rows(target, first, second):
    count = target.shape[0]
    step = 16 if count % 16 == 0 else 8

    def one(index, carry):
        rows = pl.ds(pl.multiple_of(index * step, step), step)
        total = first[rows, :].astype(jnp.float32) + second[rows, :].astype(jnp.float32)
        target[rows, :] = total.astype(target.dtype)
        return carry

    lax.fori_loop(0, count // step, one, 0)


def widen_rows(target, source):
    count = target.shape[0]
    step = 16 if count % 16 == 0 else 8

    def one(index, carry):
        rows = pl.ds(pl.multiple_of(index * step, step), step)
        target[rows, :] = source[rows, :].astype(target.dtype)
        return carry

    lax.fori_loop(0, count // step, one, 0)


class Chain:
    def __init__(self, net, at, own, place):
        depth = at.depth
        self.up, self.down = {}, {}
        for step in range(1, depth):
            low, high = at.z - step + 1, at.z + step - 1
            self.up[step] = Transfer(
                net,
                own if step == 1 else (lambda low=low: place(low)),
                lambda low=low: place(low),
                at.device(z=at.z + 1),
                sends=(at.z + 1 < depth) & (low >= 0),
                gets=at.z - step >= 0,
            )
            self.down[step] = Transfer(
                net,
                own if step == 1 else (lambda high=high: place(high)),
                lambda high=high: place(high),
                at.device(z=at.z - 1),
                sends=(at.z > 0) & (high < depth),
                gets=at.z + step < depth,
            )


def tags_of(at, chained):
    tags = [("own", at.z, None)]
    if chained:
        for step in range(1, at.depth):
            tags.append((("up", step), at.z - step, at.z - step >= 0))
            tags.append((("down", step), at.z + step, at.z + step < at.depth))
    return tags


def spread(net, at, shards, outs, chained):
    if chained:
        place = lambda out, z, x, k: out.at[z, x, k]
    else:
        place = lambda out, z, x, k: out.at[x, k]
    tags = tags_of(at, chained)
    chains, across, partner, locals_ = [], {}, {}, []
    for i, (shard, out) in enumerate(zip(shards, outs)):
        own = lambda shard=shard: shard
        if chained:
            chains.append(
                Chain(net, at, own, lambda z, out=out: place(out, z, at.x, at.k))
            )
        locals_.append(Local(net, own, lambda out=out: place(out, at.z, at.x, at.k)))
        for name, z, condition in tags:
            held = own if name == "own" else (lambda out=out, z=z: place(out, z, at.x, at.k))
            target = lambda out=out, z=z: place(out, z, at.x, at.k)
            partner[i, name, 0] = Transfer(
                net, held, target, at.device(k=1 - at.k), condition, condition
            )
            for step in range(1, at.breadth):
                across[i, name, step] = Transfer(
                    net, held, target, at.device(x=at.later_x(step)), condition, condition
                )
                other = at.later_x(at.breadth - step)
                arrived = lambda out=out, z=z, other=other: place(out, z, other, at.k)
                partner[i, name, step] = Transfer(
                    net, arrived, arrived, at.device(k=1 - at.k), condition, condition
                )
    count = len(shards)

    def launch(name):
        for i in range(count):
            for step in range(1, at.breadth):
                across[i, name, step].start()
        for i in range(count):
            partner[i, name, 0].start()

    def forward(name):
        for i in range(count):
            for step in range(1, at.breadth):
                across[i, name, step].got()
                partner[i, name, step].start()

    for chain in chains:
        chain.up[1].start()
        chain.down[1].start()
    launch("own")
    for move in locals_:
        move.start()
    yield
    previous = ["own"]
    if chained:
        for step in range(1, at.depth):
            for chain in chains:
                chain.up[step].got()
                if step + 1 < at.depth:
                    chain.up[step + 1].start()
            launch(("up", step))
            yield
            for chain in chains:
                chain.down[step].got()
                if step + 1 < at.depth:
                    chain.down[step + 1].start()
            launch(("down", step))
            yield
            for name in previous:
                forward(name)
            previous = [("up", step), ("down", step)]
    for name in previous:
        yield
        forward(name)
    yield
    for transfer in partner.values():
        transfer.got()
    for move in locals_:
        move.wait()


def fan(net, at, packs, outs):
    members = 2 * at.breadth
    swap, chains, across, locals_ = {}, [], {}, []
    mine = at.x * 2 + at.k
    for i, (pack, out) in enumerate(zip(packs, outs)):
        slot = lambda out=out: out.at[at.z, at.y, mine]
        locals_.append(Local(net, lambda pack=pack: pack.at[mine], slot))
        for step in range(at.breadth):
            for flip in (0, 1):
                if step == 0 and flip == 0:
                    continue
                x = at.later_x(step)
                k = 1 - at.k if flip else at.k
                swap[i, step, flip] = Transfer(
                    net,
                    lambda pack=pack, x=x, k=k: pack.at[x * 2 + k],
                    slot,
                    at.device(x=x, k=k),
                )
        block = lambda z, out=out: out.at[z, at.y]
        chains.append(Chain(net, at, lambda block=block: block(at.z), block))
        for name, z, condition in tags_of(at, True):
            held = lambda block=block, z=z: block(z)
            across[i, name] = Transfer(
                net, held, held, at.device(y=1 - at.y), condition, condition
            )
    for transfer in swap.values():
        transfer.start()
    for move in locals_:
        move.start()
    yield
    for transfer in swap.values():
        transfer.got()
    for move in locals_:
        move.wait()
    count = len(packs)
    for chain in chains:
        chain.up[1].start()
        chain.down[1].start()
    for i in range(count):
        across[i, "own"].start()
    for step in range(1, at.depth):
        yield
        for chain in chains:
            chain.up[step].got()
            if step + 1 < at.depth:
                chain.up[step + 1].start()
        for i in range(count):
            across[i, ("up", step)].start()
        yield
        for chain in chains:
            chain.down[step].got()
            if step + 1 < at.depth:
                chain.down[step + 1].start()
        for i in range(count):
            across[i, ("down", step)].start()
    yield
    for transfer in across.values():
        transfer.got()


def halvings(depth):
    return sorted(range(1, depth), key=lambda bits: (bits & -bits, -bits)) + [0]


def merging(bits, depth):
    limit = bits & -bits if bits else depth
    return [bits + e for e in (1 << i for i in range(depth.bit_length())) if e < limit]


def add_all(target, sources):
    count = target.shape[0]
    step = 16 if count % 16 == 0 else 8

    def one(index, carry):
        rows = pl.ds(pl.multiple_of(index * step, step), step)
        total = sources[0][rows, :].astype(jnp.float32)
        for source in sources[1:]:
            total = total + source[rows, :].astype(jnp.float32)
        target[rows, :] = total.astype(target.dtype)
        return carry

    lax.fori_loop(0, count // step, one, 0)


def collect(net, at, parts, outs, buffers, chained):
    depth = at.depth if chained else 1
    part_of = (
        (lambda part, t, x, k: part.at[t, x, k]) if chained else (lambda part, t, x, k: part.at[x, k])
    )
    loads, partner, across, beyond = {}, {}, {}, {}
    for i, (part, buffer) in enumerate(zip(parts, buffers)):
        own, core, wide = buffer["own"], buffer["core"], buffer["wide"]
        for s in range(depth):
            t = at.flip_z(s) if chained else 0
            for step in range(at.breadth):
                x = at.later_x(step)
                loads[i, s, step] = Local(
                    net,
                    lambda part=part, t=t, x=x: part_of(part, t, x, at.k),
                    lambda own=own, s=s, step=step: own.at[s, step],
                )
                partner[i, s, step] = Transfer(
                    net,
                    lambda part=part, t=t, x=x: part_of(part, t, x, 1 - at.k),
                    lambda core=core, s=s, step=step: core.at[s, step],
                    at.device(k=1 - at.k),
                )
                if step > 0:
                    across[i, s, step] = Transfer(
                        net,
                        lambda own=own, s=s, step=step: own.at[s, step],
                        lambda wide=wide, s=s, step=step: wide.at[step - 1, s],
                        at.device(x=x),
                    )
            if s > 0:
                beyond[i, s] = Transfer(
                    net,
                    lambda own=own, s=s: own.at[s, 0],
                    lambda buffer=buffer, s=s: buffer["far"].at[s - 1],
                    at.device(z=at.flip_z(s & -s)),
                )
    steps = list(range(1, at.breadth)) + [0]
    spans = halvings(depth)
    count = len(parts)
    for i in range(count):
        for s in spans:
            for step in steps:
                partner[i, s, step].start()
                loads[i, s, step].start()
    for i in range(count):
        own, core = buffers[i]["own"], buffers[i]["core"]
        for s in spans:
            yield
            for step in steps:
                loads[i, s, step].wait()
                partner[i, s, step].got()
                if step > 0:
                    add_rows(own.at[s, step], own.at[s, step], core.at[s, step])
                    across[i, s, step].start()
    for i in range(count):
        own, core, wide = buffers[i]["own"], buffers[i]["core"], buffers[i]["wide"]
        for s in spans:
            yield
            for step in steps[:-1]:
                across[i, s, step].got()
            terms = [own.at[s, 0], core.at[s, 0]] + [wide.at[step - 1, s] for step in steps[:-1]]
            for other in merging(s, depth):
                beyond[i, other].got()
                terms.append(buffers[i]["far"].at[other - 1])
            if s > 0:
                add_all(own.at[s, 0], terms)
                beyond[i, s].start()
            else:
                add_all(outs[i], terms)


def fold(net, at, parts, outs, buffers):
    mine = at.x * 2 + at.k
    members = 2 * at.breadth
    loads, across, beyond, swap, stores = {}, {}, {}, {}, []
    for i, (part, buffer) in enumerate(zip(parts, buffers)):
        own, core, far = buffer["own"], buffer["core"], buffer["far"]
        for s in range(at.depth):
            t = at.flip_z(s)
            loads[i, s] = Local(
                net,
                lambda part=part, t=t: part.at[t, at.y],
                lambda own=own, s=s: own.at[s],
            )
            across[i, s] = Transfer(
                net,
                lambda part=part, t=t: part.at[t, 1 - at.y],
                lambda core=core, s=s: core.at[s],
                at.device(y=1 - at.y),
            )
            if s > 0:
                beyond[i, s] = Transfer(
                    net,
                    lambda own=own, s=s: own.at[s],
                    lambda far=far, s=s: far.at[s - 1],
                    at.device(z=at.flip_z(s & -s)),
                )
        slot = lambda i=i: outs[i].at[mine]
        stores.append(Local(net, lambda own=own: own.at[0, mine], slot))
        for step in range(at.breadth):
            for flip in (0, 1):
                if step == 0 and flip == 0:
                    continue
                x = at.later_x(step)
                k = 1 - at.k if flip else at.k
                swap[i, step, flip] = Transfer(
                    net,
                    lambda own=own, x=x, k=k: own.at[0, x * 2 + k],
                    slot,
                    at.device(x=x, k=k),
                )
    count = len(parts)
    spans = halvings(at.depth)
    for s in spans:
        for i in range(count):
            across[i, s].start()
            loads[i, s].start()
    for s in spans:
        for i in range(count):
            yield
            own, core, far = buffers[i]["own"], buffers[i]["core"], buffers[i]["far"]
            loads[i, s].wait()
            across[i, s].got()
            others = merging(s, at.depth)
            for other in others:
                beyond[i, other].got()
            for member in range(members):
                add_all(
                    own.at[s, member],
                    [own.at[s, member], core.at[s, member]]
                    + [far.at[other - 1, member] for other in others],
                )
            if s > 0:
                beyond[i, s].start()
                continue
            stores[i].start()
            for (j, step, flip), transfer in swap.items():
                if j == i:
                    transfer.start()
    yield
    for transfer in swap.values():
        transfer.got()
    for store in stores:
        store.wait()


def everyone(at):
    return [
        (s, flip, step, turn)
        for s in range(at.depth)
        for flip in (0, 1)
        for step in range(at.breadth)
        for turn in (0, 1)
        if (s, flip, step, turn) != (0, 0, 0, 0)
    ]


def hand_out(net, at, table, out):
    members = 2 * at.breadth
    number = lambda z, y, x, k: (z * 2 + y) * members + x * 2 + k
    mine = number(at.z, at.y, at.x, at.k)
    transfers = []
    for s, flip, step, turn in everyone(at):
        z, x = at.later_z(s), at.later_x(step)
        y = 1 - at.y if flip else at.y
        k = 1 - at.k if turn else at.k
        transfers.append(
            Transfer(
                net,
                lambda z=z, y=y, x=x, k=k: table.at[number(z, y, x, k)],
                lambda: out.at[mine],
                at.device(z, y, x, k),
            )
        )
    kept = Local(net, lambda: table.at[mine], lambda: out.at[mine])
    for transfer in transfers:
        transfer.start()
    kept.start()
    for _ in range(64):
        yield
    kept.wait()
    for transfer in transfers:
        transfer.got()


def exchange(label, ident, sizes, kinds, inputs, outputs, scratch, routines, micros=1):
    space = lambda inside: pltpu.VMEM if inside else pl.ANY

    def kernel(*refs):
        sources = refs[: len(inputs)]
        targets = refs[len(inputs) : len(inputs) + len(outputs)]
        held = refs[len(inputs) + len(outputs) : -3]
        at, net = Place(*sizes), Net(*refs[-3:])
        greet(at, kinds)
        run_all(routines(net, at, sources, targets, held))
        net.settle()

    slots = 40 * sizes[0]
    return pl.pallas_call(
        kernel,
        name=label,
        out_shape=[shape for shape, _ in outputs],
        in_specs=[pl.BlockSpec(memory_space=space(inside)) for _, inside in inputs],
        out_specs=[pl.BlockSpec(memory_space=space(inside)) for _, inside in outputs],
        scratch_shapes=list(scratch)
        + [pltpu.SemaphoreType.DMA((slots,))] * 2
        + [pltpu.SemaphoreType.DMA((slots,))],
        cost_estimate=pl.CostEstimate(
            flops=0, bytes_accessed=micros * 3000000, transcendentals=0
        ),
        compiler_params=pltpu.CompilerParams(
            collective_id=ident,
            has_side_effects=True,
            vmem_limit_bytes=(60 if sizes[0] <= 4 else 63) << 20,
        ),
    )(*[array for array, _ in inputs])


def permute(array, depth, step, flip):
    pairs = [
        (z * 2 + y, ((z + step) % depth) * 2 + (1 - y if flip else y))
        for z in range(depth)
        for y in range(2)
    ]
    return lax.ppermute(array, "rows", pairs)


def shuffle(label, sizes, arrays, stages, outs, moves, most):
    def kernel(*refs):
        ins, targets = refs[: len(arrays)], refs[len(arrays) : len(arrays) + len(outs)]
        held = refs[len(arrays) + len(outs) : -2]
        loaded, stored = refs[-2:]
        started, copies = [], []
        plan = moves(Place(*sizes), ins, held, targets)
        for loads, _ in plan:
            for source, target in loads:
                copy = pltpu.make_async_copy(source, target, loaded.at[len(started)])
                copy.start()
                started.append(copy)
        pending = iter(started)
        for loads, stores in plan:
            for _ in loads:
                next(pending).wait()
            for source, target in stores:
                copy = pltpu.make_async_copy(source, target, stored.at[len(copies)])
                copy.start()
                copies.append(copy)
        for copy in copies:
            copy.wait()

    size = sum(stage.size * stage.dtype.itemsize for stage in stages)
    slots = most * len(stages)
    return pl.pallas_call(
        kernel,
        name=label,
        out_shape=outs,
        in_specs=[pl.BlockSpec(memory_space=pl.ANY)] * len(arrays),
        out_specs=[pl.BlockSpec(memory_space=pl.ANY)] * len(outs),
        scratch_shapes=[pltpu.VMEM(stage.shape, stage.dtype) for stage in stages]
        + [pltpu.SemaphoreType.DMA((slots,)), pltpu.SemaphoreType.DMA((slots,))],
        cost_estimate=pl.CostEstimate(flops=0, bytes_accessed=2 * size, transcendentals=0),
        compiler_params=pltpu.CompilerParams(vmem_limit_bytes=60 << 20),
    )(*arrays)


def widen(label, sizes, blocks, outs, parts):
    shares = sorted({(outs[out].shape[-2], share) for _, _, out, share, _ in parts})

    def kernel(*refs):
        ins, targets = refs[: len(blocks)], refs[len(blocks) : len(blocks) + len(outs)]
        held = refs[len(blocks) + len(outs) : -len(shares) - 2]
        wide = refs[-len(shares) - 2 : -2]
        loaded, stored = refs[-2:]
        at = Place(*sizes)
        loads = [
            pltpu.make_async_copy(source, held[i], loaded.at[i]) for i, source in enumerate(ins)
        ]
        for load in loads:
            load.start()
        waited, turns, previous = set(), {}, {}
        for block, distance, out, share, pieces in parts:
            if block not in waited:
                loads[block].wait()
                waited.add(block)
            kind = shares.index((outs[out].shape[-2], share))
            turn = turns.get(kind, 0) % 2
            turns[kind] = turns.get(kind, 0) + 1
            if (kind, turn) in previous:
                previous[kind, turn].wait()
            buffer = wide[kind].at[turn]
            for row, column, count, place in pieces:
                widen_rows(
                    buffer.at[pl.ds(place, count), :],
                    held[block].at[pl.ds(row, count), pl.ds(column, share)],
                )
            z = at.later_z((sizes[0] - distance) % sizes[0])
            if len(outs[out].shape) == 3:
                target = targets[out].at[z]
            else:
                target = targets[out].at[:, pl.ds(pl.multiple_of(z * share, share), share)]
            copy = pltpu.make_async_copy(buffer, target, stored.at[2 * kind + turn])
            copy.start()
            previous[kind, turn] = copy
        for copy in previous.values():
            copy.wait()

    size = sum(block.size for block in blocks)
    return pl.pallas_call(
        kernel,
        name=label,
        out_shape=outs,
        in_specs=[pl.BlockSpec(memory_space=pl.ANY)] * len(blocks),
        out_specs=[pl.BlockSpec(memory_space=pl.ANY)] * len(outs),
        scratch_shapes=[pltpu.VMEM(block.shape, block.dtype) for block in blocks]
        + [pltpu.VMEM((2,) + share, jnp.float32) for share in shares]
        + [pltpu.SemaphoreType.DMA((len(blocks),)), pltpu.SemaphoreType.DMA((2 * len(shares),))],
        cost_estimate=pl.CostEstimate(flops=0, bytes_accessed=6 * size, transcendentals=0),
        compiler_params=pltpu.CompilerParams(vmem_limit_bytes=60 << 20),
    )(*blocks)


def shape_of(dims, kind=jnp.bfloat16):
    return jax.ShapeDtypeStruct(tuple(dims), kind)


def multiply(operand, matrix):
    return jnp.dot(operand, matrix, preferred_element_type=jnp.float32)


def against(operand, matrix):
    return lax.dot_general(
        operand, matrix, (((1,), (1,)), ((), ())), preferred_element_type=jnp.float32
    )


def outer_sum(operand, matrix):
    return lax.dot_general(
        operand, matrix, (((0,), (0,)), ((), ())), preferred_element_type=jnp.float32
    )


def norm_forward(values):
    scaling = lax.rsqrt(jnp.mean(values * values, axis=-1, keepdims=True) + epsilon)
    return (values * scaling, scaling)


def norm_backward(upstream, normed_unit, scaling, gain_vector):
    weighted = upstream * gain_vector
    average = jnp.mean(weighted * normed_unit, axis=-1, keepdims=True)
    return (scaling * (weighted - normed_unit * average), jnp.sum(upstream * normed_unit, axis=0))


def visible(query_ids, query_codes, key_ids, key_codes):
    matches = query_ids[:, None] == key_ids[None, :]
    return jnp.logical_and(matches, key_codes[None, :] <= query_codes[:, None])


def gated(gate_value, expand_value):
    return jax.nn.gelu(gate_value, approximate=True) * expand_value


def low(values):
    return values.astype(jnp.bfloat16)


def gated_grads(gate_value, expand_value, inside_grad):
    gate, expand = gate_value.astype(jnp.float32), expand_value.astype(jnp.float32)
    upstream = inside_grad.astype(jnp.float32)
    slope = float((2.0 / math.pi) ** 0.5)
    square = gate * gate
    bend = jnp.tanh(slope * gate * (1.0 + 0.044715 * square))
    half = 0.5 * (1.0 + bend)
    rise = half + 0.5 * gate * (1.0 - bend * bend) * slope * (1.0 + 3.0 * 0.044715 * square)
    return (low(upstream * expand * rise), low(upstream * gate * half))


def feed_forward(normed_rows, cotangent, gate_weight, expand_weight, down_weight):
    gate_value = multiply(normed_rows, gate_weight)
    expand_value = multiply(normed_rows, expand_weight)
    inside_low = low(gated(gate_value, expand_value))
    part = low(against(inside_low, down_weight))
    inside_grad = multiply(cotangent, down_weight)
    gate_low, expand_low = gated_grads(gate_value, expand_value, inside_grad)
    normed_grad = low(against(gate_low, gate_weight) + against(expand_low, expand_weight))
    weight_grads = (
        outer_sum(normed_rows, gate_low),
        outer_sum(normed_rows, expand_low),
        outer_sum(cotangent, inside_low),
    )
    return (part, normed_grad, weight_grads)


def by_member(parts, members):
    rows = parts[0].shape[0]
    columns = jnp.concatenate([part.reshape(rows, members, -1) for part in parts], 2)
    return jnp.swapaxes(columns, 0, 1)


def body(
    prefix_tokens,
    action_tokens,
    prefix_cotangent,
    action_cotangent,
    prefix_segments,
    action_codes,
    prefix_query,
    prefix_key,
    prefix_value,
    prefix_mixer,
    action_query,
    action_key,
    action_value,
    action_mixer,
    prefix_prenorm,
    prefix_midnorm,
    action_prenorm,
    action_midnorm,
    prefix_gate,
    prefix_expand,
    prefix_down,
    action_gate,
    action_expand,
    action_down,
):
    members = lax.axis_size("cam")
    row_count = lax.axis_size("rows")
    depth, breadth = row_count // 2, members // 2
    sizes = (depth, breadth)
    head_size = prefix_key.shape[1]
    width = prefix_query.shape[1] // members
    heads = width // head_size
    pair = 2 * head_size // members
    inverse = float(head_size) ** (-0.5)
    lead_count, lead_width = prefix_tokens.shape
    tail_count, tail_width = action_tokens.shape
    idents = iter(range(100))

    def cam_spread(label, shards):
        return exchange(
            label,
            next(idents),
            sizes,
            ("cam",),
            [(shard, True) for shard in shards],
            [(shape_of((breadth, 2) + shard.shape), False) for shard in shards],
            [],
            lambda net, at, ins, outs, held: [spread(net, at, ins, outs, False)],
        )

    def cam_collect(label, parts):
        blocks = [part.shape[-2:] for part in parts]
        scratch = []
        for block in blocks:
            scratch += [
                pltpu.VMEM((1, breadth) + block, jnp.bfloat16),
                pltpu.VMEM((1, breadth) + block, jnp.bfloat16),
                pltpu.VMEM((breadth - 1, 1) + block, jnp.bfloat16),
            ]

        def routines(net, at, ins, outs, held):
            buffers = [
                dict(own=held[3 * i], core=held[3 * i + 1], wide=held[3 * i + 2])
                for i in range(len(parts))
            ]
            return [collect(net, at, ins, outs, buffers, False)]

        return exchange(
            label,
            next(idents),
            sizes,
            ("cam",),
            [(part, False) for part in parts],
            [(shape_of(block, jnp.float32), True) for block in blocks],
            scratch,
            routines,
        )

    lead_slice = prefix_gate.shape[1] // depth
    tail_slice = action_gate.shape[1] // depth
    lead_block, tail_block = prefix_gate.shape[0], action_gate.shape[0]
    floor = lax.axis_index("rows") // 2
    side = lax.rem(lax.axis_index("rows"), 2)
    ratio = lead_slice // tail_slice
    strip = tail_block // ratio
    packed = tail_slice % 128 == 0 and strip % 16 == 0
    upper = shape_of((2 * lead_block + (3 * strip if packed else 0), lead_slice))
    lower = shape_of((lead_block, lead_slice))

    def strips(i, start):
        return [(start + i * strip, j * tail_slice, j * strip) for j in range(ratio)]

    def cut(net, at, ins, outs, held):
        loads, stores = [], []
        for step in range(depth):
            z = at.later_z(step)
            columns = pl.ds(pl.multiple_of(z * lead_slice, lead_slice), lead_slice)
            high, down = held[step], held[depth + step]
            pairs = [
                (ins[i].at[:, columns], high.at[pl.ds(i * lead_block, lead_block), :])
                for i in range(2)
            ]
            if packed:
                narrow = pl.ds(pl.multiple_of(z * tail_slice, tail_slice), tail_slice)
                pairs += [
                    (
                        ins[3 + i].at[pl.ds(place, strip), narrow],
                        high.at[pl.ds(row, strip), pl.ds(column, tail_slice)],
                    )
                    for i in range(3)
                    for row, column, place in strips(i, 2 * lead_block)
                ]
            pairs.append((ins[2].at[:, columns], down))
            for source, target in pairs:
                loads.append(Local(net, lambda source=source: source, lambda target=target: target))
            for i in (step, depth + step):
                stores.append(Local(net, lambda i=i: held[i], lambda i=i: outs[i]))
        for load in loads:
            load.start()
        yield
        yield
        for load in loads:
            load.wait()
        for store in stores:
            store.start()
        for _ in range(8):
            yield
        for store in stores:
            store.wait()

    lead_weights = [prefix_gate, prefix_expand, prefix_down]
    tail_weights = [action_gate, action_expand, action_down]
    cut_inputs = lead_weights + (tail_weights if packed else [])
    groups = 2 if packed else 3
    tails_cut = [
        jnp.stack(
            [
                lax.dynamic_slice_in_dim(
                    weight, lax.rem(floor + step, depth) * tail_slice, tail_slice, 1
                )
                for weight in tail_weights
            ]
        )
        for step in range(0 if packed else depth)
    ]
    dealt, mirrored = {}, {}

    def deal(group, cuts):
        for step, block in enumerate(cuts):
            dealt[group, step] = permute(block, depth, step, False) if step > 0 else block

    def mirror(kinds, step):
        for group in kinds:
            mirrored[group, step] = permute(dealt[group, step], depth, 0, True)

    def tied(arrays, kinds, step):
        keys = [(group, step) for group in kinds]
        arrays, blocks = lax.optimization_barrier((arrays, [dealt[key] for key in keys]))
        dealt.update(zip(keys, blocks))
        return arrays

    soon = [0] if packed else [0, 2]

    lead_float = prefix_tokens.astype(jnp.float32)
    tail_float = action_tokens.astype(jnp.float32)
    lead_unit, lead_scale = norm_forward(lead_float)
    tail_unit, tail_scale = norm_forward(tail_float)
    lead_low = low(lead_unit * prefix_prenorm)
    tail_low = low(tail_unit * action_prenorm)
    lead_pack = by_member([prefix_query, jnp.concatenate([prefix_key, prefix_value], 1)], members)
    tail_pack = by_member([action_query, jnp.concatenate([action_key, action_value], 1)], members)
    lead_mixers = by_member([prefix_mixer], members)
    tail_mixers = by_member([action_mixer], members)
    packs = [lead_pack, tail_pack, lead_mixers, tail_mixers]
    shards = [prefix_cotangent, action_cotangent]
    first = [lead_low, tail_low] + packs + shards
    fanned = lambda pack: (shape_of((depth, 2) + pack.shape), False)
    gathered = lambda shard: (shape_of((depth, breadth, 2) + shard.shape), False)
    started = exchange(
        "first",
        next(idents),
        sizes,
        ("z", "y", "cam"),
        [(array, True) for array in first] + [(weight, False) for weight in cut_inputs],
        [(shape_of((breadth, 2) + array.shape), False) for array in first[:2]]
        + [fanned(pack) for pack in packs]
        + [gathered(shard) for shard in shards]
        + [(upper, False)] * depth
        + [(lower, False)] * depth,
        [pltpu.VMEM(upper.shape, upper.dtype)] * depth
        + [pltpu.VMEM(lower.shape, lower.dtype)] * depth,
        lambda net, at, ins, outs, held: [
            fan(net, at, ins[2:4], outs[2:4]),
            spread(net, at, ins[:2], outs[:2], False),
            fan(net, at, ins[4:6], outs[4:6]),
            spread(net, at, ins[6:8], outs[6:8], True),
            cut(net, at, ins[8:], outs[8:], held),
        ],
    )
    started, tails_cut = lax.optimization_barrier((started, tails_cut))
    started, high_cuts, low_cuts = started[:8], started[8 : 8 + depth], started[8 + depth :]
    deal(0, high_cuts)
    if not packed:
        deal(2, tails_cut)
    dealt[1, 0] = low_cuts[0]
    lead_normed, tail_normed, lead_in, tail_in, lead_mix, tail_mix, *uppers = started
    lead_upper, tail_upper = [array.reshape(-1, array.shape[-1]) for array in uppers]
    lead_mix, tail_mix = lead_mix.reshape(lead_width, width), tail_mix.reshape(tail_width, width)
    mirror(soon, 0)
    mirror([1], 0)
    lead_normed = lead_normed.reshape(-1, lead_width)
    tail_normed = tail_normed.reshape(-1, tail_width)
    lead_in = lead_in.reshape(lead_width, -1)
    tail_in = tail_in.reshape(tail_width, -1)
    lead_total, tail_total = lead_normed.shape[0], tail_normed.shape[0]

    projected = low(
        jnp.concatenate([multiply(lead_normed, lead_in), multiply(tail_normed, tail_in)], 0)
    )
    (pairs,) = cam_spread("pairs", [projected[:, width:]])
    pairs = jnp.swapaxes(pairs.reshape(members, -1, pair), 0, 1).reshape(-1, 2 * head_size)

    segment_row = prefix_segments[0]
    code_row = action_codes[0]
    token_ids = jnp.concatenate(
        [segment_row, jnp.arange(code_row.shape[0], dtype=jnp.int32) // ACTT]
    )
    token_codes = jnp.concatenate([jnp.zeros(segment_row.shape, jnp.int32), code_row])
    queries = projected[:, :width].reshape(-1, heads, head_size)
    keys, values = pairs[:, :head_size], pairs[:, head_size:]
    allowed = visible(token_ids, token_codes, token_ids, token_codes)
    logits = jnp.einsum("qhd,kd->hqk", queries, keys, preferred_element_type=jnp.float32) * inverse
    scores = jnp.where(allowed[None], logits, masked_score)
    exponent = jnp.exp(scores - jnp.max(scores, axis=2, keepdims=True))
    totals = jnp.transpose(jnp.sum(exponent, axis=2))[:, :, None]
    probs = low(exponent)
    attention = (
        jnp.einsum("hqk,kd->qhd", probs, values, preferred_element_type=jnp.float32) / totals
    )
    mixed = low(attention.reshape(-1, width))
    cam_blocks = lambda rows: low(rows).reshape(breadth, 2, -1, rows.shape[1])
    lead_sum, tail_sum = cam_collect(
        "mixing",
        [
            cam_blocks(against(mixed[:lead_total], lead_mix)),
            cam_blocks(against(mixed[lead_total:], tail_mix)),
        ],
    )
    lead_sum, tail_sum = tied([lead_sum, tail_sum], soon, 1)
    mirror(soon, 1)
    lead_hidden = lead_float + lead_sum
    tail_hidden = tail_float + tail_sum
    lead_center, lead_factor = norm_forward(lead_hidden)
    tail_center, tail_factor = norm_forward(tail_hidden)
    lead_second = low(lead_center * prefix_midnorm)
    tail_second = low(tail_center * action_midnorm)

    for step in range(2, depth):
        lead_second, tail_second = tied([lead_second, tail_second], soon, step)
        mirror(soon, step)

    def placed(label, kinds, firsts, outs):
        marks = [
            (group, step, flip) for group in kinds for step in range(depth) for flip in (0, 1)
        ]
        blocks = [(mirrored if flip else dealt)[group, step] for group, step, flip in marks]

        def moves(at, ins, held, targets):
            lists = []
            for number, (group, step, flip) in enumerate(marks):
                z = at.later_z((depth - step) % depth)
                y = 1 - at.y if flip else at.y
                block, slot = held[number], firsts[group]
                if group == 2:
                    stores = [(block.at[i], targets[slot + i].at[z, y]) for i in range(3)]
                else:
                    stores = [
                        (
                            block.at[pl.ds(i * lead_block, lead_block), :],
                            targets[slot + i].at[z, y],
                        )
                        for i in range(1 if group == 1 else 2)
                    ]
                if group == 0 and packed:
                    stores += [
                        (
                            block.at[pl.ds(row, strip), pl.ds(column, tail_slice)],
                            targets[2 + i].at[z, y, pl.ds(place, strip), :],
                        )
                        for i in range(3)
                        for row, column, place in strips(i, 2 * lead_block)
                    ]
                lists.append(([(ins[number], block)], stores))
            return lists

        most = 3 + 3 * ratio if packed else 3
        return [
            weight.reshape(-1, weight.shape[-1])
            for weight in shuffle(label, sizes, blocks, blocks, outs, moves, most)
        ]

    lead_out_shape = shape_of((depth, 2, lead_block, lead_slice))
    tail_out_shape = shape_of((depth, 2, tail_block, tail_slice))

    def send_across(packs):
        sent = []
        for pack in packs:
            pack = [low(grad).reshape(depth, 2, -1, grad.shape[1]) for grad in pack]
            if len(pack) > 1 and packed:
                pack[1:] = [
                    jnp.concatenate(jnp.split(grad, ratio, axis=2), axis=3) for grad in pack[1:]
                ]
            tables = [pack] if packed or len(pack) == 1 else [pack[:1], pack[1:]]
            for table in tables:
                take = lambda y: jnp.concatenate(
                    [lax.dynamic_index_in_dim(part, y, 1, False) for part in table], 1
                )
                own, other = take(side), permute(take(1 - side), depth, 0, True)
                sent.append((own, other))
        return sent

    def summed_blocks(pairs):
        summed = jnp.concatenate(
            [low(own.astype(jnp.float32) + other.astype(jnp.float32)) for own, other in pairs], 1
        )
        return [
            lax.dynamic_index_in_dim(summed, lax.rem(floor + step, depth), 0, False)
            for step in range(depth)
        ]

    def pass_on(pairs):
        blocks = summed_blocks(pairs)
        return blocks[:1] + [
            permute(block, depth, step + 1, False) for step, block in enumerate(blocks[1:])
        ]

    shards = [lead_second, tail_second]
    lead_all, tail_all = [
        array.reshape(-1, array.shape[-1])
        for array in exchange(
            "gather",
            next(idents),
            sizes,
            ("z", "cam"),
            [(shard, True) for shard in shards],
            [gathered(shard) for shard in shards],
            [],
            lambda net, at, ins, outs, held: [spread(net, at, ins, outs, True)],
        )
    ]
    (lead_all, tail_all), low_cuts = lax.optimization_barrier(((lead_all, tail_all), low_cuts))
    dealt_here = dealt[1, 0]
    deal(1, low_cuts)
    dealt[1, 0] = dealt_here
    lead_gate, lead_expand, tail_gate, tail_expand, tail_down = placed(
        "upper", soon, {0: 0, 2: 2}, [lead_out_shape] * 2 + [tail_out_shape] * 3
    )
    tail_out, tail_back, tail_ffgrads = feed_forward(
        tail_all, tail_upper, tail_gate, tail_expand, tail_down
    )
    (lead_all, tail_out, tail_back), tail_ffgrads = lax.optimization_barrier(
        ((lead_all, tail_out, tail_back), [low(grad) for grad in tail_ffgrads])
    )
    lead_all = tied(lead_all, [1], 1)
    mirror([1], 1)
    gate_value = low(multiply(lead_all, lead_gate))
    gate_value, lead_all = tied((gate_value, lead_all), [1], 2)
    mirror([1], 2)
    expand_value = low(multiply(lead_all, lead_expand))
    for step in range(3, depth):
        gate_value, expand_value = tied((gate_value, expand_value), [1], step)
        mirror([1], step)
    inside_low = low(gated(gate_value.astype(jnp.float32), expand_value.astype(jnp.float32)))
    down_grad = low(outer_sum(lead_upper, inside_low))
    down_grad, lead_upper = lax.optimization_barrier((down_grad, lead_upper))
    returns = send_across([[down_grad] + tail_ffgrads])
    (lead_down,) = placed("lower", [1], {1: 0}, [lead_out_shape])
    inside_grad = low(multiply(lead_upper, lead_down))
    gate_low, expand_low = gated_grads(gate_value, expand_value, inside_grad)
    returns += send_across(
        [[outer_sum(lead_all, gate_low)], [outer_sum(lead_all, expand_low)]]
    )
    others = [other for _, other in returns[-2:]]
    sources = [own for own, _ in returns[-2:]]
    (inside_low, gate_low, expand_low), sources = lax.optimization_barrier(
        ((inside_low, gate_low, expand_low), sources)
    )
    returns[-2:] = list(zip(sources, others))
    lead_back = low(against(gate_low, lead_gate) + against(expand_low, lead_expand))
    (inside_low, lead_back), returns[:-2] = lax.optimization_barrier(
        ((inside_low, lead_back), returns[:-2])
    )
    blocks_back = [pass_on(returns[:1])]
    if not packed:
        blocks_back.append(pass_on(returns[1:2]))
    lead_out = low(against(inside_low, lead_down))

    def token_blocks(rows):
        return rows.reshape(depth, breadth, 2, -1, rows.shape[1])

    def sum_scratch(parts):
        scratch = []
        for part in parts:
            block = part.shape[3:]
            scratch += [
                pltpu.VMEM((depth, breadth) + block, jnp.bfloat16),
                pltpu.VMEM((depth, breadth) + block, jnp.bfloat16),
                pltpu.VMEM((breadth - 1, depth) + block, jnp.bfloat16),
                pltpu.VMEM((depth - 1,) + block, jnp.bfloat16),
            ]
        return scratch

    def sum_routine(net, at, ins, outs, held):
        names = ("own", "core", "wide", "far")
        buffers = [dict(zip(names, held[4 * i : 4 * i + 4])) for i in range(len(ins))]
        return collect(net, at, ins, outs, buffers, True)

    backs = [token_blocks(lead_back), token_blocks(tail_back)]
    lead_summed, tail_summed = exchange(
        "collect",
        next(idents),
        sizes,
        ("deal", "cam"),
        [(part, False) for part in backs],
        [(shape_of(part.shape[3:], jnp.float32), True) for part in backs],
        sum_scratch(backs),
        lambda net, at, ins, outs, held: [sum_routine(net, at, ins, outs, held)],
    )

    (lead_summed, tail_summed), rest, blocks_back = lax.optimization_barrier(
        ((lead_summed, tail_summed), returns[-2:], blocks_back)
    )
    back_blocks = {}
    for i, both in enumerate(rest):
        back_blocks.update({(i, s): block for s, block in enumerate(summed_blocks([both]))})
    leaving = [(i, s) for s in [1] + list(range(3, depth)) + [2] for i in (0, 1)]
    stops = [0, len(leaving) // 3, len(leaving) * 2 // 3, len(leaving)]
    turns = [leaving[stops[i] : stops[i + 1]] for i in range(3)]

    def leave(turn):
        for i, s in turns[turn]:
            back_blocks[i, s] = permute(back_blocks[i, s], depth, s, False)

    def back_tied(arrays, turn):
        marks = turns[turn] + (turns[turn + 1] if turn < 2 else [])
        arrays, pieces = lax.optimization_barrier((arrays, [back_blocks[mark] for mark in marks]))
        back_blocks.update(zip(marks, pieces))
        if turn < 2:
            leave(turn + 1)
        return arrays

    leave(0)
    lead_residual, lead_middle = norm_backward(
        lead_summed, lead_center, lead_factor, prefix_midnorm
    )
    tail_residual, tail_middle = norm_backward(
        tail_summed, tail_center, tail_factor, action_midnorm
    )
    lead_upstream = prefix_cotangent.astype(jnp.float32) + lead_residual
    tail_upstream = action_cotangent.astype(jnp.float32) + tail_residual
    lead_sent, tail_sent = cam_spread("sent", [low(lead_upstream), low(tail_upstream)])
    lead_sent, tail_sent = back_tied((lead_sent, tail_sent), 0)
    lead_sent = lead_sent.reshape(-1, lead_width)
    tail_sent = tail_sent.reshape(-1, tail_width)
    lead_mixing = outer_sum(lead_sent, mixed[:lead_total])
    tail_mixing = outer_sum(tail_sent, mixed[lead_total:])
    attention_grad = jnp.concatenate(
        [multiply(lead_sent, lead_mix), multiply(tail_sent, tail_mix)], 0
    ).reshape(-1, heads, head_size)
    scaled_grad = low(attention_grad / totals)
    deltas = jnp.sum(attention_grad * attention, axis=2, keepdims=True) / totals
    value_grad = jnp.einsum("hqk,qhd->kd", probs, scaled_grad, preferred_element_type=jnp.float32)
    prob_grad = jnp.einsum("qhd,kd->hqk", scaled_grad, values, preferred_element_type=jnp.float32)
    score_grad = low(exponent * (prob_grad - jnp.transpose(deltas, (1, 0, 2))))
    key_grad = (
        jnp.einsum("hqk,qhd->kd", score_grad, queries, preferred_element_type=jnp.float32) * inverse
    )
    query_grad = (
        jnp.einsum("hqk,kd->qhd", score_grad, keys, preferred_element_type=jnp.float32) * inverse
    )
    pair_parts = low(jnp.concatenate([key_grad, value_grad], 1)).reshape(-1, members, pair)
    pair_parts, query_low, lead_mixing, tail_mixing = lax.optimization_barrier(
        (pair_parts, low(query_grad.reshape(-1, width)), low(lead_mixing), low(tail_mixing))
    )
    (pair_grad,) = cam_collect(
        "pair_grads", [jnp.swapaxes(pair_parts, 0, 1).reshape(breadth, 2, -1, pair)]
    )
    pair_grad = back_tied(pair_grad, 1)
    low_grad = jnp.concatenate([query_low, low(pair_grad)], 1)
    lead_part, tail_part = low_grad[:lead_total], low_grad[lead_total:]
    lead_back, tail_back = cam_collect(
        "backs",
        [cam_blocks(against(lead_part, lead_in)), cam_blocks(against(tail_part, tail_in))],
    )
    (lead_back, tail_back, low_grad, lead_mixing, tail_mixing) = back_tied(
        (lead_back, tail_back, low_grad, lead_mixing, tail_mixing), 2
    )
    lead_part, tail_part = low_grad[:lead_total], low_grad[lead_total:]
    lead_back, lead_first = norm_backward(lead_back, lead_unit, lead_scale, prefix_prenorm)
    tail_back, tail_first = norm_backward(tail_back, tail_unit, tail_scale, action_prenorm)
    lead_input = low(lead_upstream + lead_back)
    tail_input = low(tail_upstream + tail_back)

    owned_lead, owned_tail = prefix_query.shape[0], action_query.shape[0]
    split_rows = lambda grad, rows: low(grad).reshape(depth, 2, members, rows, grad.shape[1])
    attention_parts = [
        split_rows(outer_sum(lead_normed, lead_part), owned_lead),
        split_rows(outer_sum(tail_normed, tail_part), owned_tail),
        split_rows(lead_mixing, owned_lead),
        split_rows(tail_mixing, owned_tail),
    ]
    scratch = []
    for part in attention_parts:
        block = part.shape[2:]
        scratch += [pltpu.VMEM((depth,) + block, jnp.bfloat16)] * 2
        scratch += [pltpu.VMEM((depth - 1,) + block, jnp.bfloat16)]
    gains = [lead_first, lead_middle, tail_first, tail_middle]
    device_count = row_count * members
    table = jnp.concatenate([gain.reshape(device_count, -1) for gain in gains], 1)
    owned = table.shape[1]
    span = -(-owned // 128) * 128
    table = jnp.pad(table, ((0, 0), (0, span - owned)))[:, None, :]
    branches = [token_blocks(lead_out), token_blocks(tail_out)]

    def fold_routines(net, at, ins, outs, held):
        names = ("own", "core", "far")
        buffers = [dict(zip(names, held[3 * i : 3 * i + 3])) for i in range(4)]
        return [
            hand_out(net, at, ins[4], outs[4]),
            fold(net, at, ins[:4], outs[:4], buffers),
            sum_routine(net, at, ins[5:], outs[5:], held[12:]),
        ]

    folded = exchange(
        "fold",
        next(idents),
        sizes,
        ("all",),
        [(part, False) for part in attention_parts]
        + [(table, True)]
        + [(branch, False) for branch in branches],
        [(shape_of(part.shape[2:]), False) for part in attention_parts]
        + [(shape_of(table.shape, jnp.float32), True)]
        + [(shape_of(branch.shape[3:], jnp.float32), True) for branch in branches],
        scratch + sum_scratch(branches),
        fold_routines,
    )
    lead_result = low(lead_hidden + folded[5])
    tail_result = low(tail_hidden + folded[6])

    def split(projection, mixer):
        projection = jnp.swapaxes(projection, 0, 1).astype(jnp.float32)
        rows = projection.shape[0]
        query = projection[:, :, :width].reshape(rows, -1)
        pairs = projection[:, :, width:].reshape(rows, -1)
        mixer = jnp.swapaxes(mixer, 0, 1).reshape(rows, -1).astype(jnp.float32)
        return (query, pairs[:, :head_size], pairs[:, head_size:], mixer)

    lead_grads = split(folded[0], folded[2])
    tail_grads = split(folded[1], folded[3])

    whole_block = [(0, 0, lead_block, 0)]
    parts = []
    for step in range(depth):
        parts.append((step, step, 2, lead_slice, whole_block))
        for i in range(3):
            if packed:
                pieces = [(row, column, strip, place) for row, column, place in strips(i, lead_block)]
                parts.append((step, step, 3 + i, tail_slice, pieces))
            else:
                pieces = [(i * tail_block, 0, tail_block, 0)]
                parts.append((3 * depth + step, step, 3 + i, tail_slice, pieces))
    for i in range(2):
        for step in range(depth):
            parts.append(((1 + i) * depth + step, step, i, lead_slice, whole_block))
    ff_grads = widen(
        "returns",
        sizes,
        blocks_back[0]
        + [back_blocks[i, s] for i in (0, 1) for s in range(depth)]
        + sum(blocks_back[1:], []),
        [shape_of(weight.shape, jnp.float32) for weight in lead_weights]
        + [
            shape_of(
                weight.shape if packed else (depth, tail_block, tail_slice), jnp.float32
            )
            for weight in tail_weights
        ],
        parts,
    )
    if not packed:
        ff_grads = list(ff_grads[:3]) + [
            jnp.swapaxes(grad, 0, 1).reshape(tail_block, -1) for grad in ff_grads[3:]
        ]

    total = jnp.sum(folded[4][:, 0], axis=0)
    gain_grads = []
    offset = 0
    for gain in gains:
        share = gain.shape[0] // device_count
        gain_grads.append(total[offset : offset + share])
        offset += share

    return (
        (lead_result, tail_result, lead_input, tail_input)
        + lead_grads
        + tail_grads
        + tuple(gain_grads)
        + tuple(ff_grads)
    )


def solution(mesh):
    in_specs = (
        P(("rows", "cam"), None),
        P(("rows", "cam"), None),
        P(("rows", "cam"), None),
        P(("rows", "cam"), None),
        P("rows", None),
        P("rows", None),
        P(("rows", "cam"), None),
        P(("rows", "cam"), None),
        P(("rows", "cam"), None),
        P(("rows", "cam"), None),
        P(("rows", "cam"), None),
        P(("rows", "cam"), None),
        P(("rows", "cam"), None),
        P(("rows", "cam"), None),
        P(),
        P(),
        P(),
        P(),
        P("rows", "cam"),
        P("rows", "cam"),
        P("rows", "cam"),
        P("rows", "cam"),
        P("rows", "cam"),
        P("rows", "cam"),
    )
    out_specs = (
        P(("rows", "cam"), None),
        P(("rows", "cam"), None),
        P(("rows", "cam"), None),
        P(("rows", "cam"), None),
        P(("rows", "cam"), None),
        P(("rows", "cam"), None),
        P(("rows", "cam"), None),
        P(("rows", "cam"), None),
        P(("rows", "cam"), None),
        P(("rows", "cam"), None),
        P(("rows", "cam"), None),
        P(("rows", "cam"), None),
        P(("rows", "cam")),
        P(("rows", "cam")),
        P(("rows", "cam")),
        P(("rows", "cam")),
        P("rows", "cam"),
        P("rows", "cam"),
        P("rows", "cam"),
        P("rows", "cam"),
        P("rows", "cam"),
        P("rows", "cam"),
    )
    return jax.shard_map(body, mesh=mesh, in_specs=in_specs, out_specs=out_specs, check_vma=False)
```

```python
import math

import jax
import jax.numpy as jnp
from jax import lax
from jax.experimental import pallas as pl
from jax.experimental.pallas import tpu as pltpu
from jax.sharding import PartitionSpec as P

ACTT = 32


epsilon = 1e-06
masked_score = -1e30


class Place:
    def __init__(self, depth, breadth):
        self.depth, self.breadth = depth, breadth
        row, member = lax.axis_index("rows"), lax.axis_index("cam")
        self.z, self.y = row // 2, row % 2
        self.x, self.k = member // 2, member % 2

    def device(self, z=None, y=None, x=None, k=None):
        z = self.z if z is None else z
        y = self.y if y is None else y
        x = self.x if x is None else x
        k = self.k if k is None else k
        return (z * 2 + y, x * 2 + k)

    def later_x(self, step):
        return lax.rem(self.x + step, self.breadth)

    def later_z(self, step):
        return lax.rem(self.z + step, self.depth)

    def flip_z(self, bits):
        z, bit = self.z, 1
        while bit < self.depth:
            if bits & bit:
                z = z + bit - 2 * bit * lax.rem(self.z // bit, 2)
            bit *= 2
        return z


def guarded(condition, action):
    if condition is None:
        action()
    else:
        pl.when(condition)(action)


class Transfer:
    def __init__(self, net, source, target, device, sends=None, gets=None):
        self.net, self.number = net, net.remote
        net.remote += 1
        self.source, self.target, self.device = source, target, device
        self.sends, self.gets = sends, gets
        net.pending.append(self)

    def describe(self):
        return pltpu.make_async_remote_copy(
            src_ref=self.source(),
            dst_ref=self.target(),
            send_sem=self.net.sent.at[self.number],
            recv_sem=self.net.received.at[self.number],
            device_id=self.device,
            device_id_type=pl.DeviceIdType.MESH,
        )

    def start(self):
        guarded(self.sends, lambda: self.describe().start())

    def got(self):
        guarded(self.gets, lambda: self.describe().wait_recv())

    def finish(self):
        guarded(self.sends, lambda: self.describe().wait_send())


class Local:
    def __init__(self, net, source, target):
        self.net, self.number = net, net.local
        net.local += 1
        self.source, self.target = source, target

    def describe(self):
        return pltpu.make_async_copy(
            self.source(), self.target(), self.net.moved.at[self.number]
        )

    def start(self):
        self.describe().start()
        return self

    def wait(self):
        self.describe().wait()


class Net:
    def __init__(self, sent, received, moved):
        self.sent, self.received, self.moved = sent, received, moved
        self.remote, self.local = 0, 0
        self.pending = []

    def settle(self):
        for transfer in self.pending:
            transfer.finish()


def greet(at, kinds):
    peers = []
    count = 0
    if "all" in kinds:
        for s, flip, step, turn in everyone(at):
            peers.append(
                (
                    None,
                    at.device(
                        at.later_z(s),
                        1 - at.y if flip else at.y,
                        at.later_x(step),
                        1 - at.k if turn else at.k,
                    ),
                )
            )
    if "z" in kinds and "deal" not in kinds:
        count = count + (at.z > 0).astype(jnp.int32) + (at.z < at.depth - 1).astype(jnp.int32)
        peers.append((at.z > 0, at.device(z=at.z - 1)))
        peers.append((at.z < at.depth - 1, at.device(z=at.z + 1)))
    if "deal" in kinds:
        peers += [(None, at.device(z=at.later_z(step))) for step in range(1, at.depth)]
    if "y" in kinds:
        peers.append((None, at.device(y=1 - at.y)))
    if "cam" in kinds:
        for step in range(at.breadth):
            for core in (at.k, 1 - at.k):
                if step > 0 or core is not at.k:
                    peers.append((None, at.device(x=at.later_x(step), k=core)))
    barrier = pltpu.get_barrier_semaphore()
    for condition, device in peers:
        guarded(
            condition,
            lambda device=device: pl.semaphore_signal(
                barrier, inc=1, device_id=device, device_id_type=pl.DeviceIdType.MESH
            ),
        )
    count = count + sum(1 for condition, _ in peers if condition is None)
    pl.semaphore_wait(barrier, count)


def run_all(routines):
    routines = list(routines)
    while routines:
        alive = []
        for routine in routines:
            try:
                next(routine)
                alive.append(routine)
            except StopIteration:
                pass
        routines = alive


def add_rows(target, first, second):
    count = target.shape[0]
    step = 16 if count % 16 == 0 else 8

    def one(index, carry):
        rows = pl.ds(pl.multiple_of(index * step, step), step)
        total = first[rows, :].astype(jnp.float32) + second[rows, :].astype(jnp.float32)
        target[rows, :] = total.astype(target.dtype)
        return carry

    lax.fori_loop(0, count // step, one, 0)


def widen_rows(target, source):
    count = target.shape[0]
    step = 16 if count % 16 == 0 else 8

    def one(index, carry):
        rows = pl.ds(pl.multiple_of(index * step, step), step)
        target[rows, :] = source[rows, :].astype(target.dtype)
        return carry

    lax.fori_loop(0, count // step, one, 0)


class Chain:
    def __init__(self, net, at, own, place):
        depth = at.depth
        self.up, self.down = {}, {}
        for step in range(1, depth):
            low, high = at.z - step + 1, at.z + step - 1
            self.up[step] = Transfer(
                net,
                own if step == 1 else (lambda low=low: place(low)),
                lambda low=low: place(low),
                at.device(z=at.z + 1),
                sends=(at.z + 1 < depth) & (low >= 0),
                gets=at.z - step >= 0,
            )
            self.down[step] = Transfer(
                net,
                own if step == 1 else (lambda high=high: place(high)),
                lambda high=high: place(high),
                at.device(z=at.z - 1),
                sends=(at.z > 0) & (high < depth),
                gets=at.z + step < depth,
            )


def tags_of(at, chained):
    tags = [("own", at.z, None)]
    if chained:
        for step in range(1, at.depth):
            tags.append((("up", step), at.z - step, at.z - step >= 0))
            tags.append((("down", step), at.z + step, at.z + step < at.depth))
    return tags


def spread(net, at, shards, outs, chained):
    if chained:
        place = lambda out, z, x, k: out.at[z, x, k]
    else:
        place = lambda out, z, x, k: out.at[x, k]
    tags = tags_of(at, chained)
    chains, across, partner, locals_ = [], {}, {}, []
    for i, (shard, out) in enumerate(zip(shards, outs)):
        own = lambda shard=shard: shard
        if chained:
            chains.append(
                Chain(net, at, own, lambda z, out=out: place(out, z, at.x, at.k))
            )
        locals_.append(Local(net, own, lambda out=out: place(out, at.z, at.x, at.k)))
        for name, z, condition in tags:
            held = own if name == "own" else (lambda out=out, z=z: place(out, z, at.x, at.k))
            target = lambda out=out, z=z: place(out, z, at.x, at.k)
            partner[i, name, 0] = Transfer(
                net, held, target, at.device(k=1 - at.k), condition, condition
            )
            for step in range(1, at.breadth):
                across[i, name, step] = Transfer(
                    net, held, target, at.device(x=at.later_x(step)), condition, condition
                )
                other = at.later_x(at.breadth - step)
                arrived = lambda out=out, z=z, other=other: place(out, z, other, at.k)
                partner[i, name, step] = Transfer(
                    net, arrived, arrived, at.device(k=1 - at.k), condition, condition
                )
    count = len(shards)

    def launch(name):
        for i in range(count):
            for step in range(1, at.breadth):
                across[i, name, step].start()
        for i in range(count):
            partner[i, name, 0].start()

    def forward(name):
        for i in range(count):
            for step in range(1, at.breadth):
                across[i, name, step].got()
                partner[i, name, step].start()

    for chain in chains:
        chain.up[1].start()
        chain.down[1].start()
    launch("own")
    for move in locals_:
        move.start()
    yield
    previous = ["own"]
    if chained:
        for step in range(1, at.depth):
            for chain in chains:
                chain.up[step].got()
                if step + 1 < at.depth:
                    chain.up[step + 1].start()
            launch(("up", step))
            yield
            for chain in chains:
                chain.down[step].got()
                if step + 1 < at.depth:
                    chain.down[step + 1].start()
            launch(("down", step))
            yield
            for name in previous:
                forward(name)
            previous = [("up", step), ("down", step)]
    for name in previous:
        yield
        forward(name)
    yield
    for transfer in partner.values():
        transfer.got()
    for move in locals_:
        move.wait()


def fan(net, at, packs, outs):
    members = 2 * at.breadth
    swap, chains, across, locals_ = {}, [], {}, []
    mine = at.x * 2 + at.k
    for i, (pack, out) in enumerate(zip(packs, outs)):
        slot = lambda out=out: out.at[at.z, at.y, mine]
        locals_.append(Local(net, lambda pack=pack: pack.at[mine], slot))
        for step in range(at.breadth):
            for flip in (0, 1):
                if step == 0 and flip == 0:
                    continue
                x = at.later_x(step)
                k = 1 - at.k if flip else at.k
                swap[i, step, flip] = Transfer(
                    net,
                    lambda pack=pack, x=x, k=k: pack.at[x * 2 + k],
                    slot,
                    at.device(x=x, k=k),
                )
        block = lambda z, out=out: out.at[z, at.y]
        chains.append(Chain(net, at, lambda block=block: block(at.z), block))
        for name, z, condition in tags_of(at, True):
            held = lambda block=block, z=z: block(z)
            across[i, name] = Transfer(
                net, held, held, at.device(y=1 - at.y), condition, condition
            )
    for transfer in swap.values():
        transfer.start()
    for move in locals_:
        move.start()
    yield
    for transfer in swap.values():
        transfer.got()
    for move in locals_:
        move.wait()
    count = len(packs)
    for chain in chains:
        chain.up[1].start()
        chain.down[1].start()
    for i in range(count):
        across[i, "own"].start()
    for step in range(1, at.depth):
        yield
        for chain in chains:
            chain.up[step].got()
            if step + 1 < at.depth:
                chain.up[step + 1].start()
        for i in range(count):
            across[i, ("up", step)].start()
        yield
        for chain in chains:
            chain.down[step].got()
            if step + 1 < at.depth:
                chain.down[step + 1].start()
        for i in range(count):
            across[i, ("down", step)].start()
    yield
    for transfer in across.values():
        transfer.got()


def halvings(depth):
    return sorted(range(1, depth), key=lambda bits: (bits & -bits, -bits)) + [0]


def merging(bits, depth):
    limit = bits & -bits if bits else depth
    return [bits + e for e in (1 << i for i in range(depth.bit_length())) if e < limit]


def add_all(target, sources):
    count = target.shape[0]
    step = 16 if count % 16 == 0 else 8

    def one(index, carry):
        rows = pl.ds(pl.multiple_of(index * step, step), step)
        total = sources[0][rows, :].astype(jnp.float32)
        for source in sources[1:]:
            total = total + source[rows, :].astype(jnp.float32)
        target[rows, :] = total.astype(target.dtype)
        return carry

    lax.fori_loop(0, count // step, one, 0)


def collect(net, at, parts, outs, buffers, chained):
    depth = at.depth if chained else 1
    part_of = (
        (lambda part, t, x, k: part.at[t, x, k]) if chained else (lambda part, t, x, k: part.at[x, k])
    )
    loads, partner, across, beyond = {}, {}, {}, {}
    for i, (part, buffer) in enumerate(zip(parts, buffers)):
        own, core, wide = buffer["own"], buffer["core"], buffer["wide"]
        for s in range(depth):
            t = at.flip_z(s) if chained else 0
            for step in range(at.breadth):
                x = at.later_x(step)
                loads[i, s, step] = Local(
                    net,
                    lambda part=part, t=t, x=x: part_of(part, t, x, at.k),
                    lambda own=own, s=s, step=step: own.at[s, step],
                )
                partner[i, s, step] = Transfer(
                    net,
                    lambda part=part, t=t, x=x: part_of(part, t, x, 1 - at.k),
                    lambda core=core, s=s, step=step: core.at[s, step],
                    at.device(k=1 - at.k),
                )
                if step > 0:
                    across[i, s, step] = Transfer(
                        net,
                        lambda own=own, s=s, step=step: own.at[s, step],
                        lambda wide=wide, s=s, step=step: wide.at[step - 1, s],
                        at.device(x=x),
                    )
            if s > 0:
                beyond[i, s] = Transfer(
                    net,
                    lambda own=own, s=s: own.at[s, 0],
                    lambda buffer=buffer, s=s: buffer["far"].at[s - 1],
                    at.device(z=at.flip_z(s & -s)),
                )
    steps = list(range(1, at.breadth)) + [0]
    spans = halvings(depth)
    count = len(parts)
    for i in range(count):
        for s in spans:
            for step in steps:
                partner[i, s, step].start()
                loads[i, s, step].start()
    for i in range(count):
        own, core = buffers[i]["own"], buffers[i]["core"]
        for s in spans:
            yield
            for step in steps:
                loads[i, s, step].wait()
                partner[i, s, step].got()
                if step > 0:
                    add_rows(own.at[s, step], own.at[s, step], core.at[s, step])
                    across[i, s, step].start()
    for i in range(count):
        own, core, wide = buffers[i]["own"], buffers[i]["core"], buffers[i]["wide"]
        for s in spans:
            yield
            for step in steps[:-1]:
                across[i, s, step].got()
            terms = [own.at[s, 0], core.at[s, 0]] + [wide.at[step - 1, s] for step in steps[:-1]]
            for other in merging(s, depth):
                beyond[i, other].got()
                terms.append(buffers[i]["far"].at[other - 1])
            if s > 0:
                add_all(own.at[s, 0], terms)
                beyond[i, s].start()
            else:
                add_all(outs[i], terms)


def fold(net, at, parts, outs, buffers):
    mine = at.x * 2 + at.k
    members = 2 * at.breadth
    loads, across, beyond, swap, stores = {}, {}, {}, {}, []
    for i, (part, buffer) in enumerate(zip(parts, buffers)):
        own, core, far = buffer["own"], buffer["core"], buffer["far"]
        for s in range(at.depth):
            t = at.flip_z(s)
            loads[i, s] = Local(
                net,
                lambda part=part, t=t: part.at[t, at.y],
                lambda own=own, s=s: own.at[s],
            )
            across[i, s] = Transfer(
                net,
                lambda part=part, t=t: part.at[t, 1 - at.y],
                lambda core=core, s=s: core.at[s],
                at.device(y=1 - at.y),
            )
            if s > 0:
                beyond[i, s] = Transfer(
                    net,
                    lambda own=own, s=s: own.at[s],
                    lambda far=far, s=s: far.at[s - 1],
                    at.device(z=at.flip_z(s & -s)),
                )
        slot = lambda i=i: outs[i].at[mine]
        stores.append(Local(net, lambda own=own: own.at[0, mine], slot))
        for step in range(at.breadth):
            for flip in (0, 1):
                if step == 0 and flip == 0:
                    continue
                x = at.later_x(step)
                k = 1 - at.k if flip else at.k
                swap[i, step, flip] = Transfer(
                    net,
                    lambda own=own, x=x, k=k: own.at[0, x * 2 + k],
                    slot,
                    at.device(x=x, k=k),
                )
    count = len(parts)
    spans = halvings(at.depth)
    for s in spans:
        for i in range(count):
            across[i, s].start()
            loads[i, s].start()
    for s in spans:
        for i in range(count):
            yield
            own, core, far = buffers[i]["own"], buffers[i]["core"], buffers[i]["far"]
            loads[i, s].wait()
            across[i, s].got()
            others = merging(s, at.depth)
            for other in others:
                beyond[i, other].got()
            for member in range(members):
                add_all(
                    own.at[s, member],
                    [own.at[s, member], core.at[s, member]]
                    + [far.at[other - 1, member] for other in others],
                )
            if s > 0:
                beyond[i, s].start()
                continue
            stores[i].start()
            for (j, step, flip), transfer in swap.items():
                if j == i:
                    transfer.start()
    yield
    for transfer in swap.values():
        transfer.got()
    for store in stores:
        store.wait()


def everyone(at):
    return [
        (s, flip, step, turn)
        for s in range(at.depth)
        for flip in (0, 1)
        for step in range(at.breadth)
        for turn in (0, 1)
        if (s, flip, step, turn) != (0, 0, 0, 0)
    ]


def hand_out(net, at, table, out):
    members = 2 * at.breadth
    number = lambda z, y, x, k: (z * 2 + y) * members + x * 2 + k
    mine = number(at.z, at.y, at.x, at.k)
    transfers = []
    for s, flip, step, turn in everyone(at):
        z, x = at.later_z(s), at.later_x(step)
        y = 1 - at.y if flip else at.y
        k = 1 - at.k if turn else at.k
        transfers.append(
            Transfer(
                net,
                lambda z=z, y=y, x=x, k=k: table.at[number(z, y, x, k)],
                lambda: out.at[mine],
                at.device(z, y, x, k),
            )
        )
    kept = Local(net, lambda: table.at[mine], lambda: out.at[mine])
    for transfer in transfers:
        transfer.start()
    kept.start()
    for _ in range(64):
        yield
    kept.wait()
    for transfer in transfers:
        transfer.got()


def exchange(label, ident, sizes, kinds, inputs, outputs, scratch, routines, micros=1):
    space = lambda inside: pltpu.VMEM if inside else pl.ANY

    def kernel(*refs):
        sources = refs[: len(inputs)]
        targets = refs[len(inputs) : len(inputs) + len(outputs)]
        held = refs[len(inputs) + len(outputs) : -3]
        at, net = Place(*sizes), Net(*refs[-3:])
        greet(at, kinds)
        run_all(routines(net, at, sources, targets, held))
        net.settle()

    slots = 40 * sizes[0]
    return pl.pallas_call(
        kernel,
        name=label,
        out_shape=[shape for shape, _ in outputs],
        in_specs=[pl.BlockSpec(memory_space=space(inside)) for _, inside in inputs],
        out_specs=[pl.BlockSpec(memory_space=space(inside)) for _, inside in outputs],
        scratch_shapes=list(scratch)
        + [pltpu.SemaphoreType.DMA((slots,))] * 2
        + [pltpu.SemaphoreType.DMA((slots,))],
        cost_estimate=pl.CostEstimate(
            flops=0, bytes_accessed=micros * 3000000, transcendentals=0
        ),
        compiler_params=pltpu.CompilerParams(
            collective_id=ident,
            has_side_effects=True,
            vmem_limit_bytes=(60 if sizes[0] <= 4 else 63) << 20,
        ),
    )(*[array for array, _ in inputs])


def permute(array, depth, step, flip):
    pairs = [
        (z * 2 + y, ((z + step) % depth) * 2 + (1 - y if flip else y))
        for z in range(depth)
        for y in range(2)
    ]
    return lax.ppermute(array, "rows", pairs)


def shuffle(label, sizes, arrays, stages, outs, moves, most):
    def kernel(*refs):
        ins, targets = refs[: len(arrays)], refs[len(arrays) : len(arrays) + len(outs)]
        held = refs[len(arrays) + len(outs) : -2]
        loaded, stored = refs[-2:]
        started, copies = [], []
        plan = moves(Place(*sizes), ins, held, targets)
        for loads, _ in plan:
            for source, target in loads:
                copy = pltpu.make_async_copy(source, target, loaded.at[len(started)])
                copy.start()
                started.append(copy)
        pending = iter(started)
        for loads, stores in plan:
            for _ in loads:
                next(pending).wait()
            for source, target in stores:
                copy = pltpu.make_async_copy(source, target, stored.at[len(copies)])
                copy.start()
                copies.append(copy)
        for copy in copies:
            copy.wait()

    size = sum(stage.size * stage.dtype.itemsize for stage in stages)
    slots = most * len(stages)
    return pl.pallas_call(
        kernel,
        name=label,
        out_shape=outs,
        in_specs=[pl.BlockSpec(memory_space=pl.ANY)] * len(arrays),
        out_specs=[pl.BlockSpec(memory_space=pl.ANY)] * len(outs),
        scratch_shapes=[pltpu.VMEM(stage.shape, stage.dtype) for stage in stages]
        + [pltpu.SemaphoreType.DMA((slots,)), pltpu.SemaphoreType.DMA((slots,))],
        cost_estimate=pl.CostEstimate(flops=0, bytes_accessed=2 * size, transcendentals=0),
        compiler_params=pltpu.CompilerParams(vmem_limit_bytes=60 << 20),
    )(*arrays)


def widen(label, sizes, blocks, outs, parts):
    shares = sorted({(outs[out].shape[-2], share) for _, _, out, share, _ in parts})

    def kernel(*refs):
        ins, targets = refs[: len(blocks)], refs[len(blocks) : len(blocks) + len(outs)]
        held = refs[len(blocks) + len(outs) : -len(shares) - 2]
        wide = refs[-len(shares) - 2 : -2]
        loaded, stored = refs[-2:]
        at = Place(*sizes)
        loads = [
            pltpu.make_async_copy(source, held[i], loaded.at[i]) for i, source in enumerate(ins)
        ]
        for load in loads:
            load.start()
        waited, turns, previous = set(), {}, {}
        for block, distance, out, share, pieces in parts:
            if block not in waited:
                loads[block].wait()
                waited.add(block)
            kind = shares.index((outs[out].shape[-2], share))
            turn = turns.get(kind, 0) % 2
            turns[kind] = turns.get(kind, 0) + 1
            if (kind, turn) in previous:
                previous[kind, turn].wait()
            buffer = wide[kind].at[turn]
            for row, column, count, place in pieces:
                widen_rows(
                    buffer.at[pl.ds(place, count), :],
                    held[block].at[pl.ds(row, count), pl.ds(column, share)],
                )
            z = at.later_z((sizes[0] - distance) % sizes[0])
            if len(outs[out].shape) == 3:
                target = targets[out].at[z]
            else:
                target = targets[out].at[:, pl.ds(pl.multiple_of(z * share, share), share)]
            copy = pltpu.make_async_copy(buffer, target, stored.at[2 * kind + turn])
            copy.start()
            previous[kind, turn] = copy
        for copy in previous.values():
            copy.wait()

    size = sum(block.size for block in blocks)
    return pl.pallas_call(
        kernel,
        name=label,
        out_shape=outs,
        in_specs=[pl.BlockSpec(memory_space=pl.ANY)] * len(blocks),
        out_specs=[pl.BlockSpec(memory_space=pl.ANY)] * len(outs),
        scratch_shapes=[pltpu.VMEM(block.shape, block.dtype) for block in blocks]
        + [pltpu.VMEM((2,) + share, jnp.float32) for share in shares]
        + [pltpu.SemaphoreType.DMA((len(blocks),)), pltpu.SemaphoreType.DMA((2 * len(shares),))],
        cost_estimate=pl.CostEstimate(flops=0, bytes_accessed=6 * size, transcendentals=0),
        compiler_params=pltpu.CompilerParams(vmem_limit_bytes=60 << 20),
    )(*blocks)


def shape_of(dims, kind=jnp.bfloat16):
    return jax.ShapeDtypeStruct(tuple(dims), kind)


def multiply(operand, matrix):
    return jnp.dot(operand, matrix, preferred_element_type=jnp.float32)


def against(operand, matrix):
    return lax.dot_general(
        operand, matrix, (((1,), (1,)), ((), ())), preferred_element_type=jnp.float32
    )


def outer_sum(operand, matrix):
    return lax.dot_general(
        operand, matrix, (((0,), (0,)), ((), ())), preferred_element_type=jnp.float32
    )


def norm_forward(values):
    scaling = lax.rsqrt(jnp.mean(values * values, axis=-1, keepdims=True) + epsilon)
    return (values * scaling, scaling)


def norm_backward(upstream, normed_unit, scaling, gain_vector):
    weighted = upstream * gain_vector
    average = jnp.mean(weighted * normed_unit, axis=-1, keepdims=True)
    return (scaling * (weighted - normed_unit * average), jnp.sum(upstream * normed_unit, axis=0))


def visible(query_ids, query_codes, key_ids, key_codes):
    matches = query_ids[:, None] == key_ids[None, :]
    return jnp.logical_and(matches, key_codes[None, :] <= query_codes[:, None])


def gated(gate_value, expand_value):
    return jax.nn.gelu(gate_value, approximate=True) * expand_value


def low(values):
    return values.astype(jnp.bfloat16)


def gated_grads(gate_value, expand_value, inside_grad):
    gate, expand = gate_value.astype(jnp.float32), expand_value.astype(jnp.float32)
    upstream = inside_grad.astype(jnp.float32)
    slope = float((2.0 / math.pi) ** 0.5)
    square = gate * gate
    bend = jnp.tanh(slope * gate * (1.0 + 0.044715 * square))
    half = 0.5 * (1.0 + bend)
    rise = half + 0.5 * gate * (1.0 - bend * bend) * slope * (1.0 + 3.0 * 0.044715 * square)
    return (low(upstream * expand * rise), low(upstream * gate * half))


def feed_forward(normed_rows, cotangent, gate_weight, expand_weight, down_weight):
    gate_value = multiply(normed_rows, gate_weight)
    expand_value = multiply(normed_rows, expand_weight)
    inside_low = low(gated(gate_value, expand_value))
    part = low(against(inside_low, down_weight))
    inside_grad = multiply(cotangent, down_weight)
    gate_low, expand_low = gated_grads(gate_value, expand_value, inside_grad)
    normed_grad = low(against(gate_low, gate_weight) + against(expand_low, expand_weight))
    weight_grads = (
        outer_sum(normed_rows, gate_low),
        outer_sum(normed_rows, expand_low),
        outer_sum(cotangent, inside_low),
    )
    return (part, normed_grad, weight_grads)


def by_member(parts, members):
    rows = parts[0].shape[0]
    columns = jnp.concatenate([part.reshape(rows, members, -1) for part in parts], 2)
    return jnp.swapaxes(columns, 0, 1)


def body(
    prefix_tokens,
    action_tokens,
    prefix_cotangent,
    action_cotangent,
    prefix_segments,
    action_codes,
    prefix_query,
    prefix_key,
    prefix_value,
    prefix_mixer,
    action_query,
    action_key,
    action_value,
    action_mixer,
    prefix_prenorm,
    prefix_midnorm,
    action_prenorm,
    action_midnorm,
    prefix_gate,
    prefix_expand,
    prefix_down,
    action_gate,
    action_expand,
    action_down,
):
    members = lax.axis_size("cam")
    row_count = lax.axis_size("rows")
    depth, breadth = row_count // 2, members // 2
    sizes = (depth, breadth)
    head_size = prefix_key.shape[1]
    width = prefix_query.shape[1] // members
    heads = width // head_size
    pair = 2 * head_size // members
    inverse = float(head_size) ** (-0.5)
    lead_count, lead_width = prefix_tokens.shape
    tail_count, tail_width = action_tokens.shape
    idents = iter(range(100))

    def cam_spread(label, shards):
        return exchange(
            label,
            next(idents),
            sizes,
            ("cam",),
            [(shard, True) for shard in shards],
            [(shape_of((breadth, 2) + shard.shape), False) for shard in shards],
            [],
            lambda net, at, ins, outs, held: [spread(net, at, ins, outs, False)],
        )

    def cam_collect(label, parts):
        blocks = [part.shape[-2:] for part in parts]
        scratch = []
        for block in blocks:
            scratch += [
                pltpu.VMEM((1, breadth) + block, jnp.bfloat16),
                pltpu.VMEM((1, breadth) + block, jnp.bfloat16),
                pltpu.VMEM((breadth - 1, 1) + block, jnp.bfloat16),
            ]

        def routines(net, at, ins, outs, held):
            buffers = [
                dict(own=held[3 * i], core=held[3 * i + 1], wide=held[3 * i + 2])
                for i in range(len(parts))
            ]
            return [collect(net, at, ins, outs, buffers, False)]

        return exchange(
            label,
            next(idents),
            sizes,
            ("cam",),
            [(part, False) for part in parts],
            [(shape_of(block, jnp.float32), True) for block in blocks],
            scratch,
            routines,
        )

    lead_slice = prefix_gate.shape[1] // depth
    tail_slice = action_gate.shape[1] // depth
    lead_block, tail_block = prefix_gate.shape[0], action_gate.shape[0]
    floor = lax.axis_index("rows") // 2
    side = lax.rem(lax.axis_index("rows"), 2)
    ratio = lead_slice // tail_slice
    strip = tail_block // ratio
    packed = tail_slice % 128 == 0 and strip % 16 == 0
    upper = shape_of((2 * lead_block + (3 * strip if packed else 0), lead_slice))
    lower = shape_of((lead_block, lead_slice))

    def strips(i, start):
        return [(start + i * strip, j * tail_slice, j * strip) for j in range(ratio)]

    def cut(net, at, ins, outs, held):
        loads, stores = [], []
        for step in range(depth):
            z = at.later_z(step)
            columns = pl.ds(pl.multiple_of(z * lead_slice, lead_slice), lead_slice)
            high, down = held[step], held[depth + step]
            pairs = [
                (ins[i].at[:, columns], high.at[pl.ds(i * lead_block, lead_block), :])
                for i in range(2)
            ]
            if packed:
                narrow = pl.ds(pl.multiple_of(z * tail_slice, tail_slice), tail_slice)
                pairs += [
                    (
                        ins[3 + i].at[pl.ds(place, strip), narrow],
                        high.at[pl.ds(row, strip), pl.ds(column, tail_slice)],
                    )
                    for i in range(3)
                    for row, column, place in strips(i, 2 * lead_block)
                ]
            pairs.append((ins[2].at[:, columns], down))
            for source, target in pairs:
                loads.append(Local(net, lambda source=source: source, lambda target=target: target))
            for i in (step, depth + step):
                stores.append(Local(net, lambda i=i: held[i], lambda i=i: outs[i]))
        for load in loads:
            load.start()
        yield
        yield
        for load in loads:
            load.wait()
        for store in stores:
            store.start()
        for _ in range(8):
            yield
        for store in stores:
            store.wait()

    lead_weights = [prefix_gate, prefix_expand, prefix_down]
    tail_weights = [action_gate, action_expand, action_down]
    cut_inputs = lead_weights + (tail_weights if packed else [])
    groups = 2 if packed else 3
    tails_cut = [
        jnp.stack(
            [
                lax.dynamic_slice_in_dim(
                    weight, lax.rem(floor + step, depth) * tail_slice, tail_slice, 1
                )
                for weight in tail_weights
            ]
        )
        for step in range(0 if packed else depth)
    ]
    dealt, mirrored = {}, {}

    def deal(group, cuts):
        for step, block in enumerate(cuts):
            dealt[group, step] = permute(block, depth, step, False) if step > 0 else block

    def mirror(kinds, step):
        for group in kinds:
            mirrored[group, step] = permute(dealt[group, step], depth, 0, True)

    def tied(arrays, kinds, step):
        keys = [(group, step) for group in kinds]
        arrays, blocks = lax.optimization_barrier((arrays, [dealt[key] for key in keys]))
        dealt.update(zip(keys, blocks))
        return arrays

    def echoed(arrays, group, step):
        arrays, mirrored[group, step] = lax.optimization_barrier((arrays, mirrored[group, step]))
        return arrays

    soon = [0] if packed else [0, 2]

    lead_float = prefix_tokens.astype(jnp.float32)
    tail_float = action_tokens.astype(jnp.float32)
    lead_unit, lead_scale = norm_forward(lead_float)
    tail_unit, tail_scale = norm_forward(tail_float)
    lead_low = low(lead_unit * prefix_prenorm)
    tail_low = low(tail_unit * action_prenorm)
    lead_pack = by_member([prefix_query, jnp.concatenate([prefix_key, prefix_value], 1)], members)
    tail_pack = by_member([action_query, jnp.concatenate([action_key, action_value], 1)], members)
    lead_mixers = by_member([prefix_mixer], members)
    tail_mixers = by_member([action_mixer], members)
    packs = [lead_pack, tail_pack, lead_mixers, tail_mixers]
    shards = [prefix_cotangent, action_cotangent]
    first = [lead_low, tail_low] + packs + shards
    fanned = lambda pack: (shape_of((depth, 2) + pack.shape), False)
    gathered = lambda shard: (shape_of((depth, breadth, 2) + shard.shape), False)
    started = exchange(
        "first",
        next(idents),
        sizes,
        ("z", "y", "cam"),
        [(array, True) for array in first] + [(weight, False) for weight in cut_inputs],
        [(shape_of((breadth, 2) + array.shape), False) for array in first[:2]]
        + [fanned(pack) for pack in packs]
        + [gathered(shard) for shard in shards]
        + [(upper, False)] * depth
        + [(lower, False)] * depth,
        [pltpu.VMEM(upper.shape, upper.dtype)] * depth
        + [pltpu.VMEM(lower.shape, lower.dtype)] * depth,
        lambda net, at, ins, outs, held: [
            fan(net, at, ins[2:4], outs[2:4]),
            spread(net, at, ins[:2], outs[:2], False),
            fan(net, at, ins[4:6], outs[4:6]),
            spread(net, at, ins[6:8], outs[6:8], True),
            cut(net, at, ins[8:], outs[8:], held),
        ],
    )
    started, tails_cut = lax.optimization_barrier((started, tails_cut))
    started, high_cuts, low_cuts = started[:8], started[8 : 8 + depth], started[8 + depth :]
    deal(0, high_cuts)
    if not packed:
        deal(2, tails_cut)
    dealt[1, 0] = low_cuts[0]
    lead_normed, tail_normed, lead_in, tail_in, lead_mix, tail_mix, *uppers = started
    lead_upper, tail_upper = [array.reshape(-1, array.shape[-1]) for array in uppers]
    lead_mix, tail_mix = lead_mix.reshape(lead_width, width), tail_mix.reshape(tail_width, width)
    mirror(soon, 0)
    mirror([1], 0)
    lead_normed = lead_normed.reshape(-1, lead_width)
    tail_normed = tail_normed.reshape(-1, tail_width)
    lead_in = lead_in.reshape(lead_width, -1)
    tail_in = tail_in.reshape(tail_width, -1)
    lead_total, tail_total = lead_normed.shape[0], tail_normed.shape[0]

    projected = low(
        jnp.concatenate([multiply(lead_normed, lead_in), multiply(tail_normed, tail_in)], 0)
    )
    (pairs,) = cam_spread("pairs", [projected[:, width:]])
    pairs = jnp.swapaxes(pairs.reshape(members, -1, pair), 0, 1).reshape(-1, 2 * head_size)

    segment_row = prefix_segments[0]
    code_row = action_codes[0]
    token_ids = jnp.concatenate(
        [segment_row, jnp.arange(code_row.shape[0], dtype=jnp.int32) // ACTT]
    )
    token_codes = jnp.concatenate([jnp.zeros(segment_row.shape, jnp.int32), code_row])
    queries = projected[:, :width].reshape(-1, heads, head_size)
    keys, values = pairs[:, :head_size], pairs[:, head_size:]
    allowed = visible(token_ids, token_codes, token_ids, token_codes)
    logits = jnp.einsum("qhd,kd->hqk", queries, keys, preferred_element_type=jnp.float32) * inverse
    scores = jnp.where(allowed[None], logits, masked_score)
    exponent = jnp.exp(scores - jnp.max(scores, axis=2, keepdims=True))
    totals = jnp.transpose(jnp.sum(exponent, axis=2))[:, :, None]
    probs = low(exponent)
    attention = (
        jnp.einsum("hqk,kd->qhd", probs, values, preferred_element_type=jnp.float32) / totals
    )
    mixed = low(attention.reshape(-1, width))
    cam_blocks = lambda rows: low(rows).reshape(breadth, 2, -1, rows.shape[1])
    lead_sum, tail_sum = cam_collect(
        "mixing",
        [
            cam_blocks(against(mixed[:lead_total], lead_mix)),
            cam_blocks(against(mixed[lead_total:], tail_mix)),
        ],
    )
    lead_sum, tail_sum = tied([lead_sum, tail_sum], soon, 1)
    mirror(soon, 1)
    lead_hidden = lead_float + lead_sum
    tail_hidden = tail_float + tail_sum
    lead_center, lead_factor = norm_forward(lead_hidden)
    tail_center, tail_factor = norm_forward(tail_hidden)
    lead_second = low(lead_center * prefix_midnorm)
    tail_second = low(tail_center * action_midnorm)

    for step in range(2, depth):
        lead_second, tail_second = tied([lead_second, tail_second], soon, step)
        mirror(soon, step)

    def placed(label, kinds, firsts, outs):
        marks = [
            (group, step, flip) for group in kinds for step in range(depth) for flip in (0, 1)
        ]
        blocks = [(mirrored if flip else dealt)[group, step] for group, step, flip in marks]

        def moves(at, ins, held, targets):
            lists = []
            for number, (group, step, flip) in enumerate(marks):
                z = at.later_z((depth - step) % depth)
                y = 1 - at.y if flip else at.y
                block, slot = held[number], firsts[group]
                if group == 2:
                    stores = [(block.at[i], targets[slot + i].at[z, y]) for i in range(3)]
                else:
                    stores = [
                        (
                            block.at[pl.ds(i * lead_block, lead_block), :],
                            targets[slot + i].at[z, y],
                        )
                        for i in range(1 if group == 1 else 2)
                    ]
                if group == 0 and packed:
                    stores += [
                        (
                            block.at[pl.ds(row, strip), pl.ds(column, tail_slice)],
                            targets[2 + i].at[z, y, pl.ds(place, strip), :],
                        )
                        for i in range(3)
                        for row, column, place in strips(i, 2 * lead_block)
                    ]
                lists.append(([(ins[number], block)], stores))
            return lists

        most = 3 + 3 * ratio if packed else 3
        return [
            weight.reshape(-1, weight.shape[-1])
            for weight in shuffle(label, sizes, blocks, blocks, outs, moves, most)
        ]

    lead_out_shape = shape_of((depth, 2, lead_block, lead_slice))
    tail_out_shape = shape_of((depth, 2, tail_block, tail_slice))

    def send_across(packs):
        sent = []
        for pack in packs:
            pack = [low(grad).reshape(depth, 2, -1, grad.shape[1]) for grad in pack]
            if len(pack) > 1 and packed:
                pack[1:] = [
                    jnp.concatenate(jnp.split(grad, ratio, axis=2), axis=3) for grad in pack[1:]
                ]
            tables = [pack] if packed or len(pack) == 1 else [pack[:1], pack[1:]]
            for table in tables:
                take = lambda y: jnp.concatenate(
                    [lax.dynamic_index_in_dim(part, y, 1, False) for part in table], 1
                )
                own, other = take(side), permute(take(1 - side), depth, 0, True)
                sent.append((own, other))
        return sent

    def summed_blocks(pairs):
        summed = jnp.concatenate(
            [low(own.astype(jnp.float32) + other.astype(jnp.float32)) for own, other in pairs], 1
        )
        return [
            lax.dynamic_index_in_dim(summed, lax.rem(floor + step, depth), 0, False)
            for step in range(depth)
        ]

    def pass_on(pairs):
        blocks = summed_blocks(pairs)
        return blocks[:1] + [
            permute(block, depth, step + 1, False) for step, block in enumerate(blocks[1:])
        ]

    shards = [lead_second, tail_second]
    lead_all, tail_all = [
        array.reshape(-1, array.shape[-1])
        for array in exchange(
            "gather",
            next(idents),
            sizes,
            ("z", "cam"),
            [(shard, True) for shard in shards],
            [gathered(shard) for shard in shards],
            [],
            lambda net, at, ins, outs, held: [spread(net, at, ins, outs, True)],
        )
    ]
    (lead_all, tail_all), low_cuts = lax.optimization_barrier(((lead_all, tail_all), low_cuts))
    dealt_here = dealt[1, 0]
    deal(1, low_cuts)
    dealt[1, 0] = dealt_here
    lead_gate, lead_expand, tail_gate, tail_expand, tail_down = placed(
        "upper", soon, {0: 0, 2: 2}, [lead_out_shape] * 2 + [tail_out_shape] * 3
    )
    tail_out, tail_back, tail_ffgrads = feed_forward(
        tail_all, tail_upper, tail_gate, tail_expand, tail_down
    )
    (lead_all, tail_out, tail_back), tail_ffgrads = lax.optimization_barrier(
        ((lead_all, tail_out, tail_back), [low(grad) for grad in tail_ffgrads])
    )
    lead_all = tied(lead_all, [1], 1)
    mirror([1], 1)
    gate_value = low(multiply(lead_all, lead_gate))
    gate_value, lead_all = tied((gate_value, lead_all), [1], 2)
    mirror([1], 2)
    expand_value = low(multiply(lead_all, lead_expand))
    for step in range(3, depth):
        gate_value, expand_value = tied((gate_value, expand_value), [1], step)
        mirror([1], step)
    inside_low = low(gated(gate_value.astype(jnp.float32), expand_value.astype(jnp.float32)))
    down_grad = low(outer_sum(lead_upper, inside_low))
    down_grad, lead_upper = lax.optimization_barrier((down_grad, lead_upper))
    returns = send_across([[down_grad] + tail_ffgrads])
    (lead_down,) = placed("lower", [1], {1: 0}, [lead_out_shape])
    inside_grad = low(multiply(lead_upper, lead_down))
    gate_low, expand_low = gated_grads(gate_value, expand_value, inside_grad)
    returns += send_across(
        [[outer_sum(lead_all, gate_low)], [outer_sum(lead_all, expand_low)]]
    )
    others = [other for _, other in returns[-2:]]
    sources = [own for own, _ in returns[-2:]]
    (inside_low, gate_low, expand_low), sources = lax.optimization_barrier(
        ((inside_low, gate_low, expand_low), sources)
    )
    returns[-2:] = list(zip(sources, others))
    gate_back = against(gate_low, lead_gate)
    (expand_low, gate_back), returns[:-2] = lax.optimization_barrier(
        ((expand_low, gate_back), returns[:-2])
    )
    lead_back = low(gate_back + against(expand_low, lead_expand))
    blocks_back = [pass_on(returns[:1])]
    if not packed:
        blocks_back.append(pass_on(returns[1:2]))

    def token_blocks(rows):
        return rows.reshape(depth, breadth, 2, -1, rows.shape[1])

    def sum_scratch(parts):
        scratch = []
        for part in parts:
            block = part.shape[3:]
            scratch += [
                pltpu.VMEM((depth, breadth) + block, jnp.bfloat16),
                pltpu.VMEM((depth, breadth) + block, jnp.bfloat16),
                pltpu.VMEM((breadth - 1, depth) + block, jnp.bfloat16),
                pltpu.VMEM((depth - 1,) + block, jnp.bfloat16),
            ]
        return scratch

    def sum_routine(net, at, ins, outs, held):
        names = ("own", "core", "wide", "far")
        buffers = [dict(zip(names, held[4 * i : 4 * i + 4])) for i in range(len(ins))]
        return collect(net, at, ins, outs, buffers, True)

    backs = [token_blocks(lead_back), token_blocks(tail_back)]
    lead_summed, tail_summed = exchange(
        "collect",
        next(idents),
        sizes,
        ("deal", "cam"),
        [(part, False) for part in backs],
        [(shape_of(part.shape[3:], jnp.float32), True) for part in backs],
        sum_scratch(backs),
        lambda net, at, ins, outs, held: [sum_routine(net, at, ins, outs, held)],
    )

    (lead_summed, tail_summed), rest, blocks_back = lax.optimization_barrier(
        ((lead_summed, tail_summed), returns[-2:], blocks_back)
    )
    back_blocks = {}
    for i, both in enumerate(rest):
        back_blocks.update({(i, s): block for s, block in enumerate(summed_blocks([both]))})
    leaving = [(i, s) for s in [1] + list(range(3, depth)) + [2] for i in (0, 1)]
    stops = [0, len(leaving) // 3, len(leaving) * 2 // 3, len(leaving)]
    turns = [leaving[stops[i] : stops[i + 1]] for i in range(3)]

    def leave(turn):
        for i, s in turns[turn]:
            back_blocks[i, s] = permute(back_blocks[i, s], depth, s, False)

    def back_tied(arrays, turn):
        marks = turns[turn] + (turns[turn + 1] if turn < 2 else [])
        arrays, pieces = lax.optimization_barrier((arrays, [back_blocks[mark] for mark in marks]))
        back_blocks.update(zip(marks, pieces))
        if turn < 2:
            leave(turn + 1)
        return arrays

    leave(0)
    lead_residual, lead_middle = norm_backward(
        lead_summed, lead_center, lead_factor, prefix_midnorm
    )
    tail_residual, tail_middle = norm_backward(
        tail_summed, tail_center, tail_factor, action_midnorm
    )
    lead_upstream = prefix_cotangent.astype(jnp.float32) + lead_residual
    tail_upstream = action_cotangent.astype(jnp.float32) + tail_residual
    lead_sent, tail_sent = cam_spread("sent", [low(lead_upstream), low(tail_upstream)])
    lead_sent, tail_sent = back_tied((lead_sent, tail_sent), 0)
    lead_sent = lead_sent.reshape(-1, lead_width)
    tail_sent = tail_sent.reshape(-1, tail_width)
    lead_mixing = outer_sum(lead_sent, mixed[:lead_total])
    tail_mixing = outer_sum(tail_sent, mixed[lead_total:])
    attention_grad = jnp.concatenate(
        [multiply(lead_sent, lead_mix), multiply(tail_sent, tail_mix)], 0
    ).reshape(-1, heads, head_size)
    scaled_grad = low(attention_grad / totals)
    deltas = jnp.sum(attention_grad * attention, axis=2, keepdims=True) / totals
    value_grad = jnp.einsum("hqk,qhd->kd", probs, scaled_grad, preferred_element_type=jnp.float32)
    prob_grad = jnp.einsum("qhd,kd->hqk", scaled_grad, values, preferred_element_type=jnp.float32)
    score_grad = low(exponent * (prob_grad - jnp.transpose(deltas, (1, 0, 2))))
    key_grad = (
        jnp.einsum("hqk,qhd->kd", score_grad, queries, preferred_element_type=jnp.float32) * inverse
    )
    query_grad = (
        jnp.einsum("hqk,kd->qhd", score_grad, keys, preferred_element_type=jnp.float32) * inverse
    )
    pair_parts = low(jnp.concatenate([key_grad, value_grad], 1)).reshape(-1, members, pair)
    pair_parts, query_low, lead_mixing, tail_mixing = lax.optimization_barrier(
        (pair_parts, low(query_grad.reshape(-1, width)), low(lead_mixing), low(tail_mixing))
    )
    (pair_grad,) = cam_collect(
        "pair_grads", [jnp.swapaxes(pair_parts, 0, 1).reshape(breadth, 2, -1, pair)]
    )
    pair_grad, inside_low = back_tied((pair_grad, inside_low), 1)
    lead_out = low(against(inside_low, lead_down))
    low_grad = jnp.concatenate([query_low, low(pair_grad)], 1)
    lead_part, tail_part = low_grad[:lead_total], low_grad[lead_total:]
    lead_back, tail_back = cam_collect(
        "backs",
        [cam_blocks(against(lead_part, lead_in)), cam_blocks(against(tail_part, tail_in))],
    )
    (lead_back, tail_back, low_grad, lead_mixing, tail_mixing) = back_tied(
        (lead_back, tail_back, low_grad, lead_mixing, tail_mixing), 2
    )
    lead_part, tail_part = low_grad[:lead_total], low_grad[lead_total:]
    lead_back, lead_first = norm_backward(lead_back, lead_unit, lead_scale, prefix_prenorm)
    tail_back, tail_first = norm_backward(tail_back, tail_unit, tail_scale, action_prenorm)
    lead_input = low(lead_upstream + lead_back)
    tail_input = low(tail_upstream + tail_back)

    owned_lead, owned_tail = prefix_query.shape[0], action_query.shape[0]
    split_rows = lambda grad, rows: low(grad).reshape(depth, 2, members, rows, grad.shape[1])
    attention_parts = [
        split_rows(outer_sum(lead_normed, lead_part), owned_lead),
        split_rows(outer_sum(tail_normed, tail_part), owned_tail),
        split_rows(lead_mixing, owned_lead),
        split_rows(tail_mixing, owned_tail),
    ]
    scratch = []
    for part in attention_parts:
        block = part.shape[2:]
        scratch += [pltpu.VMEM((depth,) + block, jnp.bfloat16)] * 2
        scratch += [pltpu.VMEM((depth - 1,) + block, jnp.bfloat16)]
    gains = [lead_first, lead_middle, tail_first, tail_middle]
    device_count = row_count * members
    table = jnp.concatenate([gain.reshape(device_count, -1) for gain in gains], 1)
    owned = table.shape[1]
    span = -(-owned // 128) * 128
    table = jnp.pad(table, ((0, 0), (0, span - owned)))[:, None, :]
    branches = [token_blocks(lead_out), token_blocks(tail_out)]

    def fold_routines(net, at, ins, outs, held):
        names = ("own", "core", "far")
        buffers = [dict(zip(names, held[3 * i : 3 * i + 3])) for i in range(4)]
        return [
            hand_out(net, at, ins[4], outs[4]),
            fold(net, at, ins[:4], outs[:4], buffers),
            sum_routine(net, at, ins[5:], outs[5:], held[12:]),
        ]

    folded = exchange(
        "fold",
        next(idents),
        sizes,
        ("all",),
        [(part, False) for part in attention_parts]
        + [(table, True)]
        + [(branch, False) for branch in branches],
        [(shape_of(part.shape[2:]), False) for part in attention_parts]
        + [(shape_of(table.shape, jnp.float32), True)]
        + [(shape_of(branch.shape[3:], jnp.float32), True) for branch in branches],
        scratch + sum_scratch(branches),
        fold_routines,
    )
    lead_result = low(lead_hidden + folded[5])
    tail_result = low(tail_hidden + folded[6])

    def split(projection, mixer):
        projection = jnp.swapaxes(projection, 0, 1).astype(jnp.float32)
        rows = projection.shape[0]
        query = projection[:, :, :width].reshape(rows, -1)
        pairs = projection[:, :, width:].reshape(rows, -1)
        mixer = jnp.swapaxes(mixer, 0, 1).reshape(rows, -1).astype(jnp.float32)
        return (query, pairs[:, :head_size], pairs[:, head_size:], mixer)

    lead_grads = split(folded[0], folded[2])
    tail_grads = split(folded[1], folded[3])

    whole_block = [(0, 0, lead_block, 0)]
    parts = []
    for step in range(depth):
        parts.append((step, step, 2, lead_slice, whole_block))
        for i in range(3):
            if packed:
                pieces = [(row, column, strip, place) for row, column, place in strips(i, lead_block)]
                parts.append((step, step, 3 + i, tail_slice, pieces))
            else:
                pieces = [(i * tail_block, 0, tail_block, 0)]
                parts.append((3 * depth + step, step, 3 + i, tail_slice, pieces))
    for i in range(2):
        for step in range(depth):
            parts.append(((1 + i) * depth + step, step, i, lead_slice, whole_block))
    ff_grads = widen(
        "returns",
        sizes,
        blocks_back[0]
        + [back_blocks[i, s] for i in (0, 1) for s in range(depth)]
        + sum(blocks_back[1:], []),
        [shape_of(weight.shape, jnp.float32) for weight in lead_weights]
        + [
            shape_of(
                weight.shape if packed else (depth, tail_block, tail_slice), jnp.float32
            )
            for weight in tail_weights
        ],
        parts,
    )
    if not packed:
        ff_grads = list(ff_grads[:3]) + [
            jnp.swapaxes(grad, 0, 1).reshape(tail_block, -1) for grad in ff_grads[3:]
        ]

    total = jnp.sum(folded[4][:, 0], axis=0)
    gain_grads = []
    offset = 0
    for gain in gains:
        share = gain.shape[0] // device_count
        gain_grads.append(total[offset : offset + share])
        offset += share

    return (
        (lead_result, tail_result, lead_input, tail_input)
        + lead_grads
        + tail_grads
        + tuple(gain_grads)
        + tuple(ff_grads)
    )


def solution(mesh):
    in_specs = (
        P(("rows", "cam"), None),
        P(("rows", "cam"), None),
        P(("rows", "cam"), None),
        P(("rows", "cam"), None),
        P("rows", None),
        P("rows", None),
        P(("rows", "cam"), None),
        P(("rows", "cam"), None),
        P(("rows", "cam"), None),
        P(("rows", "cam"), None),
        P(("rows", "cam"), None),
        P(("rows", "cam"), None),
        P(("rows", "cam"), None),
        P(("rows", "cam"), None),
        P(),
        P(),
        P(),
        P(),
        P("rows", "cam"),
        P("rows", "cam"),
        P("rows", "cam"),
        P("rows", "cam"),
        P("rows", "cam"),
        P("rows", "cam"),
    )
    out_specs = (
        P(("rows", "cam"), None),
        P(("rows", "cam"), None),
        P(("rows", "cam"), None),
        P(("rows", "cam"), None),
        P(("rows", "cam"), None),
        P(("rows", "cam"), None),
        P(("rows", "cam"), None),
        P(("rows", "cam"), None),
        P(("rows", "cam"), None),
        P(("rows", "cam"), None),
        P(("rows", "cam"), None),
        P(("rows", "cam"), None),
        P(("rows", "cam")),
        P(("rows", "cam")),
        P(("rows", "cam")),
        P(("rows", "cam")),
        P("rows", "cam"),
        P("rows", "cam"),
        P("rows", "cam"),
        P("rows", "cam"),
        P("rows", "cam"),
        P("rows", "cam"),
    )
    return jax.shard_map(body, mesh=mesh, in_specs=in_specs, out_specs=out_specs, check_vma=False)
```

```python
import math

import jax
import jax.numpy as jnp
from jax import lax
from jax.experimental import pallas as pl
from jax.experimental.pallas import tpu as pltpu
from jax.sharding import PartitionSpec as P

ACTT = 32


epsilon = 1e-06
masked_score = -1e30


class Place:
    def __init__(self, depth, breadth):
        self.depth, self.breadth = depth, breadth
        row, member = lax.axis_index("rows"), lax.axis_index("cam")
        self.z, self.y = row // 2, row % 2
        self.x, self.k = member // 2, member % 2

    def device(self, z=None, y=None, x=None, k=None):
        z = self.z if z is None else z
        y = self.y if y is None else y
        x = self.x if x is None else x
        k = self.k if k is None else k
        return (z * 2 + y, x * 2 + k)

    def later_x(self, step):
        return lax.rem(self.x + step, self.breadth)

    def later_z(self, step):
        return lax.rem(self.z + step, self.depth)

    def flip_z(self, bits):
        z, bit = self.z, 1
        while bit < self.depth:
            if bits & bit:
                z = z + bit - 2 * bit * lax.rem(self.z // bit, 2)
            bit *= 2
        return z


def guarded(condition, action):
    if condition is None:
        action()
    else:
        pl.when(condition)(action)


class Transfer:
    def __init__(self, net, source, target, device, sends=None, gets=None):
        self.net, self.number = net, net.remote
        net.remote += 1
        self.source, self.target, self.device = source, target, device
        self.sends, self.gets = sends, gets
        net.pending.append(self)

    def describe(self):
        return pltpu.make_async_remote_copy(
            src_ref=self.source(),
            dst_ref=self.target(),
            send_sem=self.net.sent.at[self.number],
            recv_sem=self.net.received.at[self.number],
            device_id=self.device,
            device_id_type=pl.DeviceIdType.MESH,
        )

    def start(self):
        guarded(self.sends, lambda: self.describe().start())

    def got(self):
        guarded(self.gets, lambda: self.describe().wait_recv())

    def finish(self):
        guarded(self.sends, lambda: self.describe().wait_send())


class Local:
    def __init__(self, net, source, target):
        self.net, self.number = net, net.local
        net.local += 1
        self.source, self.target = source, target

    def describe(self):
        return pltpu.make_async_copy(
            self.source(), self.target(), self.net.moved.at[self.number]
        )

    def start(self):
        self.describe().start()
        return self

    def wait(self):
        self.describe().wait()


class Net:
    def __init__(self, sent, received, moved):
        self.sent, self.received, self.moved = sent, received, moved
        self.remote, self.local = 0, 0
        self.pending = []

    def settle(self):
        for transfer in self.pending:
            transfer.finish()


def greet(at, kinds):
    peers = []
    count = 0
    if "all" in kinds:
        for s, flip, step, turn in everyone(at):
            peers.append(
                (
                    None,
                    at.device(
                        at.later_z(s),
                        1 - at.y if flip else at.y,
                        at.later_x(step),
                        1 - at.k if turn else at.k,
                    ),
                )
            )
    if "z" in kinds and "deal" not in kinds:
        count = count + (at.z > 0).astype(jnp.int32) + (at.z < at.depth - 1).astype(jnp.int32)
        peers.append((at.z > 0, at.device(z=at.z - 1)))
        peers.append((at.z < at.depth - 1, at.device(z=at.z + 1)))
    if "deal" in kinds:
        peers += [(None, at.device(z=at.later_z(step))) for step in range(1, at.depth)]
    if "y" in kinds:
        peers.append((None, at.device(y=1 - at.y)))
    if "cam" in kinds:
        for step in range(at.breadth):
            for core in (at.k, 1 - at.k):
                if step > 0 or core is not at.k:
                    peers.append((None, at.device(x=at.later_x(step), k=core)))
    barrier = pltpu.get_barrier_semaphore()
    for condition, device in peers:
        guarded(
            condition,
            lambda device=device: pl.semaphore_signal(
                barrier, inc=1, device_id=device, device_id_type=pl.DeviceIdType.MESH
            ),
        )
    count = count + sum(1 for condition, _ in peers if condition is None)
    pl.semaphore_wait(barrier, count)


def run_all(routines):
    routines = list(routines)
    while routines:
        alive = []
        for routine in routines:
            try:
                next(routine)
                alive.append(routine)
            except StopIteration:
                pass
        routines = alive


def add_rows(target, first, second):
    count = target.shape[0]
    step = 16 if count % 16 == 0 else 8

    def one(index, carry):
        rows = pl.ds(pl.multiple_of(index * step, step), step)
        total = first[rows, :].astype(jnp.float32) + second[rows, :].astype(jnp.float32)
        target[rows, :] = total.astype(target.dtype)
        return carry

    lax.fori_loop(0, count // step, one, 0)


def widen_rows(target, source):
    count = target.shape[0]
    step = 16 if count % 16 == 0 else 8

    def one(index, carry):
        rows = pl.ds(pl.multiple_of(index * step, step), step)
        target[rows, :] = source[rows, :].astype(target.dtype)
        return carry

    lax.fori_loop(0, count // step, one, 0)


class Chain:
    def __init__(self, net, at, own, place):
        depth = at.depth
        self.up, self.down = {}, {}
        for step in range(1, depth):
            low, high = at.z - step + 1, at.z + step - 1
            self.up[step] = Transfer(
                net,
                own if step == 1 else (lambda low=low: place(low)),
                lambda low=low: place(low),
                at.device(z=at.z + 1),
                sends=(at.z + 1 < depth) & (low >= 0),
                gets=at.z - step >= 0,
            )
            self.down[step] = Transfer(
                net,
                own if step == 1 else (lambda high=high: place(high)),
                lambda high=high: place(high),
                at.device(z=at.z - 1),
                sends=(at.z > 0) & (high < depth),
                gets=at.z + step < depth,
            )


def tags_of(at, chained):
    tags = [("own", at.z, None)]
    if chained:
        for step in range(1, at.depth):
            tags.append((("up", step), at.z - step, at.z - step >= 0))
            tags.append((("down", step), at.z + step, at.z + step < at.depth))
    return tags


def spread(net, at, shards, outs, chained):
    if chained:
        place = lambda out, z, x, k: out.at[z, x, k]
    else:
        place = lambda out, z, x, k: out.at[x, k]
    tags = tags_of(at, chained)
    chains, across, partner, locals_ = [], {}, {}, []
    for i, (shard, out) in enumerate(zip(shards, outs)):
        own = lambda shard=shard: shard
        if chained:
            chains.append(
                Chain(net, at, own, lambda z, out=out: place(out, z, at.x, at.k))
            )
        locals_.append(Local(net, own, lambda out=out: place(out, at.z, at.x, at.k)))
        for name, z, condition in tags:
            held = own if name == "own" else (lambda out=out, z=z: place(out, z, at.x, at.k))
            target = lambda out=out, z=z: place(out, z, at.x, at.k)
            partner[i, name, 0] = Transfer(
                net, held, target, at.device(k=1 - at.k), condition, condition
            )
            for step in range(1, at.breadth):
                across[i, name, step] = Transfer(
                    net, held, target, at.device(x=at.later_x(step)), condition, condition
                )
                other = at.later_x(at.breadth - step)
                arrived = lambda out=out, z=z, other=other: place(out, z, other, at.k)
                partner[i, name, step] = Transfer(
                    net, arrived, arrived, at.device(k=1 - at.k), condition, condition
                )
    count = len(shards)

    def launch(name):
        for i in range(count):
            for step in range(1, at.breadth):
                across[i, name, step].start()
        for i in range(count):
            partner[i, name, 0].start()

    def forward(name):
        for i in range(count):
            for step in range(1, at.breadth):
                across[i, name, step].got()
                partner[i, name, step].start()

    for chain in chains:
        chain.up[1].start()
        chain.down[1].start()
    launch("own")
    for move in locals_:
        move.start()
    yield
    previous = ["own"]
    if chained:
        for step in range(1, at.depth):
            for chain in chains:
                chain.up[step].got()
                if step + 1 < at.depth:
                    chain.up[step + 1].start()
            launch(("up", step))
            yield
            for chain in chains:
                chain.down[step].got()
                if step + 1 < at.depth:
                    chain.down[step + 1].start()
            launch(("down", step))
            yield
            for name in previous:
                forward(name)
            previous = [("up", step), ("down", step)]
    for name in previous:
        yield
        forward(name)
    yield
    for transfer in partner.values():
        transfer.got()
    for move in locals_:
        move.wait()


def fan(net, at, packs, outs):
    members = 2 * at.breadth
    swap, chains, across, locals_ = {}, [], {}, []
    mine = at.x * 2 + at.k
    for i, (pack, out) in enumerate(zip(packs, outs)):
        slot = lambda out=out: out.at[at.z, at.y, mine]
        locals_.append(Local(net, lambda pack=pack: pack.at[mine], slot))
        for step in range(at.breadth):
            for flip in (0, 1):
                if step == 0 and flip == 0:
                    continue
                x = at.later_x(step)
                k = 1 - at.k if flip else at.k
                swap[i, step, flip] = Transfer(
                    net,
                    lambda pack=pack, x=x, k=k: pack.at[x * 2 + k],
                    slot,
                    at.device(x=x, k=k),
                )
        block = lambda z, out=out: out.at[z, at.y]
        chains.append(Chain(net, at, lambda block=block: block(at.z), block))
        for name, z, condition in tags_of(at, True):
            held = lambda block=block, z=z: block(z)
            across[i, name] = Transfer(
                net, held, held, at.device(y=1 - at.y), condition, condition
            )
    for transfer in swap.values():
        transfer.start()
    for move in locals_:
        move.start()
    yield
    for transfer in swap.values():
        transfer.got()
    for move in locals_:
        move.wait()
    count = len(packs)
    for chain in chains:
        chain.up[1].start()
        chain.down[1].start()
    for i in range(count):
        across[i, "own"].start()
    for step in range(1, at.depth):
        yield
        for chain in chains:
            chain.up[step].got()
            if step + 1 < at.depth:
                chain.up[step + 1].start()
        for i in range(count):
            across[i, ("up", step)].start()
        yield
        for chain in chains:
            chain.down[step].got()
            if step + 1 < at.depth:
                chain.down[step + 1].start()
        for i in range(count):
            across[i, ("down", step)].start()
    yield
    for transfer in across.values():
        transfer.got()


def halvings(depth):
    return sorted(range(1, depth), key=lambda bits: (bits & -bits, -bits)) + [0]


def merging(bits, depth):
    limit = bits & -bits if bits else depth
    return [bits + e for e in (1 << i for i in range(depth.bit_length())) if e < limit]


def add_all(target, sources):
    count = target.shape[0]
    step = 16 if count % 16 == 0 else 8

    def one(index, carry):
        rows = pl.ds(pl.multiple_of(index * step, step), step)
        total = sources[0][rows, :].astype(jnp.float32)
        for source in sources[1:]:
            total = total + source[rows, :].astype(jnp.float32)
        target[rows, :] = total.astype(target.dtype)
        return carry

    lax.fori_loop(0, count // step, one, 0)


def collect(net, at, parts, outs, buffers, chained):
    depth = at.depth if chained else 1
    part_of = (
        (lambda part, t, x, k: part.at[t, x, k]) if chained else (lambda part, t, x, k: part.at[x, k])
    )
    loads, partner, across, beyond = {}, {}, {}, {}
    for i, (part, buffer) in enumerate(zip(parts, buffers)):
        own, core, wide = buffer["own"], buffer["core"], buffer["wide"]
        for s in range(depth):
            t = at.flip_z(s) if chained else 0
            for step in range(at.breadth):
                x = at.later_x(step)
                loads[i, s, step] = Local(
                    net,
                    lambda part=part, t=t, x=x: part_of(part, t, x, at.k),
                    lambda own=own, s=s, step=step: own.at[s, step],
                )
                partner[i, s, step] = Transfer(
                    net,
                    lambda part=part, t=t, x=x: part_of(part, t, x, 1 - at.k),
                    lambda core=core, s=s, step=step: core.at[s, step],
                    at.device(k=1 - at.k),
                )
                if step > 0:
                    across[i, s, step] = Transfer(
                        net,
                        lambda own=own, s=s, step=step: own.at[s, step],
                        lambda wide=wide, s=s, step=step: wide.at[step - 1, s],
                        at.device(x=x),
                    )
            if s > 0:
                beyond[i, s] = Transfer(
                    net,
                    lambda own=own, s=s: own.at[s, 0],
                    lambda buffer=buffer, s=s: buffer["far"].at[s - 1],
                    at.device(z=at.flip_z(s & -s)),
                )
    steps = list(range(1, at.breadth)) + [0]
    spans = halvings(depth)
    count = len(parts)
    for i in range(count):
        for s in spans:
            for step in steps:
                partner[i, s, step].start()
                loads[i, s, step].start()
    for i in range(count):
        own, core = buffers[i]["own"], buffers[i]["core"]
        for s in spans:
            yield
            for step in steps:
                loads[i, s, step].wait()
                partner[i, s, step].got()
                if step > 0:
                    add_rows(own.at[s, step], own.at[s, step], core.at[s, step])
                    across[i, s, step].start()
    for i in range(count):
        own, core, wide = buffers[i]["own"], buffers[i]["core"], buffers[i]["wide"]
        for s in spans:
            yield
            for step in steps[:-1]:
                across[i, s, step].got()
            terms = [own.at[s, 0], core.at[s, 0]] + [wide.at[step - 1, s] for step in steps[:-1]]
            for other in merging(s, depth):
                beyond[i, other].got()
                terms.append(buffers[i]["far"].at[other - 1])
            if s > 0:
                add_all(own.at[s, 0], terms)
                beyond[i, s].start()
            else:
                add_all(outs[i], terms)


def fold(net, at, parts, outs, buffers):
    mine = at.x * 2 + at.k
    members = 2 * at.breadth
    loads, across, beyond, swap, stores = {}, {}, {}, {}, []
    for i, (part, buffer) in enumerate(zip(parts, buffers)):
        own, core, far = buffer["own"], buffer["core"], buffer["far"]
        for s in range(at.depth):
            t = at.flip_z(s)
            loads[i, s] = Local(
                net,
                lambda part=part, t=t: part.at[t, at.y],
                lambda own=own, s=s: own.at[s],
            )
            across[i, s] = Transfer(
                net,
                lambda part=part, t=t: part.at[t, 1 - at.y],
                lambda core=core, s=s: core.at[s],
                at.device(y=1 - at.y),
            )
            if s > 0:
                beyond[i, s] = Transfer(
                    net,
                    lambda own=own, s=s: own.at[s],
                    lambda far=far, s=s: far.at[s - 1],
                    at.device(z=at.flip_z(s & -s)),
                )
        slot = lambda i=i: outs[i].at[mine]
        stores.append(Local(net, lambda own=own: own.at[0, mine], slot))
        for step in range(at.breadth):
            for flip in (0, 1):
                if step == 0 and flip == 0:
                    continue
                x = at.later_x(step)
                k = 1 - at.k if flip else at.k
                swap[i, step, flip] = Transfer(
                    net,
                    lambda own=own, x=x, k=k: own.at[0, x * 2 + k],
                    slot,
                    at.device(x=x, k=k),
                )
    count = len(parts)
    spans = halvings(at.depth)
    for s in spans:
        for i in range(count):
            across[i, s].start()
            loads[i, s].start()
    for s in spans:
        for i in range(count):
            yield
            own, core, far = buffers[i]["own"], buffers[i]["core"], buffers[i]["far"]
            loads[i, s].wait()
            across[i, s].got()
            others = merging(s, at.depth)
            for other in others:
                beyond[i, other].got()
            for member in range(members):
                add_all(
                    own.at[s, member],
                    [own.at[s, member], core.at[s, member]]
                    + [far.at[other - 1, member] for other in others],
                )
            if s > 0:
                beyond[i, s].start()
                continue
            stores[i].start()
            for (j, step, flip), transfer in swap.items():
                if j == i:
                    transfer.start()
    yield
    for transfer in swap.values():
        transfer.got()
    for store in stores:
        store.wait()


def everyone(at):
    return [
        (s, flip, step, turn)
        for s in range(at.depth)
        for flip in (0, 1)
        for step in range(at.breadth)
        for turn in (0, 1)
        if (s, flip, step, turn) != (0, 0, 0, 0)
    ]


def hand_out(net, at, table, out):
    members = 2 * at.breadth
    number = lambda z, y, x, k: (z * 2 + y) * members + x * 2 + k
    mine = number(at.z, at.y, at.x, at.k)
    transfers = []
    for s, flip, step, turn in everyone(at):
        z, x = at.later_z(s), at.later_x(step)
        y = 1 - at.y if flip else at.y
        k = 1 - at.k if turn else at.k
        transfers.append(
            Transfer(
                net,
                lambda z=z, y=y, x=x, k=k: table.at[number(z, y, x, k)],
                lambda: out.at[mine],
                at.device(z, y, x, k),
            )
        )
    kept = Local(net, lambda: table.at[mine], lambda: out.at[mine])
    for transfer in transfers:
        transfer.start()
    kept.start()
    for _ in range(64):
        yield
    kept.wait()
    for transfer in transfers:
        transfer.got()


def exchange(label, ident, sizes, kinds, inputs, outputs, scratch, routines, micros=1):
    space = lambda inside: pltpu.VMEM if inside else pl.ANY

    def kernel(*refs):
        sources = refs[: len(inputs)]
        targets = refs[len(inputs) : len(inputs) + len(outputs)]
        held = refs[len(inputs) + len(outputs) : -3]
        at, net = Place(*sizes), Net(*refs[-3:])
        greet(at, kinds)
        run_all(routines(net, at, sources, targets, held))
        net.settle()

    slots = 40 * sizes[0]
    return pl.pallas_call(
        kernel,
        name=label,
        out_shape=[shape for shape, _ in outputs],
        in_specs=[pl.BlockSpec(memory_space=space(inside)) for _, inside in inputs],
        out_specs=[pl.BlockSpec(memory_space=space(inside)) for _, inside in outputs],
        scratch_shapes=list(scratch)
        + [pltpu.SemaphoreType.DMA((slots,))] * 2
        + [pltpu.SemaphoreType.DMA((slots,))],
        cost_estimate=pl.CostEstimate(
            flops=0, bytes_accessed=micros * 3000000, transcendentals=0
        ),
        compiler_params=pltpu.CompilerParams(
            collective_id=ident,
            has_side_effects=True,
            vmem_limit_bytes=(60 if sizes[0] <= 4 else 63) << 20,
        ),
    )(*[array for array, _ in inputs])


def permute(array, depth, step, flip):
    pairs = [
        (z * 2 + y, ((z + step) % depth) * 2 + (1 - y if flip else y))
        for z in range(depth)
        for y in range(2)
    ]
    return lax.ppermute(array, "rows", pairs)


def shuffle(label, sizes, arrays, stages, outs, moves, most):
    def kernel(*refs):
        ins, targets = refs[: len(arrays)], refs[len(arrays) : len(arrays) + len(outs)]
        held = refs[len(arrays) + len(outs) : -2]
        loaded, stored = refs[-2:]
        started, copies = [], []
        plan = moves(Place(*sizes), ins, held, targets)
        for loads, _ in plan:
            for source, target in loads:
                copy = pltpu.make_async_copy(source, target, loaded.at[len(started)])
                copy.start()
                started.append(copy)
        pending = iter(started)
        for loads, stores in plan:
            for _ in loads:
                next(pending).wait()
            for source, target in stores:
                copy = pltpu.make_async_copy(source, target, stored.at[len(copies)])
                copy.start()
                copies.append(copy)
        for copy in copies:
            copy.wait()

    size = sum(stage.size * stage.dtype.itemsize for stage in stages)
    slots = most * len(stages)
    return pl.pallas_call(
        kernel,
        name=label,
        out_shape=outs,
        in_specs=[pl.BlockSpec(memory_space=pl.ANY)] * len(arrays),
        out_specs=[pl.BlockSpec(memory_space=pl.ANY)] * len(outs),
        scratch_shapes=[pltpu.VMEM(stage.shape, stage.dtype) for stage in stages]
        + [pltpu.SemaphoreType.DMA((slots,)), pltpu.SemaphoreType.DMA((slots,))],
        cost_estimate=pl.CostEstimate(flops=0, bytes_accessed=2 * size, transcendentals=0),
        compiler_params=pltpu.CompilerParams(vmem_limit_bytes=60 << 20),
    )(*arrays)


def widen(label, sizes, blocks, outs, parts):
    shares = sorted({(outs[out].shape[-2], share) for _, _, out, share, _ in parts})

    def kernel(*refs):
        ins, targets = refs[: len(blocks)], refs[len(blocks) : len(blocks) + len(outs)]
        held = refs[len(blocks) + len(outs) : -len(shares) - 2]
        wide = refs[-len(shares) - 2 : -2]
        loaded, stored = refs[-2:]
        at = Place(*sizes)
        loads = [
            pltpu.make_async_copy(source, held[i], loaded.at[i]) for i, source in enumerate(ins)
        ]
        for load in loads:
            load.start()
        waited, turns, previous = set(), {}, {}
        for block, distance, out, share, pieces in parts:
            if block not in waited:
                loads[block].wait()
                waited.add(block)
            kind = shares.index((outs[out].shape[-2], share))
            turn = turns.get(kind, 0) % 4
            turns[kind] = turns.get(kind, 0) + 1
            if (kind, turn) in previous:
                previous[kind, turn].wait()
            buffer = wide[kind].at[turn]
            for row, column, count, place in pieces:
                widen_rows(
                    buffer.at[pl.ds(place, count), :],
                    held[block].at[pl.ds(row, count), pl.ds(column, share)],
                )
            z = at.later_z((sizes[0] - distance) % sizes[0])
            if len(outs[out].shape) == 3:
                target = targets[out].at[z]
            else:
                target = targets[out].at[:, pl.ds(pl.multiple_of(z * share, share), share)]
            copy = pltpu.make_async_copy(buffer, target, stored.at[4 * kind + turn])
            copy.start()
            previous[kind, turn] = copy
        for copy in previous.values():
            copy.wait()

    size = sum(block.size for block in blocks)
    return pl.pallas_call(
        kernel,
        name=label,
        out_shape=outs,
        in_specs=[pl.BlockSpec(memory_space=pl.ANY)] * len(blocks),
        out_specs=[pl.BlockSpec(memory_space=pl.ANY)] * len(outs),
        scratch_shapes=[pltpu.VMEM(block.shape, block.dtype) for block in blocks]
        + [pltpu.VMEM((4,) + share, jnp.float32) for share in shares]
        + [pltpu.SemaphoreType.DMA((len(blocks),)), pltpu.SemaphoreType.DMA((4 * len(shares),))],
        cost_estimate=pl.CostEstimate(flops=0, bytes_accessed=6 * size, transcendentals=0),
        compiler_params=pltpu.CompilerParams(vmem_limit_bytes=60 << 20),
    )(*blocks)


def shape_of(dims, kind=jnp.bfloat16):
    return jax.ShapeDtypeStruct(tuple(dims), kind)


def multiply(operand, matrix):
    return jnp.dot(operand, matrix, preferred_element_type=jnp.float32)


def against(operand, matrix):
    return lax.dot_general(
        operand, matrix, (((1,), (1,)), ((), ())), preferred_element_type=jnp.float32
    )


def outer_sum(operand, matrix):
    return lax.dot_general(
        operand, matrix, (((0,), (0,)), ((), ())), preferred_element_type=jnp.float32
    )


def norm_forward(values):
    scaling = lax.rsqrt(jnp.mean(values * values, axis=-1, keepdims=True) + epsilon)
    return (values * scaling, scaling)


def norm_backward(upstream, normed_unit, scaling, gain_vector):
    weighted = upstream * gain_vector
    average = jnp.mean(weighted * normed_unit, axis=-1, keepdims=True)
    return (scaling * (weighted - normed_unit * average), jnp.sum(upstream * normed_unit, axis=0))


def visible(query_ids, query_codes, key_ids, key_codes):
    matches = query_ids[:, None] == key_ids[None, :]
    return jnp.logical_and(matches, key_codes[None, :] <= query_codes[:, None])


def gated(gate_value, expand_value):
    return jax.nn.gelu(gate_value, approximate=True) * expand_value


def low(values):
    return values.astype(jnp.bfloat16)


def gated_grads(gate_value, expand_value, inside_grad):
    gate, expand = gate_value.astype(jnp.float32), expand_value.astype(jnp.float32)
    upstream = inside_grad.astype(jnp.float32)
    slope = float((2.0 / math.pi) ** 0.5)
    square = gate * gate
    bend = jnp.tanh(slope * gate * (1.0 + 0.044715 * square))
    half = 0.5 * (1.0 + bend)
    rise = half + 0.5 * gate * (1.0 - bend * bend) * slope * (1.0 + 3.0 * 0.044715 * square)
    return (low(upstream * expand * rise), low(upstream * gate * half))


def feed_forward(normed_rows, cotangent, gate_weight, expand_weight, down_weight):
    gate_value = multiply(normed_rows, gate_weight)
    expand_value = multiply(normed_rows, expand_weight)
    inside_low = low(gated(gate_value, expand_value))
    part = low(against(inside_low, down_weight))
    inside_grad = multiply(cotangent, down_weight)
    gate_low, expand_low = gated_grads(gate_value, expand_value, inside_grad)
    normed_grad = low(against(gate_low, gate_weight) + against(expand_low, expand_weight))
    weight_grads = (
        outer_sum(normed_rows, gate_low),
        outer_sum(normed_rows, expand_low),
        outer_sum(cotangent, inside_low),
    )
    return (part, normed_grad, weight_grads)


def by_member(parts, members):
    rows = parts[0].shape[0]
    columns = jnp.concatenate([part.reshape(rows, members, -1) for part in parts], 2)
    return jnp.swapaxes(columns, 0, 1)


def body(
    prefix_tokens,
    action_tokens,
    prefix_cotangent,
    action_cotangent,
    prefix_segments,
    action_codes,
    prefix_query,
    prefix_key,
    prefix_value,
    prefix_mixer,
    action_query,
    action_key,
    action_value,
    action_mixer,
    prefix_prenorm,
    prefix_midnorm,
    action_prenorm,
    action_midnorm,
    prefix_gate,
    prefix_expand,
    prefix_down,
    action_gate,
    action_expand,
    action_down,
):
    members = lax.axis_size("cam")
    row_count = lax.axis_size("rows")
    depth, breadth = row_count // 2, members // 2
    sizes = (depth, breadth)
    head_size = prefix_key.shape[1]
    width = prefix_query.shape[1] // members
    heads = width // head_size
    pair = 2 * head_size // members
    inverse = float(head_size) ** (-0.5)
    lead_count, lead_width = prefix_tokens.shape
    tail_count, tail_width = action_tokens.shape
    idents = iter(range(100))

    def cam_spread(label, shards):
        return exchange(
            label,
            next(idents),
            sizes,
            ("cam",),
            [(shard, True) for shard in shards],
            [(shape_of((breadth, 2) + shard.shape), False) for shard in shards],
            [],
            lambda net, at, ins, outs, held: [spread(net, at, ins, outs, False)],
        )

    def cam_collect(label, parts):
        blocks = [part.shape[-2:] for part in parts]
        scratch = []
        for block in blocks:
            scratch += [
                pltpu.VMEM((1, breadth) + block, jnp.bfloat16),
                pltpu.VMEM((1, breadth) + block, jnp.bfloat16),
                pltpu.VMEM((breadth - 1, 1) + block, jnp.bfloat16),
            ]

        def routines(net, at, ins, outs, held):
            buffers = [
                dict(own=held[3 * i], core=held[3 * i + 1], wide=held[3 * i + 2])
                for i in range(len(parts))
            ]
            return [collect(net, at, ins, outs, buffers, False)]

        return exchange(
            label,
            next(idents),
            sizes,
            ("cam",),
            [(part, False) for part in parts],
            [(shape_of(block, jnp.float32), True) for block in blocks],
            scratch,
            routines,
        )

    lead_slice = prefix_gate.shape[1] // depth
    tail_slice = action_gate.shape[1] // depth
    lead_block, tail_block = prefix_gate.shape[0], action_gate.shape[0]
    floor = lax.axis_index("rows") // 2
    side = lax.rem(lax.axis_index("rows"), 2)
    ratio = lead_slice // tail_slice
    strip = tail_block // ratio
    packed = tail_slice % 128 == 0 and strip % 16 == 0
    upper = shape_of((2 * lead_block + (3 * strip if packed else 0), lead_slice))
    lower = shape_of((lead_block, lead_slice))

    def strips(i, start):
        return [(start + i * strip, j * tail_slice, j * strip) for j in range(ratio)]

    def cut(net, at, ins, outs, held):
        loads, stores = [], []
        for step in range(depth):
            z = at.later_z(step)
            columns = pl.ds(pl.multiple_of(z * lead_slice, lead_slice), lead_slice)
            high, down = held[step], held[depth + step]
            pairs = [
                (ins[i].at[:, columns], high.at[pl.ds(i * lead_block, lead_block), :])
                for i in range(2)
            ]
            if packed:
                narrow = pl.ds(pl.multiple_of(z * tail_slice, tail_slice), tail_slice)
                pairs += [
                    (
                        ins[3 + i].at[pl.ds(place, strip), narrow],
                        high.at[pl.ds(row, strip), pl.ds(column, tail_slice)],
                    )
                    for i in range(3)
                    for row, column, place in strips(i, 2 * lead_block)
                ]
            pairs.append((ins[2].at[:, columns], down))
            for source, target in pairs:
                loads.append(Local(net, lambda source=source: source, lambda target=target: target))
            for i in (step, depth + step):
                stores.append(Local(net, lambda i=i: held[i], lambda i=i: outs[i]))
        for load in loads:
            load.start()
        yield
        yield
        for load in loads:
            load.wait()
        for store in stores:
            store.start()
        for _ in range(8):
            yield
        for store in stores:
            store.wait()

    lead_weights = [prefix_gate, prefix_expand, prefix_down]
    tail_weights = [action_gate, action_expand, action_down]
    cut_inputs = lead_weights + (tail_weights if packed else [])
    groups = 2 if packed else 3
    tails_cut = [
        jnp.stack(
            [
                lax.dynamic_slice_in_dim(
                    weight, lax.rem(floor + step, depth) * tail_slice, tail_slice, 1
                )
                for weight in tail_weights
            ]
        )
        for step in range(0 if packed else depth)
    ]
    dealt, mirrored = {}, {}

    def deal(group, cuts):
        for step, block in enumerate(cuts):
            dealt[group, step] = permute(block, depth, step, False) if step > 0 else block

    def mirror(kinds, step):
        for group in kinds:
            mirrored[group, step] = permute(dealt[group, step], depth, 0, True)

    def tied(arrays, kinds, step):
        keys = [(group, step) for group in kinds]
        arrays, blocks = lax.optimization_barrier((arrays, [dealt[key] for key in keys]))
        dealt.update(zip(keys, blocks))
        return arrays

    def echoed(arrays, group, step):
        arrays, mirrored[group, step] = lax.optimization_barrier((arrays, mirrored[group, step]))
        return arrays

    soon = [0] if packed else [0, 2]

    lead_float = prefix_tokens.astype(jnp.float32)
    tail_float = action_tokens.astype(jnp.float32)
    lead_unit, lead_scale = norm_forward(lead_float)
    tail_unit, tail_scale = norm_forward(tail_float)
    lead_low = low(lead_unit * prefix_prenorm)
    tail_low = low(tail_unit * action_prenorm)
    lead_pack = by_member([prefix_query, jnp.concatenate([prefix_key, prefix_value], 1)], members)
    tail_pack = by_member([action_query, jnp.concatenate([action_key, action_value], 1)], members)
    lead_mixers = by_member([prefix_mixer], members)
    tail_mixers = by_member([action_mixer], members)
    packs = [lead_pack, tail_pack, lead_mixers, tail_mixers]
    shards = [prefix_cotangent, action_cotangent]
    first = [lead_low, tail_low] + packs + shards
    fanned = lambda pack: (shape_of((depth, 2) + pack.shape), False)
    gathered = lambda shard: (shape_of((depth, breadth, 2) + shard.shape), False)
    started = exchange(
        "first",
        next(idents),
        sizes,
        ("z", "y", "cam"),
        [(array, True) for array in first] + [(weight, False) for weight in cut_inputs],
        [(shape_of((breadth, 2) + array.shape), False) for array in first[:2]]
        + [fanned(pack) for pack in packs]
        + [gathered(shard) for shard in shards]
        + [(upper, False)] * depth
        + [(lower, False)] * depth,
        [pltpu.VMEM(upper.shape, upper.dtype)] * depth
        + [pltpu.VMEM(lower.shape, lower.dtype)] * depth,
        lambda net, at, ins, outs, held: [
            fan(net, at, ins[2:4], outs[2:4]),
            spread(net, at, ins[:2], outs[:2], False),
            fan(net, at, ins[4:6], outs[4:6]),
            spread(net, at, ins[6:8], outs[6:8], True),
            cut(net, at, ins[8:], outs[8:], held),
        ],
    )
    started, tails_cut = lax.optimization_barrier((started, tails_cut))
    started, high_cuts, low_cuts = started[:8], started[8 : 8 + depth], started[8 + depth :]
    deal(0, high_cuts)
    if not packed:
        deal(2, tails_cut)
    dealt[1, 0] = low_cuts[0]
    lead_normed, tail_normed, lead_in, tail_in, lead_mix, tail_mix, *uppers = started
    lead_upper, tail_upper = [array.reshape(-1, array.shape[-1]) for array in uppers]
    lead_mix, tail_mix = lead_mix.reshape(lead_width, width), tail_mix.reshape(tail_width, width)
    mirror(soon, 0)
    mirror([1], 0)
    lead_normed = lead_normed.reshape(-1, lead_width)
    tail_normed = tail_normed.reshape(-1, tail_width)
    lead_in = lead_in.reshape(lead_width, -1)
    tail_in = tail_in.reshape(tail_width, -1)
    lead_total, tail_total = lead_normed.shape[0], tail_normed.shape[0]

    projected = low(
        jnp.concatenate([multiply(lead_normed, lead_in), multiply(tail_normed, tail_in)], 0)
    )
    (pairs,) = cam_spread("pairs", [projected[:, width:]])
    pairs = jnp.swapaxes(pairs.reshape(members, -1, pair), 0, 1).reshape(-1, 2 * head_size)

    segment_row = prefix_segments[0]
    code_row = action_codes[0]
    token_ids = jnp.concatenate(
        [segment_row, jnp.arange(code_row.shape[0], dtype=jnp.int32) // ACTT]
    )
    token_codes = jnp.concatenate([jnp.zeros(segment_row.shape, jnp.int32), code_row])
    queries = projected[:, :width].reshape(-1, heads, head_size)
    keys, values = pairs[:, :head_size], pairs[:, head_size:]
    allowed = visible(token_ids, token_codes, token_ids, token_codes)
    logits = jnp.einsum("qhd,kd->hqk", queries, keys, preferred_element_type=jnp.float32) * inverse
    scores = jnp.where(allowed[None], logits, masked_score)
    exponent = jnp.exp(scores - jnp.max(scores, axis=2, keepdims=True))
    totals = jnp.transpose(jnp.sum(exponent, axis=2))[:, :, None]
    probs = low(exponent)
    attention = (
        jnp.einsum("hqk,kd->qhd", probs, values, preferred_element_type=jnp.float32) / totals
    )
    mixed = low(attention.reshape(-1, width))
    cam_blocks = lambda rows: low(rows).reshape(breadth, 2, -1, rows.shape[1])
    lead_sum, tail_sum = cam_collect(
        "mixing",
        [
            cam_blocks(against(mixed[:lead_total], lead_mix)),
            cam_blocks(against(mixed[lead_total:], tail_mix)),
        ],
    )
    lead_sum, tail_sum = tied([lead_sum, tail_sum], soon, 1)
    mirror(soon, 1)
    lead_hidden = lead_float + lead_sum
    tail_hidden = tail_float + tail_sum
    lead_center, lead_factor = norm_forward(lead_hidden)
    tail_center, tail_factor = norm_forward(tail_hidden)
    lead_second = low(lead_center * prefix_midnorm)
    tail_second = low(tail_center * action_midnorm)

    for step in range(2, depth):
        lead_second, tail_second = tied([lead_second, tail_second], soon, step)
        mirror(soon, step)

    def placed(label, kinds, firsts, outs):
        marks = [
            (group, step, flip) for group in kinds for step in range(depth) for flip in (0, 1)
        ]
        blocks = [(mirrored if flip else dealt)[group, step] for group, step, flip in marks]

        def moves(at, ins, held, targets):
            lists = []
            for number, (group, step, flip) in enumerate(marks):
                z = at.later_z((depth - step) % depth)
                y = 1 - at.y if flip else at.y
                block, slot = held[number], firsts[group]
                if group == 2:
                    stores = [(block.at[i], targets[slot + i].at[z, y]) for i in range(3)]
                else:
                    stores = [
                        (
                            block.at[pl.ds(i * lead_block, lead_block), :],
                            targets[slot + i].at[z, y],
                        )
                        for i in range(1 if group == 1 else 2)
                    ]
                if group == 0 and packed:
                    stores += [
                        (
                            block.at[pl.ds(row, strip), pl.ds(column, tail_slice)],
                            targets[2 + i].at[z, y, pl.ds(place, strip), :],
                        )
                        for i in range(3)
                        for row, column, place in strips(i, 2 * lead_block)
                    ]
                lists.append(([(ins[number], block)], stores))
            return lists

        most = 3 + 3 * ratio if packed else 3
        return [
            weight.reshape(-1, weight.shape[-1])
            for weight in shuffle(label, sizes, blocks, blocks, outs, moves, most)
        ]

    lead_out_shape = shape_of((depth, 2, lead_block, lead_slice))
    tail_out_shape = shape_of((depth, 2, tail_block, tail_slice))

    def send_across(packs):
        sent = []
        for pack in packs:
            pack = [low(grad).reshape(depth, 2, -1, grad.shape[1]) for grad in pack]
            if len(pack) > 1 and packed:
                pack[1:] = [
                    jnp.concatenate(jnp.split(grad, ratio, axis=2), axis=3) for grad in pack[1:]
                ]
            tables = [pack] if packed or len(pack) == 1 else [pack[:1], pack[1:]]
            for table in tables:
                take = lambda y: jnp.concatenate(
                    [lax.dynamic_index_in_dim(part, y, 1, False) for part in table], 1
                )
                own, other = take(side), permute(take(1 - side), depth, 0, True)
                sent.append((own, other))
        return sent

    def summed_blocks(pairs):
        summed = jnp.concatenate(
            [low(own.astype(jnp.float32) + other.astype(jnp.float32)) for own, other in pairs], 1
        )
        return [
            lax.dynamic_index_in_dim(summed, lax.rem(floor + step, depth), 0, False)
            for step in range(depth)
        ]

    def pass_on(pairs):
        blocks = summed_blocks(pairs)
        return blocks[:1] + [
            permute(block, depth, step + 1, False) for step, block in enumerate(blocks[1:])
        ]

    shards = [lead_second, tail_second]
    lead_all, tail_all = [
        array.reshape(-1, array.shape[-1])
        for array in exchange(
            "gather",
            next(idents),
            sizes,
            ("z", "cam"),
            [(shard, True) for shard in shards],
            [gathered(shard) for shard in shards],
            [],
            lambda net, at, ins, outs, held: [spread(net, at, ins, outs, True)],
        )
    ]
    (lead_all, tail_all), low_cuts = lax.optimization_barrier(((lead_all, tail_all), low_cuts))
    dealt_here = dealt[1, 0]
    deal(1, low_cuts)
    dealt[1, 0] = dealt_here
    lead_gate, lead_expand, tail_gate, tail_expand, tail_down = placed(
        "upper", soon, {0: 0, 2: 2}, [lead_out_shape] * 2 + [tail_out_shape] * 3
    )
    tail_out, tail_back, tail_ffgrads = feed_forward(
        tail_all, tail_upper, tail_gate, tail_expand, tail_down
    )
    (lead_all, tail_out, tail_back), tail_ffgrads = lax.optimization_barrier(
        ((lead_all, tail_out, tail_back), [low(grad) for grad in tail_ffgrads])
    )
    lead_all = tied(lead_all, [1], 1)
    mirror([1], 1)
    gate_value = low(multiply(lead_all, lead_gate))
    gate_value, lead_all = tied((gate_value, lead_all), [1], 2)
    mirror([1], 2)
    expand_value = low(multiply(lead_all, lead_expand))
    for step in range(3, depth):
        gate_value, expand_value = tied((gate_value, expand_value), [1], step)
        mirror([1], step)
    inside_low = low(gated(gate_value.astype(jnp.float32), expand_value.astype(jnp.float32)))
    down_grad = low(outer_sum(lead_upper, inside_low))
    down_grad, lead_upper = lax.optimization_barrier((down_grad, lead_upper))
    returns = send_across([[down_grad] + tail_ffgrads])
    (lead_down,) = placed("lower", [1], {1: 0}, [lead_out_shape])
    inside_grad = low(multiply(lead_upper, lead_down))
    gate_low, expand_low = gated_grads(gate_value, expand_value, inside_grad)
    returns += send_across(
        [[outer_sum(lead_all, gate_low)], [outer_sum(lead_all, expand_low)]]
    )
    others = [other for _, other in returns[-2:]]
    sources = [own for own, _ in returns[-2:]]
    (inside_low, gate_low, expand_low), sources = lax.optimization_barrier(
        ((inside_low, gate_low, expand_low), sources)
    )
    returns[-2:] = list(zip(sources, others))
    gate_back = against(gate_low, lead_gate)
    (expand_low, gate_back), returns[:-2] = lax.optimization_barrier(
        ((expand_low, gate_back), returns[:-2])
    )
    lead_back = low(gate_back + against(expand_low, lead_expand))
    blocks_back = [pass_on(returns[:1])]
    if not packed:
        blocks_back.append(pass_on(returns[1:2]))

    def token_blocks(rows):
        return rows.reshape(depth, breadth, 2, -1, rows.shape[1])

    def sum_scratch(parts):
        scratch = []
        for part in parts:
            block = part.shape[3:]
            scratch += [
                pltpu.VMEM((depth, breadth) + block, jnp.bfloat16),
                pltpu.VMEM((depth, breadth) + block, jnp.bfloat16),
                pltpu.VMEM((breadth - 1, depth) + block, jnp.bfloat16),
                pltpu.VMEM((depth - 1,) + block, jnp.bfloat16),
            ]
        return scratch

    def sum_routine(net, at, ins, outs, held):
        names = ("own", "core", "wide", "far")
        buffers = [dict(zip(names, held[4 * i : 4 * i + 4])) for i in range(len(ins))]
        return collect(net, at, ins, outs, buffers, True)

    backs = [token_blocks(lead_back), token_blocks(tail_back)]
    lead_summed, tail_summed = exchange(
        "collect",
        next(idents),
        sizes,
        ("deal", "cam"),
        [(part, False) for part in backs],
        [(shape_of(part.shape[3:], jnp.float32), True) for part in backs],
        sum_scratch(backs),
        lambda net, at, ins, outs, held: [sum_routine(net, at, ins, outs, held)],
    )

    (lead_summed, tail_summed), rest, blocks_back = lax.optimization_barrier(
        ((lead_summed, tail_summed), returns[-2:], blocks_back)
    )
    back_blocks = {}
    for i, both in enumerate(rest):
        back_blocks.update({(i, s): block for s, block in enumerate(summed_blocks([both]))})
    leaving = [(i, s) for s in [1] + list(range(3, depth)) + [2] for i in (0, 1)]
    stops = [0, len(leaving) // 3, len(leaving) * 2 // 3, len(leaving)]
    turns = [leaving[stops[i] : stops[i + 1]] for i in range(3)]

    def leave(turn):
        for i, s in turns[turn]:
            back_blocks[i, s] = permute(back_blocks[i, s], depth, s, False)

    def back_tied(arrays, turn):
        marks = turns[turn] + (turns[turn + 1] if turn < 2 else [])
        arrays, pieces = lax.optimization_barrier((arrays, [back_blocks[mark] for mark in marks]))
        back_blocks.update(zip(marks, pieces))
        if turn < 2:
            leave(turn + 1)
        return arrays

    leave(0)
    lead_residual, lead_middle = norm_backward(
        lead_summed, lead_center, lead_factor, prefix_midnorm
    )
    tail_residual, tail_middle = norm_backward(
        tail_summed, tail_center, tail_factor, action_midnorm
    )
    lead_upstream = prefix_cotangent.astype(jnp.float32) + lead_residual
    tail_upstream = action_cotangent.astype(jnp.float32) + tail_residual
    lead_sent, tail_sent = cam_spread("sent", [low(lead_upstream), low(tail_upstream)])
    lead_sent, tail_sent = back_tied((lead_sent, tail_sent), 0)
    lead_sent = lead_sent.reshape(-1, lead_width)
    tail_sent = tail_sent.reshape(-1, tail_width)
    lead_mixing = outer_sum(lead_sent, mixed[:lead_total])
    tail_mixing = outer_sum(tail_sent, mixed[lead_total:])
    attention_grad = jnp.concatenate(
        [multiply(lead_sent, lead_mix), multiply(tail_sent, tail_mix)], 0
    ).reshape(-1, heads, head_size)
    scaled_grad = low(attention_grad / totals)
    deltas = jnp.sum(attention_grad * attention, axis=2, keepdims=True) / totals
    value_grad = jnp.einsum("hqk,qhd->kd", probs, scaled_grad, preferred_element_type=jnp.float32)
    prob_grad = jnp.einsum("qhd,kd->hqk", scaled_grad, values, preferred_element_type=jnp.float32)
    score_grad = low(exponent * (prob_grad - jnp.transpose(deltas, (1, 0, 2))))
    key_grad = (
        jnp.einsum("hqk,qhd->kd", score_grad, queries, preferred_element_type=jnp.float32) * inverse
    )
    query_grad = (
        jnp.einsum("hqk,kd->qhd", score_grad, keys, preferred_element_type=jnp.float32) * inverse
    )
    pair_parts = low(jnp.concatenate([key_grad, value_grad], 1)).reshape(-1, members, pair)
    pair_parts, query_low, lead_mixing, tail_mixing = lax.optimization_barrier(
        (pair_parts, low(query_grad.reshape(-1, width)), low(lead_mixing), low(tail_mixing))
    )
    (pair_grad,) = cam_collect(
        "pair_grads", [jnp.swapaxes(pair_parts, 0, 1).reshape(breadth, 2, -1, pair)]
    )
    pair_grad, inside_low = back_tied((pair_grad, inside_low), 1)
    lead_out = low(against(inside_low, lead_down))
    low_grad = jnp.concatenate([query_low, low(pair_grad)], 1)
    lead_part, tail_part = low_grad[:lead_total], low_grad[lead_total:]
    lead_back, tail_back = cam_collect(
        "backs",
        [cam_blocks(against(lead_part, lead_in)), cam_blocks(against(tail_part, tail_in))],
    )
    (lead_back, tail_back, low_grad, lead_mixing, tail_mixing) = back_tied(
        (lead_back, tail_back, low_grad, lead_mixing, tail_mixing), 2
    )
    lead_part, tail_part = low_grad[:lead_total], low_grad[lead_total:]
    lead_back, lead_first = norm_backward(lead_back, lead_unit, lead_scale, prefix_prenorm)
    tail_back, tail_first = norm_backward(tail_back, tail_unit, tail_scale, action_prenorm)
    lead_input = low(lead_upstream + lead_back)
    tail_input = low(tail_upstream + tail_back)

    owned_lead, owned_tail = prefix_query.shape[0], action_query.shape[0]
    split_rows = lambda grad, rows: low(grad).reshape(depth, 2, members, rows, grad.shape[1])
    attention_parts = [
        split_rows(outer_sum(lead_normed, lead_part), owned_lead),
        split_rows(outer_sum(tail_normed, tail_part), owned_tail),
        split_rows(lead_mixing, owned_lead),
        split_rows(tail_mixing, owned_tail),
    ]
    scratch = []
    for part in attention_parts:
        block = part.shape[2:]
        scratch += [pltpu.VMEM((depth,) + block, jnp.bfloat16)] * 2
        scratch += [pltpu.VMEM((depth - 1,) + block, jnp.bfloat16)]
    gains = [lead_first, lead_middle, tail_first, tail_middle]
    device_count = row_count * members
    table = jnp.concatenate([gain.reshape(device_count, -1) for gain in gains], 1)
    owned = table.shape[1]
    span = -(-owned // 128) * 128
    table = jnp.pad(table, ((0, 0), (0, span - owned)))[:, None, :]
    branches = [token_blocks(lead_out), token_blocks(tail_out)]

    def fold_routines(net, at, ins, outs, held):
        names = ("own", "core", "far")
        buffers = [dict(zip(names, held[3 * i : 3 * i + 3])) for i in range(4)]
        return [
            hand_out(net, at, ins[4], outs[4]),
            fold(net, at, ins[:4], outs[:4], buffers),
            sum_routine(net, at, ins[5:], outs[5:], held[12:]),
        ]

    folded = exchange(
        "fold",
        next(idents),
        sizes,
        ("all",),
        [(part, False) for part in attention_parts]
        + [(table, True)]
        + [(branch, False) for branch in branches],
        [(shape_of(part.shape[2:]), False) for part in attention_parts]
        + [(shape_of(table.shape, jnp.float32), True)]
        + [(shape_of(branch.shape[3:], jnp.float32), True) for branch in branches],
        scratch + sum_scratch(branches),
        fold_routines,
    )
    lead_result = low(lead_hidden + folded[5])
    tail_result = low(tail_hidden + folded[6])

    def split(projection, mixer):
        projection = jnp.swapaxes(projection, 0, 1).astype(jnp.float32)
        rows = projection.shape[0]
        query = projection[:, :, :width].reshape(rows, -1)
        pairs = projection[:, :, width:].reshape(rows, -1)
        mixer = jnp.swapaxes(mixer, 0, 1).reshape(rows, -1).astype(jnp.float32)
        return (query, pairs[:, :head_size], pairs[:, head_size:], mixer)

    lead_grads = split(folded[0], folded[2])
    tail_grads = split(folded[1], folded[3])

    whole_block = [(0, 0, lead_block, 0)]
    parts = []
    for step in range(depth):
        parts.append((step, step, 2, lead_slice, whole_block))
        for i in range(3):
            if packed:
                pieces = [(row, column, strip, place) for row, column, place in strips(i, lead_block)]
                parts.append((step, step, 3 + i, tail_slice, pieces))
            else:
                pieces = [(i * tail_block, 0, tail_block, 0)]
                parts.append((3 * depth + step, step, 3 + i, tail_slice, pieces))
    for i in range(2):
        for step in range(depth):
            parts.append(((1 + i) * depth + step, step, i, lead_slice, whole_block))
    ff_grads = widen(
        "returns",
        sizes,
        blocks_back[0]
        + [back_blocks[i, s] for i in (0, 1) for s in range(depth)]
        + sum(blocks_back[1:], []),
        [shape_of(weight.shape, jnp.float32) for weight in lead_weights]
        + [
            shape_of(
                weight.shape if packed else (depth, tail_block, tail_slice), jnp.float32
            )
            for weight in tail_weights
        ],
        parts,
    )
    if not packed:
        ff_grads = list(ff_grads[:3]) + [
            jnp.swapaxes(grad, 0, 1).reshape(tail_block, -1) for grad in ff_grads[3:]
        ]

    total = jnp.sum(folded[4][:, 0], axis=0)
    gain_grads = []
    offset = 0
    for gain in gains:
        share = gain.shape[0] // device_count
        gain_grads.append(total[offset : offset + share])
        offset += share

    return (
        (lead_result, tail_result, lead_input, tail_input)
        + lead_grads
        + tail_grads
        + tuple(gain_grads)
        + tuple(ff_grads)
    )


def solution(mesh):
    in_specs = (
        P(("rows", "cam"), None),
        P(("rows", "cam"), None),
        P(("rows", "cam"), None),
        P(("rows", "cam"), None),
        P("rows", None),
        P("rows", None),
        P(("rows", "cam"), None),
        P(("rows", "cam"), None),
        P(("rows", "cam"), None),
        P(("rows", "cam"), None),
        P(("rows", "cam"), None),
        P(("rows", "cam"), None),
        P(("rows", "cam"), None),
        P(("rows", "cam"), None),
        P(),
        P(),
        P(),
        P(),
        P("rows", "cam"),
        P("rows", "cam"),
        P("rows", "cam"),
        P("rows", "cam"),
        P("rows", "cam"),
        P("rows", "cam"),
    )
    out_specs = (
        P(("rows", "cam"), None),
        P(("rows", "cam"), None),
        P(("rows", "cam"), None),
        P(("rows", "cam"), None),
        P(("rows", "cam"), None),
        P(("rows", "cam"), None),
        P(("rows", "cam"), None),
        P(("rows", "cam"), None),
        P(("rows", "cam"), None),
        P(("rows", "cam"), None),
        P(("rows", "cam"), None),
        P(("rows", "cam"), None),
        P(("rows", "cam")),
        P(("rows", "cam")),
        P(("rows", "cam")),
        P(("rows", "cam")),
        P("rows", "cam"),
        P("rows", "cam"),
        P("rows", "cam"),
        P("rows", "cam"),
        P("rows", "cam"),
        P("rows", "cam"),
    )
    return jax.shard_map(body, mesh=mesh, in_specs=in_specs, out_specs=out_specs, check_vma=False)
```
